32 devices in a mesh: ctx: 8 (over y, x, core), fsdp: 4 (over z).
Axes of the slice: x: 2, y: 2, z: 4, core: 2. Of those that a mesh axis runs over, the one named last changes fastest.
Arguments:
- layer_in: bfloat16 [8, 1024, 1024], P('fsdp', 'ctx'), may hold values from -6 to 6
- block_order: int32 [8, 16], P('fsdp'), may hold values from 0 to 15, as said below
- ln1_gain: bfloat16 [1024], P('fsdp'), may hold values from 0.5 to 1.5
- ln1_shift: bfloat16 [1024], P('fsdp'), may hold values from -3 to 3
- w_qkv: bfloat16 [1024, 3072], P('fsdp'), may hold values from -0.1875 to 0.1875
- b_query: bfloat16 [1024], P('fsdp'), may hold values from -3 to 3
- b_value: bfloat16 [1024], P('fsdp'), may hold values from -3 to 3
- w_out: bfloat16 [1024, 1024], P('fsdp'), may hold values from -1 to 1
- b_out: bfloat16 [1024], P('fsdp'), may hold values from -2 to 2
- ln2_gain: bfloat16 [1024], P('fsdp'), may hold values from 0.5 to 1.5
- ln2_shift: bfloat16 [1024], P('fsdp'), may hold values from -3 to 3
- w_up: bfloat16 [1024, 4096], P('fsdp'), may hold values from -0.1875 to 0.1875
- b_up: bfloat16 [4096], P('fsdp'), may hold values from -3 to 3
- w_down: bfloat16 [4096, 1024], P('fsdp'), may hold values from -0.09375 to 0.09375
- b_down: bfloat16 [1024], P('fsdp'), may hold values from -3 to 3
- cotangent: bfloat16 [8, 1024, 1024], P('fsdp', 'ctx'), may hold values from -6 to 6
Outputs:
- layer_out: bfloat16 [8, 1024, 1024], P('fsdp', 'ctx')
- input_grad: bfloat16 [8, 1024, 1024], P('fsdp', 'ctx')
- grad_ln1_gain: float32 [1024], P(('ctx', 'fsdp'))
- grad_ln1_shift: float32 [1024], P(('ctx', 'fsdp'))
- grad_w_qkv: float32 [1024, 3072], P(('ctx', 'fsdp'))
- grad_b_query: float32 [1024], P(('ctx', 'fsdp'))
- grad_b_value: float32 [1024], P(('ctx', 'fsdp'))
- grad_w_out: float32 [1024, 1024], P(('ctx', 'fsdp'))
- grad_b_out: float32 [1024], P(('ctx', 'fsdp'))
- grad_ln2_gain: float32 [1024], P(('ctx', 'fsdp'))
- grad_ln2_shift: float32 [1024], P(('ctx', 'fsdp'))
- grad_w_up: float32 [1024, 4096], P(('ctx', 'fsdp'))
- grad_b_up: float32 [4096], P(('ctx', 'fsdp'))
- grad_w_down: float32 [4096, 1024], P(('ctx', 'fsdp'))
- grad_b_down: float32 [1024], P(('ctx', 'fsdp'))
The draws below stay inside these ranges and needn't reach their ends.
Inputs may be any that keep to these rules, and one draw needn't show every extreme that they name: Stored block j of sequence s (rows j * 64 to (j + 1) * 64 - 1 as stored) holds block block_order[s, j] of the true order; each row is a permutation, and entry 2c + 1 is 15 minus entry 2c.
All inputs are finite; a program needn't handle non-finite values.
Results may differ from the reference program's by a relative error of at most 0.012.
Values may be sent and summed in bfloat16 or wider, within the bound.
A program may use at most 512 MiB of HBM per device.

```python
import jax
import jax.numpy as jnp
from jax import lax

D = 1024
HEADS = 8
HEAD_DIM = 128
FF = 4096
SEQLEN = 1024
HALF = 64
BLOCKS = 16
SEQS = 8


def draw_block_order(key, part):
    keys = jax.random.split(jax.random.fold_in(key, 17), SEQS)
    perms = jax.vmap(lambda one_key: jax.random.permutation(one_key, BLOCKS // 2))(keys).astype(jnp.int32)
    mirrored = BLOCKS - 1 - perms
    return jnp.stack([perms, mirrored], axis=2).reshape(SEQS, BLOCKS).astype(jnp.int32)


def strengthened(values, rng, source, target, shards_of, factor):
    owner, partner = [(jnp.arange(values.shape[axis_at]) // (values.shape[axis_at] // shards_of)).reshape([-1 if axis == axis_at else 1 for axis in range(values.ndim)]) for axis_at in (source, target)]
    chosen = jax.random.permutation(rng, shards_of)[partner]
    strong = (owner == chosen) | (owner == (partner + shards_of // 2) % shards_of)
    return jnp.where(strong, factor * values, values)


def block_levels(rng, extent, pieces, smallest, largest):
    loudness, own = 1.0, jax.random.fold_in(rng, 6)
    for axis_at, parts in pieces:
        heights = jnp.exp(jax.random.uniform(jax.random.fold_in(own, axis_at), (parts,), jnp.float32, smallest / len(pieces), largest / len(pieces)))
        loudness = loudness * jnp.repeat(heights, extent[axis_at] // parts).reshape([-1 if axis == axis_at else 1 for axis in range(len(extent))])
    return loudness


def centred(own_key, shape, width, limit, cuts=(), kind=jnp.bfloat16):
    entries = width * jax.random.normal(own_key, shape, jnp.float32)
    if cuts:
        entries = entries * block_levels(own_key, shape, cuts, -0.22, 0.18)
    return jnp.clip(entries, -limit, limit).astype(kind)


def noise_with(key, dims, width, bound, shards, heavy, kind=jnp.bfloat16):
    values = width * jax.random.normal(key, dims, jnp.float32)
    if shards:
        values = values * block_levels(key, dims, shards, -0.22, 0.18)
    return jnp.clip(strengthened(values, jax.random.fold_in(key, 3), *heavy), -bound, bound).astype(kind)


def setup_inputs(seed: int = 0) -> dict:
    seeds = jax.random.split(jax.random.key(seed), 17)
    return {
        "layer_in": noise_with(seeds[0], (SEQS, SEQLEN, D), 1.0, 6.0, ((0, 4), (1, 8)), (1, 2, 8, 2.0)),
        "block_order": draw_block_order(jax.random.fold_in(seeds[16], 71), 0),
        "ln1_gain": jnp.clip(0.5 + 1.0 * jax.random.uniform(seeds[2], (D,), jnp.float32) ** block_levels(seeds[2], (D,), ((0, 4),), -0.2, 0.2), 0.5, 1.5).astype(jnp.bfloat16),
        "ln1_shift": centred(seeds[3], (D,), 0.5, 3.0, ((0, 4),)),
        "w_qkv": centred(seeds[4], (D, 3 * D), D ** -0.5, 0.1875, ((0, 4),)),
        "b_query": centred(seeds[5], (D,), 0.5, 3.0, ((0, 4),)),
        "b_value": centred(seeds[6], (D,), 0.5, 3.0, ((0, 4),)),
        "w_out": centred(seeds[7], (D, D), (max(D * 32 // SEQLEN, 1)) ** -0.5, 1.0, ((0, 4),)),
        "b_out": centred(seeds[8], (D,), 0.3, 2.0, ((0, 4),)),
        "ln2_gain": jnp.clip(0.5 + 1.0 * jax.random.uniform(seeds[9], (D,), jnp.float32) ** block_levels(seeds[9], (D,), ((0, 4),), -0.2, 0.2), 0.5, 1.5).astype(jnp.bfloat16),
        "ln2_shift": centred(seeds[10], (D,), 0.5, 3.0, ((0, 4),)),
        "w_up": centred(seeds[11], (D, FF), D ** -0.5, 0.1875, ((0, 4),)),
        "b_up": centred(seeds[12], (FF,), 0.5, 3.0, ((0, 4),)),
        "w_down": centred(seeds[13], (FF, D), FF ** -0.5, 0.09375, ((0, 4),)),
        "b_down": centred(seeds[14], (D,), 0.5, 3.0, ((0, 4),)),
        "cotangent": noise_with(seeds[15], (SEQS, SEQLEN, D), 1.0, 6.0, ((0, 4), (1, 8)), (1, 2, 8, 2.0)),
    }


@jax.custom_vjp
def low(v):
    return lax.optimization_barrier(v.astype(jnp.bfloat16)).astype(jnp.float32)

@jax.custom_vjp
def low_back(v):
    return v

def low_keep(v):
    return (low(v), None)

def low_pass(kept, grad):
    return (grad,)

def back_keep(v):
    return (v, None)

def back_low(kept, grad):
    return (low(grad),)
low.defvjp(low_keep, low_pass)
low_back.defvjp(back_keep, back_low)
EPSILON = 1e-05
HIGHEST_PRECISION = lax.Precision.HIGHEST
NEG_LARGE = -1e+30

def layer_norm(values, gain_vec, shift_vec):
    average = lax.optimization_barrier(jnp.mean(values, axis=-1, keepdims=True))
    centered = values - average
    variance = lax.optimization_barrier(jnp.mean(centered * centered, axis=-1, keepdims=True))
    return centered * lax.rsqrt(variance + EPSILON) * gain_vec + shift_vec

def positions_of(order_row):
    rows = jnp.arange(SEQLEN, dtype=jnp.int32)
    return order_row[rows // HALF].astype(jnp.int32) * HALF + rows % HALF

def attend_block(query_blk, query_pos, key_all, value_all, key_pos):
    raw_scores = jnp.einsum('qhd,khd->hqk', query_blk, key_all, precision=HIGHEST_PRECISION)
    scores = low_back(raw_scores) * HEAD_DIM ** (-0.5)
    allowed = (query_pos[:, None] >= key_pos[None, :])[None]
    scores = jnp.where(allowed, scores, NEG_LARGE)
    probs = low(jax.nn.softmax(scores, axis=-1))
    return jnp.einsum('hqk,khd->qhd', probs, value_all, precision=HIGHEST_PRECISION)

def attend_sequence(query_all, key_all, value_all, pos):
    block = min(512, SEQLEN)
    query_blocks = query_all.reshape(SEQLEN // block, block, HEADS, HEAD_DIM)
    pos_blocks = pos.reshape(SEQLEN // block, block)
    step = jax.checkpoint(lambda pair: attend_block(pair[0], pair[1], key_all, value_all, pos))
    return lax.map(step, (query_blocks, pos_blocks)).reshape(SEQLEN, HEADS, HEAD_DIM)

def sequence_forward(inputs, pos, params):
    first_gain, first_shift, qkv_weight, query_bias, value_bias, out_weight, out_bias, second_gain, second_shift, up_weight, up_bias, down_weight, down_bias = params
    first_low = low(layer_norm(inputs, first_gain, first_shift))
    projected = jnp.dot(first_low, qkv_weight, precision=HIGHEST_PRECISION, preferred_element_type=jnp.float32)
    query_all = low_back(low(projected[:, :D] + query_bias))
    key_all = low_back(low(projected[:, D:2 * D]))
    value_all = low_back(low(projected[:, 2 * D:] + value_bias))
    heads_shape = (SEQLEN, HEADS, HEAD_DIM)
    attended = attend_sequence(query_all.reshape(heads_shape), key_all.reshape(heads_shape), value_all.reshape(heads_shape), pos)
    attn_low = low_back(low(attended.reshape(SEQLEN, D)))
    branch = low_back(jnp.dot(attn_low, out_weight, precision=HIGHEST_PRECISION, preferred_element_type=jnp.float32) + out_bias)
    resid = inputs + branch
    second_low = low(layer_norm(resid, second_gain, second_shift))
    hidden = low_back(jnp.dot(second_low, up_weight, precision=HIGHEST_PRECISION, preferred_element_type=jnp.float32) + up_bias)
    active = low(jax.nn.gelu(hidden, approximate=True))
    return resid + jnp.dot(active, down_weight, precision=HIGHEST_PRECISION, preferred_element_type=jnp.float32) + down_bias

def reference(layer_in, block_order, ln1_gain, ln1_shift, w_qkv, b_query, b_value, w_out, b_out, ln2_gain, ln2_shift, w_up, b_up, w_down, b_down, cotangent):
    pos = lax.map(positions_of, block_order)
    params = tuple((item.astype(jnp.float32) for item in (ln1_gain, ln1_shift, w_qkv, b_query, b_value, w_out, b_out, ln2_gain, ln2_shift, w_up, b_up, w_down, b_down)))
    inputs = layer_in.astype(jnp.float32)

    def run(input_vals, *weights):
        one_seq = jax.checkpoint(lambda pair: sequence_forward(pair[0], pair[1], weights))
        return lax.map(one_seq, (input_vals, pos))
    result, pull = jax.vjp(run, inputs, *params)
    grads = pull(cotangent.astype(jnp.float32))
    return (result.astype(jnp.bfloat16), grads[0].astype(jnp.bfloat16), grads[1], grads[2], grads[3], grads[4], grads[5], grads[6], grads[7], grads[8], grads[9], grads[10], grads[11], grads[12], grads[13])
```

```python
import math

import jax
import jax.numpy as jnp
from jax import lax
from jax.sharding import PartitionSpec as P

D = 1024
HEADS = 8
HEAD_DIM = 128


EPSILON = 1e-05
NEG_LARGE = -1e30
GELU_C = math.sqrt(2.0 / math.pi)
GELU_K = 0.044715


def gelu_tanh(values):
    inner = jnp.tanh(GELU_C * (values + GELU_K * values * values * values))
    return 0.5 * values * (1.0 + inner)


def gelu_slope(values):
    inner = jnp.tanh(GELU_C * (values + GELU_K * values * values * values))
    return 0.5 * (1.0 + inner) + 0.5 * values * (1.0 - inner * inner) * GELU_C * (
        1.0 + 3.0 * GELU_K * values * values
    )


def normalize(values, gain_vec, shift_vec):
    average = jnp.mean(values, axis=-1, keepdims=True)
    centered = values - average
    inv_dev = lax.rsqrt(jnp.mean(centered * centered, axis=-1, keepdims=True) + EPSILON)
    normed = centered * inv_dev
    return (normed * gain_vec + shift_vec, normed, inv_dev)


def normalize_back(grad, normed, inv_dev, gain_vec):
    scaled = grad * gain_vec
    return inv_dev * (
        scaled
        - jnp.mean(scaled, axis=-1, keepdims=True)
        - normed * jnp.mean(scaled * normed, axis=-1, keepdims=True)
    )


def token_positions(order_row, seq_len, half_rows):
    rows = jnp.arange(seq_len, dtype=jnp.int32)
    slots = jnp.arange(order_row.shape[0], dtype=jnp.int32)
    picked = jnp.sum(
        jnp.where((rows // half_rows)[:, None] == slots[None, :], order_row[None, :], 0), axis=1
    )
    return picked * half_rows + rows % half_rows


def block_probs(query_heads, key_heads, query_pos, key_pos, row_lse, scale):
    raw_scores = jnp.einsum(
        "qhd,khd->hqk", query_heads, key_heads, preferred_element_type=jnp.float32
    )
    allowed = (query_pos[:, None] >= key_pos[None, :])[None]
    shifted = jnp.where(allowed, raw_scores * scale - row_lse[:, :, None], NEG_LARGE)
    return jnp.where(allowed, jnp.exp(shifted), 0.0)


def score_grads(probs, grad_probs, row_delta, scale):
    return (probs * (grad_probs - row_delta[:, :, None]) * scale).astype(jnp.bfloat16)


def per_device_ctx(
    layer_in,
    block_order,
    ln1_gain,
    ln1_shift,
    w_qkv,
    b_query,
    b_value,
    w_out,
    b_out,
    ln2_gain,
    ln2_shift,
    w_up,
    b_up,
    w_down,
    b_down,
    cotangent,
):
    full = (
        lax.all_gather(ln1_gain, "fsdp", axis=0, tiled=True),
        lax.all_gather(ln1_shift, "fsdp", axis=0, tiled=True),
        lax.all_gather(w_qkv, "fsdp", axis=0, tiled=True),
        lax.all_gather(b_query, "fsdp", axis=0, tiled=True),
        lax.all_gather(b_value, "fsdp", axis=0, tiled=True),
        lax.all_gather(w_out, "fsdp", axis=0, tiled=True),
        lax.all_gather(b_out, "fsdp", axis=0, tiled=True),
        lax.all_gather(ln2_gain, "fsdp", axis=0, tiled=True),
        lax.all_gather(ln2_shift, "fsdp", axis=0, tiled=True),
        lax.all_gather(w_up, "fsdp", axis=0, tiled=True),
        lax.all_gather(b_up, "fsdp", axis=0, tiled=True),
        lax.all_gather(w_down, "fsdp", axis=0, tiled=True),
        lax.all_gather(b_down, "fsdp", axis=0, tiled=True),
    )
    qkv_full, out_full, up_full, down_full = (full[2], full[5], full[9], full[11])
    first_gain = full[0].astype(jnp.float32)
    first_shift = full[1].astype(jnp.float32)
    query_bias = full[3].astype(jnp.float32)
    value_bias = full[4].astype(jnp.float32)
    out_bias = full[6].astype(jnp.float32)
    second_gain = full[7].astype(jnp.float32)
    second_shift = full[8].astype(jnp.float32)
    up_bias = full[10].astype(jnp.float32)
    down_bias = full[12].astype(jnp.float32)
    micro = layer_in.shape[0]
    tokens = layer_in.shape[1]
    seq_len = tokens * lax.axis_size("ctx")
    half_rows = tokens // 2
    key_block = min(512, seq_len)
    blocks = seq_len // key_block
    scale = HEAD_DIM ** (-0.5)
    here = lax.axis_index("ctx")
    heads_shape = (blocks, key_block, HEADS, HEAD_DIM)
    totals = [jnp.zeros(item.shape, jnp.float32) for item in full]
    outputs_fwd = []
    outputs_grad = []
    for micro_step in range(micro):
        pos_all = token_positions(block_order[micro_step], seq_len, half_rows)
        pos_mine = lax.dynamic_slice_in_dim(pos_all, here * tokens, tokens)
        pos_blocks = pos_all.reshape(blocks, key_block)
        inputs = layer_in[micro_step].astype(jnp.float32)
        first_out, first_normed, first_inv = normalize(inputs, first_gain, first_shift)
        first_low = first_out.astype(jnp.bfloat16)
        projected = jnp.dot(first_low, qkv_full, preferred_element_type=jnp.float32)
        query_low = (projected[:, :D] + query_bias).astype(jnp.bfloat16)
        key_low = projected[:, D : 2 * D].astype(jnp.bfloat16)
        value_low = (projected[:, 2 * D :] + value_bias).astype(jnp.bfloat16)
        keys_all, values_all = (
            lax.all_gather(key_low, "ctx", axis=0, tiled=True),
            lax.all_gather(value_low, "ctx", axis=0, tiled=True),
        )
        query_heads = query_low.reshape(tokens, HEADS, HEAD_DIM)
        key_blocks = keys_all.reshape(heads_shape)
        value_blocks = values_all.reshape(heads_shape)

        def stats_step(carry, piece):
            run_max, run_sum = carry
            key_piece, key_pos = piece
            raw_scores = (
                jnp.einsum(
                    "qhd,khd->hqk", query_heads, key_piece, preferred_element_type=jnp.float32
                )
                * scale
            )
            allowed = (pos_mine[:, None] >= key_pos[None, :])[None]
            masked = jnp.where(allowed, raw_scores, NEG_LARGE)
            new_max = jnp.maximum(run_max, jnp.max(masked, axis=-1))
            weights = jnp.where(allowed, jnp.exp(masked - new_max[:, :, None]), 0.0)
            run_sum = run_sum * jnp.exp(run_max - new_max) + jnp.sum(weights, axis=-1)
            return ((new_max, run_sum), None)

        start_state = (
            jnp.full((HEADS, tokens), NEG_LARGE, jnp.float32),
            jnp.zeros((HEADS, tokens), jnp.float32),
        )
        (run_max, run_sum), unused = lax.scan(stats_step, start_state, (key_blocks, pos_blocks))
        row_lse = run_max + jnp.log(run_sum)

        def output_step(carry, piece):
            acc_low, acc_exact = carry
            key_piece, value_piece, key_pos = piece
            probs = block_probs(query_heads, key_piece, pos_mine, key_pos, row_lse, scale)
            acc_low = acc_low + jnp.einsum(
                "hqk,khd->hqd",
                probs.astype(jnp.bfloat16),
                value_piece,
                preferred_element_type=jnp.float32,
            )
            acc_exact = acc_exact + jnp.einsum(
                "hqk,khd->hqd",
                probs,
                value_piece.astype(jnp.float32),
                preferred_element_type=jnp.float32,
            )
            return ((acc_low, acc_exact), None)

        start_acc = (
            jnp.zeros((HEADS, tokens, HEAD_DIM), jnp.float32),
            jnp.zeros((HEADS, tokens, HEAD_DIM), jnp.float32),
        )
        (attn_heads, exact_heads), unused = lax.scan(
            output_step, start_acc, (key_blocks, value_blocks, pos_blocks)
        )
        attn_low = jnp.transpose(attn_heads, (1, 0, 2)).reshape(tokens, D).astype(jnp.bfloat16)
        resid = inputs + jnp.dot(attn_low, out_full, preferred_element_type=jnp.float32) + out_bias
        second_out, second_normed, second_inv = normalize(resid, second_gain, second_shift)
        second_low = second_out.astype(jnp.bfloat16)
        hidden = jnp.dot(second_low, up_full, preferred_element_type=jnp.float32) + up_bias
        active_low = gelu_tanh(hidden).astype(jnp.bfloat16)
        result = (
            resid + jnp.dot(active_low, down_full, preferred_element_type=jnp.float32) + down_bias
        )
        outputs_fwd.append(result.astype(jnp.bfloat16))
        grad_out = cotangent[micro_step]
        grad_outf = grad_out.astype(jnp.float32)
        term_down = jnp.einsum(
            "tf,td->fd", active_low, grad_out, preferred_element_type=jnp.float32
        )
        grad_active = jnp.einsum(
            "td,fd->tf", grad_out, down_full, preferred_element_type=jnp.float32
        )
        grad_hidden = (grad_active * gelu_slope(hidden)).astype(jnp.bfloat16)
        term_up = jnp.einsum(
            "td,tf->df", second_low, grad_hidden, preferred_element_type=jnp.float32
        )
        grad_second = jnp.einsum(
            "tf,df->td", grad_hidden, up_full, preferred_element_type=jnp.float32
        )
        grad_resid = grad_outf + normalize_back(grad_second, second_normed, second_inv, second_gain)
        grad_branch = grad_resid.astype(jnp.bfloat16)
        term_out = jnp.einsum(
            "td,te->de", attn_low, grad_branch, preferred_element_type=jnp.float32
        )
        grad_attn = jnp.einsum(
            "te,de->td", grad_branch, out_full, preferred_element_type=jnp.float32
        ).astype(jnp.bfloat16)
        grad_heads = grad_attn.reshape(tokens, HEADS, HEAD_DIM)
        row_delta = jnp.einsum("qhd,hqd->hq", grad_heads.astype(jnp.float32), exact_heads)

        def backward_step(grad_query, piece):
            key_piece, value_piece, key_pos = piece
            probs = block_probs(query_heads, key_piece, pos_mine, key_pos, row_lse, scale)
            grad_value = jnp.einsum(
                "hqk,qhd->khd",
                probs.astype(jnp.bfloat16),
                grad_heads,
                preferred_element_type=jnp.float32,
            )
            grad_probs = jnp.einsum(
                "qhd,khd->hqk", grad_heads, value_piece, preferred_element_type=jnp.float32
            )
            grad_scores = score_grads(probs, grad_probs, row_delta, scale)
            grad_query = grad_query + jnp.einsum(
                "hqk,khd->qhd", grad_scores, key_piece, preferred_element_type=jnp.float32
            )
            grad_key = jnp.einsum(
                "hqk,qhd->khd", grad_scores, query_heads, preferred_element_type=jnp.float32
            )
            rows_here = key_piece.shape[0]
            return (
                grad_query,
                jnp.concatenate(
                    [grad_key.reshape(rows_here, D), grad_value.reshape(rows_here, D)], axis=1
                ),
            )

        grad_query, key_terms = lax.scan(
            backward_step,
            jnp.zeros((tokens, HEADS, HEAD_DIM), jnp.float32),
            (key_blocks, value_blocks, pos_blocks),
        )
        key_sums = lax.psum_scatter(
            key_terms.reshape(seq_len, 2 * D), "ctx", scatter_dimension=0, tiled=True
        )
        grad_key_low = key_sums[:, :D].astype(jnp.bfloat16)
        grad_value_low = key_sums[:, D:].astype(jnp.bfloat16)
        grad_query_low = grad_query.reshape(tokens, D).astype(jnp.bfloat16)
        grad_projected = jnp.concatenate([grad_query_low, grad_key_low, grad_value_low], axis=1)
        term_qkv = jnp.einsum(
            "td,te->de", first_low, grad_projected, preferred_element_type=jnp.float32
        )
        grad_first = jnp.einsum(
            "te,de->td", grad_projected, qkv_full, preferred_element_type=jnp.float32
        )
        grad_input = grad_resid + normalize_back(grad_first, first_normed, first_inv, first_gain)
        outputs_grad.append(grad_input.astype(jnp.bfloat16))
        terms = (
            jnp.sum(grad_first * first_normed, axis=0),
            jnp.sum(grad_first, axis=0),
            term_qkv,
            jnp.sum(grad_query_low.astype(jnp.float32), axis=0),
            jnp.sum(grad_value_low.astype(jnp.float32), axis=0),
            term_out,
            jnp.sum(grad_branch.astype(jnp.float32), axis=0),
            jnp.sum(grad_second * second_normed, axis=0),
            jnp.sum(grad_second, axis=0),
            term_up,
            jnp.sum(grad_hidden.astype(jnp.float32), axis=0),
            term_down,
            jnp.sum(grad_outf, axis=0),
        )
        totals = [older + newer for older, newer in zip(totals, terms)]
    summed = (
        lax.psum_scatter(totals[0], ("ctx", "fsdp"), scatter_dimension=0, tiled=True),
        lax.psum_scatter(totals[1], ("ctx", "fsdp"), scatter_dimension=0, tiled=True),
        lax.psum_scatter(totals[2], ("ctx", "fsdp"), scatter_dimension=0, tiled=True),
        lax.psum_scatter(totals[3], ("ctx", "fsdp"), scatter_dimension=0, tiled=True),
        lax.psum_scatter(totals[4], ("ctx", "fsdp"), scatter_dimension=0, tiled=True),
        lax.psum_scatter(totals[5], ("ctx", "fsdp"), scatter_dimension=0, tiled=True),
        lax.psum_scatter(totals[6], ("ctx", "fsdp"), scatter_dimension=0, tiled=True),
        lax.psum_scatter(totals[7], ("ctx", "fsdp"), scatter_dimension=0, tiled=True),
        lax.psum_scatter(totals[8], ("ctx", "fsdp"), scatter_dimension=0, tiled=True),
        lax.psum_scatter(totals[9], ("ctx", "fsdp"), scatter_dimension=0, tiled=True),
        lax.psum_scatter(totals[10], ("ctx", "fsdp"), scatter_dimension=0, tiled=True),
        lax.psum_scatter(totals[11], ("ctx", "fsdp"), scatter_dimension=0, tiled=True),
        lax.psum_scatter(totals[12], ("ctx", "fsdp"), scatter_dimension=0, tiled=True),
    )
    return (
        jnp.stack(outputs_fwd),
        jnp.stack(outputs_grad),
        summed[0],
        summed[1],
        summed[2],
        summed[3],
        summed[4],
        summed[5],
        summed[6],
        summed[7],
        summed[8],
        summed[9],
        summed[10],
        summed[11],
        summed[12],
    )


def gather_z(item, axis=0):
    return lax.all_gather(item, "fsdp", axis=axis, tiled=True)


def per_device_tp(
    layer_in,
    block_order,
    ln1_gain,
    ln1_shift,
    w_qkv,
    b_query,
    b_value,
    w_out,
    b_out,
    ln2_gain,
    ln2_shift,
    w_up,
    b_up,
    w_down,
    b_down,
    cotangent,
):
    n_ctx = lax.axis_size("ctx")
    n_z = lax.axis_size("fsdp")
    mine = lax.axis_index("ctx")
    seqs, tokens, width = layer_in.shape
    seq_len = tokens * n_ctx
    half_rows = tokens // 2
    ff = w_up.shape[1]
    hid = ff // (n_ctx * n_z)
    scale = HEAD_DIM ** (-0.5)
    f32, bf16 = jnp.float32, jnp.bfloat16

    def pick(item, count):
        return lax.dynamic_slice_in_dim(item, mine * count, count, axis=0)

    smalls = gather_z(
        jnp.stack(
            [ln1_gain, ln1_shift, b_query, b_value, b_out, ln2_gain, ln2_shift, b_down]
            + [b_up.reshape(n_z, -1)[part] for part in range(n_z)]
        ),
        axis=1,
    ).astype(f32)
    first_gain, first_shift, query_bias, value_bias, out_bias, second_gain, second_shift, down_bias = (
        smalls[row] for row in range(8)
    )
    up_bias = jnp.transpose(smalls[8:].reshape(n_z, n_z, -1), (1, 0, 2)).reshape(n_z, n_ctx, hid)
    up_bias = lax.dynamic_index_in_dim(up_bias, mine, axis=1, keepdims=False).reshape(-1)
    query_bias = pick(query_bias, HEAD_DIM)
    value_bias = pick(value_bias, HEAD_DIM)

    rows_z = w_qkv.shape[0]
    qkv_slice = lax.dynamic_index_in_dim(
        w_qkv.reshape(rows_z, 3, HEADS, HEAD_DIM), mine, axis=2, keepdims=False
    ).reshape(rows_z, 3 * HEAD_DIM)
    up_slice = lax.dynamic_index_in_dim(
        w_up.reshape(rows_z, n_z, n_ctx, hid), mine, axis=2, keepdims=False
    ).reshape(rows_z, n_z * hid)
    down_slice = pick(w_down, hid)
    qkv_w = gather_z(qkv_slice)
    out_w = gather_z(w_out)
    up_w = gather_z(up_slice)
    down_w = gather_z(down_slice)

    inputs = layer_in.astype(f32)
    first_out, first_normed, first_inv = normalize(inputs, first_gain, first_shift)
    h1 = lax.all_gather(first_out.astype(bf16), "ctx", axis=1, tiled=True)
    cot = lax.all_gather(cotangent, "ctx", axis=1, tiled=True)
    projected = jnp.einsum("std,de->ste", h1, qkv_w, preferred_element_type=f32)
    query = (projected[..., :HEAD_DIM] + query_bias).astype(bf16)
    key = projected[..., HEAD_DIM : 2 * HEAD_DIM].astype(bf16)
    value = (projected[..., 2 * HEAD_DIM :] + value_bias).astype(bf16)
    pos = jnp.stack([token_positions(block_order[s], seq_len, half_rows) for s in range(seqs)])
    allowed = pos[:, :, None] >= pos[:, None, :]
    scores = jnp.einsum("sqd,skd->sqk", query, key, preferred_element_type=f32) * scale
    scores = jnp.where(allowed, scores, NEG_LARGE)
    top = jnp.max(scores, axis=-1, keepdims=True)
    weights = jnp.where(allowed, jnp.exp(scores - top), 0.0)
    probs = weights / jnp.sum(weights, axis=-1, keepdims=True)
    probs_low = probs.astype(bf16)
    attn = jnp.einsum("sqk,skd->sqd", probs_low, value, preferred_element_type=f32).astype(bf16)
    attn_low = lax.all_to_all(attn, "ctx", split_axis=1, concat_axis=2, tiled=True)
    resid = inputs + jnp.einsum("std,de->ste", attn_low, out_w, preferred_element_type=f32) + out_bias
    second_out, second_normed, second_inv = normalize(resid, second_gain, second_shift)
    h2 = lax.all_gather(second_out.astype(bf16), "ctx", axis=1, tiled=True)
    hidden = jnp.einsum("std,df->stf", h2, up_w, preferred_element_type=f32) + up_bias
    active = gelu_tanh(hidden).astype(bf16)
    down_part = jnp.einsum("stf,fd->std", active, down_w, preferred_element_type=f32)
    grad_active = jnp.einsum("std,fd->stf", cot, down_w, preferred_element_type=f32)
    grad_hidden = (grad_active * gelu_slope(hidden)).astype(bf16)
    second_part = jnp.einsum("stf,df->std", grad_hidden, up_w, preferred_element_type=f32)
    term_down = jnp.einsum("stf,std->fd", active, cot, preferred_element_type=f32)
    term_up = jnp.einsum("std,stf->df", h2, grad_hidden, preferred_element_type=f32)
    down_sum = lax.psum_scatter(down_part, "ctx", scatter_dimension=1, tiled=True)
    grad_second = lax.psum_scatter(second_part, "ctx", scatter_dimension=1, tiled=True)
    result = (resid + down_sum + down_bias).astype(bf16)
    grad_outf = cotangent.astype(f32)
    grad_resid = grad_outf + normalize_back(grad_second, second_normed, second_inv, second_gain)
    grad_branch = grad_resid.astype(bf16)
    term_out = jnp.einsum("std,ste->de", attn_low, grad_branch, preferred_element_type=f32)
    grad_attn = jnp.einsum("ste,de->std", grad_branch, out_w, preferred_element_type=f32).astype(bf16)
    dout = lax.all_to_all(grad_attn, "ctx", split_axis=2, concat_axis=1, tiled=True)
    grad_value = jnp.einsum("sqk,sqd->skd", probs_low, dout, preferred_element_type=f32)
    grad_probs = jnp.einsum("sqd,skd->sqk", dout, value, preferred_element_type=f32)
    delta = jnp.sum(probs * grad_probs, axis=-1, keepdims=True)
    grad_scores = (probs * (grad_probs - delta) * scale).astype(bf16)
    grad_query = jnp.einsum("sqk,skd->sqd", grad_scores, key, preferred_element_type=f32)
    grad_key = jnp.einsum("sqk,sqd->skd", grad_scores, query, preferred_element_type=f32)
    grad_proj = jnp.concatenate([grad_query, grad_key, grad_value], axis=-1).astype(bf16)
    term_qkv = jnp.einsum("std,ste->de", h1, grad_proj, preferred_element_type=f32)
    first_part = jnp.einsum("ste,de->std", grad_proj, qkv_w, preferred_element_type=f32)
    grad_first = lax.psum_scatter(first_part, "ctx", scatter_dimension=1, tiled=True)
    grad_input = grad_resid + normalize_back(grad_first, first_normed, first_inv, first_gain)

    both = (0, 1)
    grad_projf = grad_proj.astype(f32)
    every = jnp.stack(
        [
            jnp.sum(grad_first * first_normed, axis=both),
            jnp.sum(grad_first, axis=both),
            jnp.sum(grad_branch.astype(f32), axis=both),
            jnp.sum(grad_second * second_normed, axis=both),
            jnp.sum(grad_second, axis=both),
            jnp.sum(grad_outf, axis=both),
        ]
    )
    every = lax.psum_scatter(every, ("ctx", "fsdp"), scatter_dimension=1, tiled=True)
    sum_query = jnp.sum(grad_projf[..., :HEAD_DIM], axis=both)
    sum_value = jnp.sum(grad_projf[..., 2 * HEAD_DIM :], axis=both)
    own = lax.psum_scatter(
        jnp.stack([sum_query, sum_value]), "fsdp", scatter_dimension=1, tiled=True
    )

    def to_owner(block):
        moves = []
        for col in range(n_ctx):
            for layer in range(n_z):
                place = layer * n_ctx + col
                moves.append((col * n_z + layer, place))
        return lax.ppermute(block, ("ctx", "fsdp"), moves)

    grad_down = to_owner(lax.psum_scatter(term_down, "fsdp", scatter_dimension=0, tiled=True))
    up_sum = jnp.sum(grad_hidden.astype(f32), axis=both)
    grad_up_bias = to_owner(lax.psum_scatter(up_sum, "fsdp", scatter_dimension=0, tiled=True))

    def rows_to_owner(term, groups):
        cols = term.shape[1]
        part = term.reshape(n_ctx, n_z, -1, cols)
        part = lax.psum_scatter(part, "fsdp", scatter_dimension=1, tiled=True)[:, 0]
        part = lax.all_to_all(part, "ctx", split_axis=0, concat_axis=0, tiled=True)
        part = part.reshape(n_ctx, -1, groups, cols // groups)
        return jnp.transpose(part, (1, 2, 0, 3)).reshape(part.shape[1], n_ctx * cols)

    grad_up = rows_to_owner(term_up, n_z)
    grad_qkv = rows_to_owner(term_qkv, 3)
    grad_out_w = lax.psum_scatter(term_out, ("ctx", "fsdp"), scatter_dimension=0, tiled=True)
    return (
        result,
        grad_input.astype(bf16),
        every[0],
        every[1],
        grad_qkv,
        own[0],
        own[1],
        grad_out_w,
        every[2],
        every[3],
        every[4],
        grad_up,
        grad_up_bias,
        grad_down,
        every[5],
    )


def solution(mesh):
    placed = (
        P("fsdp", "ctx", None),
        P("fsdp", None),
        P("fsdp"),
        P("fsdp"),
        P("fsdp", None),
        P("fsdp"),
        P("fsdp"),
        P("fsdp", None),
        P("fsdp"),
        P("fsdp"),
        P("fsdp"),
        P("fsdp", None),
        P("fsdp"),
        P("fsdp", None),
        P("fsdp"),
        P("fsdp", "ctx", None),
    )
    by_heads = mesh.shape["ctx"] == HEADS
    return jax.shard_map(
        per_device_tp if by_heads else per_device_ctx,
        mesh=mesh,
        in_specs=placed,
        out_specs=(
            P("fsdp", "ctx", None),
            P("fsdp", "ctx", None),
            P(("ctx", "fsdp")),
            P(("ctx", "fsdp")),
            P(("ctx", "fsdp"), None),
            P(("ctx", "fsdp")),
            P(("ctx", "fsdp")),
            P(("ctx", "fsdp"), None),
            P(("ctx", "fsdp")),
            P(("ctx", "fsdp")),
            P(("ctx", "fsdp")),
            P(("ctx", "fsdp"), None),
            P(("ctx", "fsdp")),
            P(("ctx", "fsdp"), None),
            P(("ctx", "fsdp")),
        ),
        check_vma=False,
    )
```

```python
import math
import types

import jax
import jax.numpy as jnp
from jax import lax
from jax.experimental import pallas as pl
from jax.experimental.pallas import tpu as pltpu
from jax.sharding import PartitionSpec as P

D = 1024
HEADS = 8
HEAD_DIM = 128


EPSILON = 1e-05
NEG_LARGE = -1e30
GELU_C = math.sqrt(2.0 / math.pi)
GELU_K = 0.044715
VMEM_BYTES = 63 << 20


def gelu_tanh(values):
    inner = jnp.tanh(GELU_C * (values + GELU_K * values * values * values))
    return 0.5 * values * (1.0 + inner)


def gelu_slope(values):
    inner = jnp.tanh(GELU_C * (values + GELU_K * values * values * values))
    return 0.5 * (1.0 + inner) + 0.5 * values * (1.0 - inner * inner) * GELU_C * (
        1.0 + 3.0 * GELU_K * values * values
    )


def normalize(values, gain_vec, shift_vec):
    average = jnp.mean(values, axis=-1, keepdims=True)
    centered = values - average
    inv_dev = lax.rsqrt(jnp.mean(centered * centered, axis=-1, keepdims=True) + EPSILON)
    normed = centered * inv_dev
    return (normed * gain_vec + shift_vec, normed, inv_dev)


def normalize_back(grad, normed, inv_dev, gain_vec):
    scaled = grad * gain_vec
    return inv_dev * (
        scaled
        - jnp.mean(scaled, axis=-1, keepdims=True)
        - normed * jnp.mean(scaled * normed, axis=-1, keepdims=True)
    )


def token_positions(order_row, seq_len, half_rows):
    rows = jnp.arange(seq_len, dtype=jnp.int32)
    slots = jnp.arange(order_row.shape[0], dtype=jnp.int32)
    picked = jnp.sum(
        jnp.where((rows // half_rows)[:, None] == slots[None, :], order_row[None, :], 0), axis=1
    )
    return picked * half_rows + rows % half_rows


def block_probs(query_heads, key_heads, query_pos, key_pos, row_lse, scale):
    raw_scores = jnp.einsum(
        "qhd,khd->hqk", query_heads, key_heads, preferred_element_type=jnp.float32
    )
    allowed = (query_pos[:, None] >= key_pos[None, :])[None]
    shifted = jnp.where(allowed, raw_scores * scale - row_lse[:, :, None], NEG_LARGE)
    return jnp.where(allowed, jnp.exp(shifted), 0.0)


def score_grads(probs, grad_probs, row_delta, scale):
    return (probs * (grad_probs - row_delta[:, :, None]) * scale).astype(jnp.bfloat16)


def per_device_ctx(
    layer_in,
    block_order,
    ln1_gain,
    ln1_shift,
    w_qkv,
    b_query,
    b_value,
    w_out,
    b_out,
    ln2_gain,
    ln2_shift,
    w_up,
    b_up,
    w_down,
    b_down,
    cotangent,
):
    full = (
        lax.all_gather(ln1_gain, "fsdp", axis=0, tiled=True),
        lax.all_gather(ln1_shift, "fsdp", axis=0, tiled=True),
        lax.all_gather(w_qkv, "fsdp", axis=0, tiled=True),
        lax.all_gather(b_query, "fsdp", axis=0, tiled=True),
        lax.all_gather(b_value, "fsdp", axis=0, tiled=True),
        lax.all_gather(w_out, "fsdp", axis=0, tiled=True),
        lax.all_gather(b_out, "fsdp", axis=0, tiled=True),
        lax.all_gather(ln2_gain, "fsdp", axis=0, tiled=True),
        lax.all_gather(ln2_shift, "fsdp", axis=0, tiled=True),
        lax.all_gather(w_up, "fsdp", axis=0, tiled=True),
        lax.all_gather(b_up, "fsdp", axis=0, tiled=True),
        lax.all_gather(w_down, "fsdp", axis=0, tiled=True),
        lax.all_gather(b_down, "fsdp", axis=0, tiled=True),
    )
    qkv_full, out_full, up_full, down_full = (full[2], full[5], full[9], full[11])
    first_gain = full[0].astype(jnp.float32)
    first_shift = full[1].astype(jnp.float32)
    query_bias = full[3].astype(jnp.float32)
    value_bias = full[4].astype(jnp.float32)
    out_bias = full[6].astype(jnp.float32)
    second_gain = full[7].astype(jnp.float32)
    second_shift = full[8].astype(jnp.float32)
    up_bias = full[10].astype(jnp.float32)
    down_bias = full[12].astype(jnp.float32)
    micro = layer_in.shape[0]
    tokens = layer_in.shape[1]
    seq_len = tokens * lax.axis_size("ctx")
    half_rows = tokens // 2
    key_block = min(512, seq_len)
    blocks = seq_len // key_block
    scale = HEAD_DIM ** (-0.5)
    here = lax.axis_index("ctx")
    heads_shape = (blocks, key_block, HEADS, HEAD_DIM)
    totals = [jnp.zeros(item.shape, jnp.float32) for item in full]
    outputs_fwd = []
    outputs_grad = []
    for micro_step in range(micro):
        pos_all = token_positions(block_order[micro_step], seq_len, half_rows)
        pos_mine = lax.dynamic_slice_in_dim(pos_all, here * tokens, tokens)
        pos_blocks = pos_all.reshape(blocks, key_block)
        inputs = layer_in[micro_step].astype(jnp.float32)
        first_out, first_normed, first_inv = normalize(inputs, first_gain, first_shift)
        first_low = first_out.astype(jnp.bfloat16)
        projected = jnp.dot(first_low, qkv_full, preferred_element_type=jnp.float32)
        query_low = (projected[:, :D] + query_bias).astype(jnp.bfloat16)
        key_low = projected[:, D : 2 * D].astype(jnp.bfloat16)
        value_low = (projected[:, 2 * D :] + value_bias).astype(jnp.bfloat16)
        keys_all, values_all = (
            lax.all_gather(key_low, "ctx", axis=0, tiled=True),
            lax.all_gather(value_low, "ctx", axis=0, tiled=True),
        )
        query_heads = query_low.reshape(tokens, HEADS, HEAD_DIM)
        key_blocks = keys_all.reshape(heads_shape)
        value_blocks = values_all.reshape(heads_shape)

        def stats_step(carry, piece):
            run_max, run_sum = carry
            key_piece, key_pos = piece
            raw_scores = (
                jnp.einsum(
                    "qhd,khd->hqk", query_heads, key_piece, preferred_element_type=jnp.float32
                )
                * scale
            )
            allowed = (pos_mine[:, None] >= key_pos[None, :])[None]
            masked = jnp.where(allowed, raw_scores, NEG_LARGE)
            new_max = jnp.maximum(run_max, jnp.max(masked, axis=-1))
            weights = jnp.where(allowed, jnp.exp(masked - new_max[:, :, None]), 0.0)
            run_sum = run_sum * jnp.exp(run_max - new_max) + jnp.sum(weights, axis=-1)
            return ((new_max, run_sum), None)

        start_state = (
            jnp.full((HEADS, tokens), NEG_LARGE, jnp.float32),
            jnp.zeros((HEADS, tokens), jnp.float32),
        )
        (run_max, run_sum), unused = lax.scan(stats_step, start_state, (key_blocks, pos_blocks))
        row_lse = run_max + jnp.log(run_sum)

        def output_step(carry, piece):
            acc_low, acc_exact = carry
            key_piece, value_piece, key_pos = piece
            probs = block_probs(query_heads, key_piece, pos_mine, key_pos, row_lse, scale)
            acc_low = acc_low + jnp.einsum(
                "hqk,khd->hqd",
                probs.astype(jnp.bfloat16),
                value_piece,
                preferred_element_type=jnp.float32,
            )
            acc_exact = acc_exact + jnp.einsum(
                "hqk,khd->hqd",
                probs,
                value_piece.astype(jnp.float32),
                preferred_element_type=jnp.float32,
            )
            return ((acc_low, acc_exact), None)

        start_acc = (
            jnp.zeros((HEADS, tokens, HEAD_DIM), jnp.float32),
            jnp.zeros((HEADS, tokens, HEAD_DIM), jnp.float32),
        )
        (attn_heads, exact_heads), unused = lax.scan(
            output_step, start_acc, (key_blocks, value_blocks, pos_blocks)
        )
        attn_low = jnp.transpose(attn_heads, (1, 0, 2)).reshape(tokens, D).astype(jnp.bfloat16)
        resid = inputs + jnp.dot(attn_low, out_full, preferred_element_type=jnp.float32) + out_bias
        second_out, second_normed, second_inv = normalize(resid, second_gain, second_shift)
        second_low = second_out.astype(jnp.bfloat16)
        hidden = jnp.dot(second_low, up_full, preferred_element_type=jnp.float32) + up_bias
        active_low = gelu_tanh(hidden).astype(jnp.bfloat16)
        result = (
            resid + jnp.dot(active_low, down_full, preferred_element_type=jnp.float32) + down_bias
        )
        outputs_fwd.append(result.astype(jnp.bfloat16))
        grad_out = cotangent[micro_step]
        grad_outf = grad_out.astype(jnp.float32)
        term_down = jnp.einsum(
            "tf,td->fd", active_low, grad_out, preferred_element_type=jnp.float32
        )
        grad_active = jnp.einsum(
            "td,fd->tf", grad_out, down_full, preferred_element_type=jnp.float32
        )
        grad_hidden = (grad_active * gelu_slope(hidden)).astype(jnp.bfloat16)
        term_up = jnp.einsum(
            "td,tf->df", second_low, grad_hidden, preferred_element_type=jnp.float32
        )
        grad_second = jnp.einsum(
            "tf,df->td", grad_hidden, up_full, preferred_element_type=jnp.float32
        )
        grad_resid = grad_outf + normalize_back(grad_second, second_normed, second_inv, second_gain)
        grad_branch = grad_resid.astype(jnp.bfloat16)
        term_out = jnp.einsum(
            "td,te->de", attn_low, grad_branch, preferred_element_type=jnp.float32
        )
        grad_attn = jnp.einsum(
            "te,de->td", grad_branch, out_full, preferred_element_type=jnp.float32
        ).astype(jnp.bfloat16)
        grad_heads = grad_attn.reshape(tokens, HEADS, HEAD_DIM)
        row_delta = jnp.einsum("qhd,hqd->hq", grad_heads.astype(jnp.float32), exact_heads)

        def backward_step(grad_query, piece):
            key_piece, value_piece, key_pos = piece
            probs = block_probs(query_heads, key_piece, pos_mine, key_pos, row_lse, scale)
            grad_value = jnp.einsum(
                "hqk,qhd->khd",
                probs.astype(jnp.bfloat16),
                grad_heads,
                preferred_element_type=jnp.float32,
            )
            grad_probs = jnp.einsum(
                "qhd,khd->hqk", grad_heads, value_piece, preferred_element_type=jnp.float32
            )
            grad_scores = score_grads(probs, grad_probs, row_delta, scale)
            grad_query = grad_query + jnp.einsum(
                "hqk,khd->qhd", grad_scores, key_piece, preferred_element_type=jnp.float32
            )
            grad_key = jnp.einsum(
                "hqk,qhd->khd", grad_scores, query_heads, preferred_element_type=jnp.float32
            )
            rows_here = key_piece.shape[0]
            return (
                grad_query,
                jnp.concatenate(
                    [grad_key.reshape(rows_here, D), grad_value.reshape(rows_here, D)], axis=1
                ),
            )

        grad_query, key_terms = lax.scan(
            backward_step,
            jnp.zeros((tokens, HEADS, HEAD_DIM), jnp.float32),
            (key_blocks, value_blocks, pos_blocks),
        )
        key_sums = lax.psum_scatter(
            key_terms.reshape(seq_len, 2 * D), "ctx", scatter_dimension=0, tiled=True
        )
        grad_key_low = key_sums[:, :D].astype(jnp.bfloat16)
        grad_value_low = key_sums[:, D:].astype(jnp.bfloat16)
        grad_query_low = grad_query.reshape(tokens, D).astype(jnp.bfloat16)
        grad_projected = jnp.concatenate([grad_query_low, grad_key_low, grad_value_low], axis=1)
        term_qkv = jnp.einsum(
            "td,te->de", first_low, grad_projected, preferred_element_type=jnp.float32
        )
        grad_first = jnp.einsum(
            "te,de->td", grad_projected, qkv_full, preferred_element_type=jnp.float32
        )
        grad_input = grad_resid + normalize_back(grad_first, first_normed, first_inv, first_gain)
        outputs_grad.append(grad_input.astype(jnp.bfloat16))
        terms = (
            jnp.sum(grad_first * first_normed, axis=0),
            jnp.sum(grad_first, axis=0),
            term_qkv,
            jnp.sum(grad_query_low.astype(jnp.float32), axis=0),
            jnp.sum(grad_value_low.astype(jnp.float32), axis=0),
            term_out,
            jnp.sum(grad_branch.astype(jnp.float32), axis=0),
            jnp.sum(grad_second * second_normed, axis=0),
            jnp.sum(grad_second, axis=0),
            term_up,
            jnp.sum(grad_hidden.astype(jnp.float32), axis=0),
            term_down,
            jnp.sum(grad_outf, axis=0),
        )
        totals = [older + newer for older, newer in zip(totals, terms)]
    summed = (
        lax.psum_scatter(totals[0], ("ctx", "fsdp"), scatter_dimension=0, tiled=True),
        lax.psum_scatter(totals[1], ("ctx", "fsdp"), scatter_dimension=0, tiled=True),
        lax.psum_scatter(totals[2], ("ctx", "fsdp"), scatter_dimension=0, tiled=True),
        lax.psum_scatter(totals[3], ("ctx", "fsdp"), scatter_dimension=0, tiled=True),
        lax.psum_scatter(totals[4], ("ctx", "fsdp"), scatter_dimension=0, tiled=True),
        lax.psum_scatter(totals[5], ("ctx", "fsdp"), scatter_dimension=0, tiled=True),
        lax.psum_scatter(totals[6], ("ctx", "fsdp"), scatter_dimension=0, tiled=True),
        lax.psum_scatter(totals[7], ("ctx", "fsdp"), scatter_dimension=0, tiled=True),
        lax.psum_scatter(totals[8], ("ctx", "fsdp"), scatter_dimension=0, tiled=True),
        lax.psum_scatter(totals[9], ("ctx", "fsdp"), scatter_dimension=0, tiled=True),
        lax.psum_scatter(totals[10], ("ctx", "fsdp"), scatter_dimension=0, tiled=True),
        lax.psum_scatter(totals[11], ("ctx", "fsdp"), scatter_dimension=0, tiled=True),
        lax.psum_scatter(totals[12], ("ctx", "fsdp"), scatter_dimension=0, tiled=True),
    )
    return (
        jnp.stack(outputs_fwd),
        jnp.stack(outputs_grad),
        summed[0],
        summed[1],
        summed[2],
        summed[3],
        summed[4],
        summed[5],
        summed[6],
        summed[7],
        summed[8],
        summed[9],
        summed[10],
        summed[11],
        summed[12],
    )


LOG2E = 1.4426950408889634
HOPS = 3
SMALL_ROWS = 16


def dot_as(left, right, left_dim, right_dim):
    return lax.dot_general(
        left, right, (((left_dim,), (right_dim,)), ((), ())), preferred_element_type=jnp.float32
    )


def dot_nn(left, right):
    return dot_as(left, right, 1, 0)


def dot_nt(left, right):
    return dot_as(left, right, 1, 1)


def dot_tn(left, right):
    return dot_as(left, right, 0, 0)


class Ring:
    def __init__(self):
        self.col = lax.axis_index("ctx")
        self.layer = lax.axis_index("fsdp")
        col = self.col
        self.sib = col + 1 - 2 * (col % 2)
        self.xnb = col + 2 - 4 * ((col // 2) % 2)
        self.ynb = col + 4 - 8 * (col // 4)
        self.diag = self.xnb + self.ynb - col
        self.xsib = self.xnb + self.sib - col
        self.ysib = self.ynb + self.sib - col
        self.dsib = self.diag + self.sib - col

    def flat(self, col):
        return (col, self.layer)

    def up(self, hop):
        return (self.layer + hop) % 4


def send(src, dst, send_sem, recv_sem, where):
    copy = pltpu.make_async_remote_copy(
        src_ref=src,
        dst_ref=dst,
        send_sem=send_sem,
        recv_sem=recv_sem,
        device_id=where,
        device_id_type=pl.DeviceIdType.MESH,
    )
    copy.start()
    return copy


def move(src, dst, sem):
    copy = pltpu.make_async_copy(src, dst, sem)
    copy.start()
    return copy


class Gather:
    def __init__(self, ring, block, half, ssem, rsem):
        self.ring, self.block, self.half = ring, block, half
        self.ssem, self.rsem = ssem, rsem
        self.open = []

    def go(self, ref, slot_s, slot_r, col):
        copy = send(ref, ref, self.ssem.at[slot_s], self.rsem.at[slot_r], self.ring.flat(col))
        self.open.append(copy)
        return copy

    def start(self):
        ring = self.ring
        own = self.block(ring.col)
        self.by_x = self.go(own, 0, 0, ring.xnb)
        self.by_y = self.go(own, 1, 1, ring.ynb)
        self.by_sib = self.go(own, 2, 2, ring.sib)

    def relay(self):
        ring = self.ring
        self.by_x.wait_recv()
        self.diag_y = self.go(self.half(ring.xnb, 0), 3, 3, ring.ynb)
        self.x_sib = self.go(self.block(ring.xnb), 4, 4, ring.sib)
        self.by_y.wait_recv()
        self.diag_x = self.go(self.half(ring.ynb, 1), 5, 5, ring.xnb)
        self.y_sib = self.go(self.block(ring.ynb), 6, 6, ring.sib)

    def relay_diag(self):
        ring = self.ring
        self.diag_y.wait_recv()
        self.diag_x.wait_recv()
        self.d_sib = self.go(self.block(ring.diag), 7, 7, ring.sib)

    def finish(self):
        self.by_sib.wait_recv()
        self.x_sib.wait_recv()
        self.y_sib.wait_recv()
        self.d_sib.wait_recv()

    def drain(self):
        for copy in self.open:
            copy.wait_send()


class Scatter:
    def __init__(self, ring, part, rows, from_sib, from_diag, from_side, ssem, rsem):
        self.ring, self.part, self.rows = ring, part, rows
        self.from_sib, self.from_diag, self.from_side = from_sib, from_diag, from_side
        self.ssem, self.rsem = ssem, rsem
        self.open = []

    def at(self, col, first=0, count=None):
        count = self.rows if count is None else count
        return pl.ds(pl.multiple_of(col * self.rows + first, count), count)

    def go(self, src, dst, slot, col):
        copy = send(src, dst, self.ssem.at[slot], self.rsem.at[slot], self.ring.flat(col))
        self.open.append(copy)
        return copy

    def start(self):
        ring = self.ring
        self.chip = {}
        for slot, col in ((3, ring.dsib), (1, ring.xsib), (2, ring.ysib), (0, ring.sib)):
            self.chip[slot] = self.go(
                self.part.at[self.at(col)], self.from_sib.at[slot], slot, ring.sib
            )

    def add(self, col, extra, first=0, count=None):
        where = self.at(col, first, count)
        total = self.part[where].astype(jnp.float32)
        for item in extra:
            total = total + item.astype(jnp.float32)
        self.part[where] = total.astype(jnp.bfloat16)

    def middle(self):
        ring = self.ring
        half = self.rows // 2
        self.chip[3].wait_recv()
        self.add(ring.diag, [self.from_sib[3]])
        self.diag_x = self.go(
            self.part.at[self.at(ring.diag, 0, half)], self.from_diag.at[0], 4, ring.xnb
        )
        self.diag_y = self.go(
            self.part.at[self.at(ring.diag, half, half)], self.from_diag.at[1], 5, ring.ynb
        )

    def last(self):
        ring = self.ring
        half = self.rows // 2
        self.chip[1].wait_recv()
        self.chip[2].wait_recv()
        self.diag_x.wait_recv()
        self.add(ring.ynb, [self.from_sib[2, :half], self.from_diag[0]], 0, half)
        self.add(ring.ynb, [self.from_sib[2, half:]], half, half)
        self.side_y = self.go(self.part.at[self.at(ring.ynb)], self.from_side.at[1], 7, ring.ynb)
        self.diag_y.wait_recv()
        self.add(ring.xnb, [self.from_sib[1, :half]], 0, half)
        self.add(ring.xnb, [self.from_sib[1, half:], self.from_diag[1]], half, half)
        self.side_x = self.go(self.part.at[self.at(ring.xnb)], self.from_side.at[0], 6, ring.xnb)

    def finish(self):
        self.chip[0].wait_recv()
        self.side_y.wait_recv()
        self.side_x.wait_recv()
        total = self.part[self.at(self.ring.col)].astype(jnp.float32)
        total = total + self.from_sib[0].astype(jnp.float32)
        return (
            total + self.from_side[0].astype(jnp.float32) + self.from_side[1].astype(jnp.float32)
        )

    def drain(self):
        for copy in self.open:
            copy.wait_send()


def row_norm(values):
    average = jnp.mean(values, axis=-1, keepdims=True)
    centered = values - average
    inv_dev = lax.rsqrt(jnp.mean(centered * centered, axis=-1, keepdims=True) + EPSILON)
    return centered * inv_dev, inv_dev


def layer_kernel(scale, refs):
    f32, bf16 = jnp.float32, jnp.bfloat16
    ring = Ring()
    col, layer = ring.col, ring.layer
    seqs, tokens, width = refs.x.shape
    seq_len = tokens * 8
    head = HEAD_DIM
    rows_z = width // 4
    hid = refs.wu.shape[1] // 4
    step_c2 = scale * LOG2E
    R = refs
    mine = pl.ds(pl.multiple_of(col * tokens, tokens), tokens)
    head_cols = pl.multiple_of(col * head, head)

    barrier = pltpu.get_barrier_semaphore()
    me = col * 4 + layer
    for hop in range(1, 32):
        other = (me + hop) % 32
        pl.semaphore_signal(
            barrier, 1, device_id=(other // 4, other % 4), device_id_type=pl.DeviceIdType.MESH
        )
    local = R.lsem
    load_x = move(R.x, R.xb, local.at[0])
    load_ct = [move(R.cot.at[s], R.ct.at[s, mine], local.at[1 + s]) for s in range(seqs)]
    qkv_rows = pl.ds(pl.multiple_of(layer * rows_z, rows_z), rows_z)
    load_q = []
    for g in range(3):
        src = R.w_qkv.at[:, pl.ds(pl.multiple_of(g * width + col * head, head), head)]
        load_q.append(move(src, R.wq.at[qkv_rows, g * head : (g + 1) * head], local.at[3 + g]))
    small_rows = 32
    out_src = R.w_out.at[pl.ds(pl.multiple_of(col * small_rows, small_rows), small_rows)]
    load_o = move(out_src, R.wo.at[layer, col], local.at[6])
    load_u = []
    for g in range(4):
        src = R.w_up.at[:, pl.ds(pl.multiple_of(g * width + col * hid, hid), hid)]
        load_u.append(move(src, R.wu.at[qkv_rows, g * hid : (g + 1) * hid], local.at[7 + g]))
    down_src = R.w_down.at[pl.ds(pl.multiple_of(col * hid, hid), hid)]
    down_rows = pl.ds(pl.multiple_of(layer * hid, hid), hid)
    load_d = move(down_src, R.wd.at[down_rows], local.at[11])
    R.par[layer] = R.params[...]
    pl.semaphore_wait(barrier, 31)

    zs, zr = R.zs, R.zr

    def to_planes(src, dst, slot):
        return [
            send(src, dst, zs.at[slot, hop - 1], zr.at[slot, hop - 1], (col, ring.up(hop)))
            for hop in range(1, 4)
        ]

    send_par = to_planes(R.params, R.par.at[layer], 0)
    send_q = []
    for g in range(3):
        src = R.w_qkv.at[:, pl.ds(pl.multiple_of(g * width + col * head, head), head)]
        send_q += to_planes(src, R.wq.at[qkv_rows, g * head : (g + 1) * head], 1 + g)

    def gather_rows(ref, s, slot):

        def block(index):
            return ref.at[s, pl.ds(pl.multiple_of(index * tokens, tokens), tokens)]

        def half(index, part):
            count = tokens // 2
            first = pl.multiple_of(index * tokens + part * count, count)
            return ref.at[s, pl.ds(first, count)]

        return Gather(ring, block, half, R.gs.at[slot], R.gr.at[slot])

    h1_gather = [gather_rows(R.h1, s, s) for s in range(seqs)]
    ct_gather = [gather_rows(R.ct, s, 2 + s) for s in range(seqs)]
    h2_gather = [gather_rows(R.h2, s, 4 + s) for s in range(seqs)]
    wo_gather = Gather(
        ring,
        lambda index: R.wo.at[:, index],
        lambda index, part: R.wo.at[2 * part : 2 * part + 2, index],
        R.gs.at[6],
        R.gr.at[6],
    )

    for s in range(seqs):
        lane = lax.broadcasted_iota(jnp.int32, (1, seq_len), 1)
        half_rows = tokens // 2
        pos = jnp.zeros((1, seq_len), jnp.int32)
        down = lax.broadcasted_iota(jnp.int32, (half_rows, 128), 0)
        for j in range(seq_len // half_rows):
            start = R.order[s, j] * half_rows
            pos = jnp.where(lane // half_rows == j, start, pos)
            R.kpos[s, j * half_rows : (j + 1) * half_rows, :] = down + start
        R.qpos[s] = pos + lane % half_rows

    load_x.wait()

    def params_row(row):
        return jnp.concatenate([R.par[k, row : row + 1, :] for k in range(4)], axis=1)

    def norm_one(s):
        return row_norm(R.xb[s].astype(f32))

    first = norm_one(0)
    for copy in send_par:
        copy.wait_recv()
    gain1, shift1 = params_row(0), params_row(1)
    R.h1[0, mine] = (first[0] * gain1 + shift1).astype(bf16)
    h1_gather[0].start()
    second = norm_one(1)
    R.h1[1, mine] = (second[0] * gain1 + shift1).astype(bf16)
    h1_gather[1].start()
    load_o.wait()
    send_o = to_planes(out_src, R.wo.at[layer, col], 4)
    send_u = []
    for g in range(4):
        src = R.w_up.at[:, pl.ds(pl.multiple_of(g * width + col * hid, hid), hid)]
        send_u += to_planes(src, R.wu.at[qkv_rows, g * hid : (g + 1) * hid], 5 + g)
    send_d = to_planes(down_src, R.wd.at[down_rows], 9)

    plane_lane = pl.ds(pl.multiple_of((col % 2) * head, head), head)
    held = [R.par[k, :, plane_lane] for k in range(4)]

    def held_row(first, parts):
        total = jnp.zeros((1, head), f32)
        for k, part in enumerate(parts):
            total = jnp.where(col // 2 == k, part[first(k) : first(k) + 1, :], total)
        return total

    bias_q = held_row(lambda k: 2, held)
    bias_v = held_row(lambda k: 3, held)
    bias_u = jnp.concatenate(
        [held_row(lambda k: 8 + k, [held[g]] * 4) for g in range(4)], axis=1
    )
    tile = 256

    def project(s):
        def body(t, _):
            r = pl.ds(pl.multiple_of(t * tile, tile), tile)
            both = dot_nn(R.h1[s, r, :], R.wq[...])
            R.q[s, r, :] = (both[:, :head] + bias_q).astype(bf16)
            R.k[s, r, :] = both[:, head : 2 * head].astype(bf16)
            R.v[s, r, :] = (both[:, 2 * head :] + bias_v).astype(bf16)
            return 0

        lax.fori_loop(0, seq_len // tile, body, 0)
        R.kt[s] = R.k[s].T
        R.vt[s] = R.v[s].T

    def masked(s, r, scores, other):
        keys = jnp.concatenate([R.kpos[s]] * (tile // 128), axis=1)
        return jnp.where(R.qpos[s, :, r] >= keys, scores, other)

    def attend(s):
        def body(t, _):
            r = pl.ds(pl.multiple_of(t * tile, tile), tile)
            raw = masked(s, r, dot_nt(R.k[s], R.q[s, r, :]), NEG_LARGE)
            top = jnp.max(raw, axis=0, keepdims=True)
            weights = jnp.exp2((raw - top) * step_c2)
            total = jnp.sum(weights, axis=0, keepdims=True)
            turned = dot_nn(R.vt[s], weights.astype(bf16)) * (1.0 / total)
            R.ol[s, r, :] = turned.T.astype(bf16)
            R.lse[s, :, r] = top * step_c2 + jnp.log2(total)
            return 0

        lax.fori_loop(0, seq_len // tile, body, 0)

    others = (ring.dsib, ring.diag, ring.xsib, ring.xnb, ring.ysib, ring.ynb, ring.sib)

    def heads_to_rows(s):
        R.ob[s, :, pl.ds(head_cols, head)] = R.ol[s, mine, :]
        copies = []
        for slot, other in enumerate(others):
            src = R.ol.at[s, pl.ds(pl.multiple_of(other * tokens, tokens), tokens)]
            dst = R.ob.at[s, :, pl.ds(head_cols, head)]
            copies.append(
                send(src, dst, R.a_s.at[s, slot], R.a_r.at[s, slot], ring.flat(other))
            )
        return copies

    def rows_to_heads(s):
        R.dh[s, mine, :] = R.db[s, :, pl.ds(head_cols, head)]
        copies = []
        for slot, other in enumerate(others):
            src = R.db.at[s, :, pl.ds(pl.multiple_of(other * head, head), head)]
            dst = R.dh.at[s, mine]
            copies.append(
                send(src, dst, R.a_s.at[2 + s, slot], R.a_r.at[2 + s, slot], ring.flat(other))
            )
        return copies

    h1_gather[0].relay()
    h1_gather[0].relay_diag()
    h1_gather[1].relay()
    h1_gather[0].finish()
    for copy in load_q:
        copy.wait()
    for copy in send_q:
        copy.wait_recv()
    project(0)
    h1_gather[1].relay_diag()
    for copy in send_o:
        copy.wait_recv()
    wo_gather.start()
    for copy in load_ct:
        copy.wait()
    ct_gather[0].start()
    attend(0)
    moved_o = [heads_to_rows(0)]
    wo_gather.relay()
    ct_gather[0].relay()
    h1_gather[1].finish()
    project(1)
    wo_gather.relay_diag()
    ct_gather[0].relay_diag()
    wo_gather.finish()
    ct_gather[1].start()

    bias_o = params_row(4)
    gain2, shift2 = params_row(5), params_row(6)
    out_w = R.wo

    def out_project(s):
        for copy in moved_o[s]:
            copy.wait_recv()
        weight = out_w[...].reshape(width, width)
        resid = R.xb[s].astype(f32) + dot_nn(R.ob[s], weight) + bias_o
        R.r1[s] = resid
        normed, _ = row_norm(resid)
        R.h2[s, mine] = (normed * gain2 + shift2).astype(bf16)

    out_project(0)
    h2_gather[0].start()
    attend(1)
    moved_o.append(heads_to_rows(1))
    ct_gather[1].relay()
    h2_gather[0].relay()
    ct_gather[1].relay_diag()
    h2_gather[0].relay_diag()
    out_project(1)
    h2_gather[1].start()
    for copy in load_u:
        copy.wait()
    for copy in send_u:
        copy.wait_recv()
    load_d.wait()
    for copy in send_d:
        copy.wait_recv()
    ct_gather[0].finish()
    h2_gather[0].finish()

    def feed(s):
        def body(t, sums):
            r = pl.ds(pl.multiple_of(t * tile, tile), tile)
            hidden = dot_nn(R.h2[s, r, :], R.wu[...]) + bias_u
            square = hidden * hidden
            bend = jnp.tanh(hidden * (GELU_C + (GELU_C * GELU_K) * square))
            half = 0.5 * (1.0 + bend)
            active = (hidden * half).astype(bf16)
            slope = half + (0.5 * hidden) * (1.0 - bend * bend) * (
                GELU_C + (3.0 * GELU_C * GELU_K) * square
            )
            R.act[s, r, :] = active
            R.po[s, r, :] = dot_nn(active, R.wd[...]).astype(bf16)
            grad = dot_nt(R.ct[s, r, :], R.wd[...])
            grad = (grad * slope).astype(bf16)
            R.du[s, r, :] = grad
            R.pd[s, r, :] = dot_nt(grad, R.wu[...]).astype(bf16)
            return sums + jnp.sum(grad.astype(f32), axis=0, keepdims=True)

        return lax.fori_loop(0, seq_len // tile, body, jnp.zeros((1, 4 * hid), f32))

    def scatter(part, s, recv, slot, rows=None):
        return Scatter(
            ring,
            part,
            tokens,
            R.r_sib.at[recv],
            R.r_diag.at[recv],
            R.r_side.at[recv],
            R.ss.at[slot],
            R.sr.at[slot],
        )

    up_sums = feed(0)
    d2 = [scatter(R.pd.at[s], s, s, s) for s in range(2)]
    out_sc = [scatter(R.po.at[s], s, 2 + s, 2 + s) for s in range(2)]
    d2[0].start()
    h2_gather[1].relay()
    h2_gather[1].relay_diag()
    d2[0].middle()
    ct_gather[1].finish()
    h2_gather[1].finish()
    d2[0].last()
    up_sums = up_sums + feed(1)
    d2[1].start()

    bz = R.bz
    for g in range(4):
        bz[2 + g : 3 + g, :] = up_sums[:, g * hid : (g + 1) * hid]

    down_slots, up_slots = [], []

    def grad_down():
        for j in range(2):
            cols = slice(j * 2 * hid, (j + 1) * 2 * hid)
            total = dot_tn(R.act[0, :, cols], R.ct[0])
            total = total + dot_tn(R.act[1, :, cols], R.ct[1])
            R.gd[cols, :] = total.astype(bf16)

    def grad_up():
        for j in range(2):
            cols = slice(j * 2 * hid, (j + 1) * 2 * hid)
            total = dot_tn(R.du[0, :, cols], R.h2[0])
            total = total + dot_tn(R.du[1, :, cols], R.h2[1])
            total = total.T.astype(bf16).reshape(8, 4, 32, 2 * hid)
            R.gu[:, :, :, cols] = total

    def to_planes_part(piece, dst, slot):
        return [
            send(
                piece(ring.up(hop)),
                dst.at[hop - 1],
                zs.at[slot, hop - 1],
                zr.at[slot, hop - 1],
                (col, ring.up(hop)),
            )
            for hop in range(1, 4)
        ]

    sums = {}

    def back_norm2(s):
        grad = d2[s].finish()
        normed, inv_dev = row_norm(R.r1[s])
        cot = R.ct[s, mine].astype(f32)
        scaled = grad * gain2
        resid = cot + inv_dev * (
            scaled
            - jnp.mean(scaled, axis=-1, keepdims=True)
            - normed * jnp.mean(scaled * normed, axis=-1, keepdims=True)
        )
        R.dr[s] = resid
        low = resid.astype(bf16)
        R.dz[s] = low
        lowf = low.astype(f32)
        parts = (
            jnp.sum(lowf, axis=0, keepdims=True),
            jnp.sum(grad * normed, axis=0, keepdims=True),
            jnp.sum(grad, axis=0, keepdims=True),
            jnp.sum(cot, axis=0, keepdims=True),
        )
        for row, item in enumerate(parts):
            sums[row] = sums[row] + item if row in sums else item
        R.db[s] = dot_nt(low, out_w[...].reshape(width, width)).astype(bf16)

    def attend_back(s):
        R.dka[...] = jnp.zeros_like(R.dka)
        R.dva[...] = jnp.zeros_like(R.dva)

        def body(t, _):
            r = pl.ds(pl.multiple_of(t * tile, tile), tile)
            query, dout = R.q[s, r, :], R.dh[s, r, :]
            raw = dot_nt(R.k[s], query)
            probs = masked(s, r, jnp.exp2(raw * step_c2 - R.lse[s, :, r]), 0.0)
            grad = dot_nt(R.v[s], dout)
            R.dva[...] += dot_nn(probs.astype(bf16), dout)
            delta = jnp.sum(probs * grad, axis=0, keepdims=True)
            low = (probs * ((grad - delta) * scale)).astype(bf16)
            R.dka[...] += dot_nn(low, query)
            R.dp[s, r, :head] = dot_nn(R.kt[s], low).T.astype(bf16)
            return 0

        lax.fori_loop(0, seq_len // tile, body, 0)
        R.dp[s, :, head : 2 * head] = R.dka[...].astype(bf16)
        R.dp[s, :, 2 * head :] = R.dva[...].astype(bf16)

    def first_part(s):
        def body(t, _):
            r = pl.ds(pl.multiple_of(t * tile, tile), tile)
            R.pd[s, r, :] = dot_nt(R.dp[s, r, :], R.wq[...]).astype(bf16)
            return 0

        lax.fori_loop(0, seq_len // tile, body, 0)

    back_norm2(0)
    moved_d = [rows_to_heads(0)]
    d2[1].middle()
    grad_down()
    z_down = to_planes_part(
        lambda other: R.gd.at[pl.ds(pl.multiple_of(other * hid, hid), hid)], R.zd, 10
    )
    d2[1].last()
    for copy in moved_d[0]:
        copy.wait_recv()
    attend_back(0)
    back_norm2(1)
    moved_d.append(rows_to_heads(1))
    d2[0].drain()
    first_part(0)
    d1 = [scatter(R.pd.at[s], s, s, 4 + s) for s in range(2)]
    d1[0].start()
    grad_up()
    z_up = to_planes_part(lambda other: R.gu.at[:, other], R.zu, 11)
    d1[0].middle()
    out_sc[0].start()
    for copy in moved_d[1]:
        copy.wait_recv()
    d1[0].last()
    out_sc[0].middle()
    attend_back(1)
    out_sc[0].last()
    d2[1].drain()
    first_part(1)
    d1[1].start()
    out_sc[1].start()

    for g in range(3):
        cols = slice(g * head, (g + 1) * head)
        total = dot_tn(R.dp[0, :, cols], R.h1[0]) + dot_tn(R.dp[1, :, cols], R.h1[1])
        R.gq[:, :, :, cols] = total.T.astype(bf16).reshape(8, 4, 32, head)
    z_q = to_planes_part(lambda other: R.gq.at[:, other], R.zq, 12)
    d1[1].middle()
    out_sc[1].middle()
    proj_sums = jnp.sum(R.dp[0].astype(f32), axis=0, keepdims=True) + jnp.sum(
        R.dp[1].astype(f32), axis=0, keepdims=True
    )
    bz[0:1, :] = proj_sums[:, :head]
    bz[1:2, :] = proj_sums[:, 2 * head :]
    bz[6:8, :] = jnp.zeros((2, head), f32)
    z_b = to_planes(bz, R.zb.at[layer], 13)
    d1[1].last()
    out_sc[1].last()

    h2_flat = R.h2.at[0]
    for copies in (h2_gather[0], h2_gather[1]):
        copies.drain()
    h2_flat[...] = (
        dot_tn(R.ob[0], R.dz[0]) + dot_tn(R.ob[1], R.dz[1])
    ).astype(bf16)
    wo_sc = scatter(h2_flat, 0, 4, 6)
    wo_sc.start()

    owner_col, owner_layer = 2 * layer + col // 4, col % 4
    at_home = owner_col * 4 + owner_layer == me
    for copy in z_down:
        copy.wait_recv()
    total = R.gd[down_rows].astype(f32)
    for k in range(3):
        total = total + R.zd[k].astype(f32)
    R.gdo[...] = total.astype(bf16)
    wo_sc.middle()
    for copy in z_b:
        copy.wait_recv()
    bz_all = bz[...] + (R.zb[ring.up(1)] + R.zb[ring.up(2)] + R.zb[ring.up(3)])
    R.bzs[...] = bz_all
    chosen = jnp.zeros((1, head), f32)
    for k in range(4):
        chosen = jnp.where(layer == k, bz_all[2 + k : 3 + k, :], chosen)
    R.bu[...] = jnp.broadcast_to(chosen, (8, head))
    psem = R.ps

    @pl.when(at_home)
    def _():
        one = move(R.gdo, R.o_gd, psem.at[0])
        two = move(R.bu, R.o_bu, psem.at[1])
        one.wait()
        two.wait()

    def away():
        where = (owner_col, owner_layer)
        one = pltpu.make_async_remote_copy(
            R.gdo, R.o_gd, psem.at[2], psem.at[3], where, pl.DeviceIdType.MESH
        )
        two = pltpu.make_async_remote_copy(
            R.bu, R.o_bu, psem.at[4], psem.at[5], where, pl.DeviceIdType.MESH
        )
        return one, two

    @pl.when(jnp.logical_not(at_home))
    def _():
        one, two = away()
        one.start()
        two.start()

    for copy in z_up:
        copy.wait_recv()
    total = R.gu[:, layer].astype(f32)
    for k in range(3):
        total = total + R.zu[k].astype(f32)
    R.guo[...] = total.astype(bf16)

    def to_columns(src, dst, row):
        keep = move(src.at[col], dst.at[col], local.at[12 + row])
        copies = []
        for slot, other in enumerate(others):
            copies.append(
                send(
                    src.at[other],
                    dst.at[col],
                    R.a_s.at[4 + row, slot],
                    R.a_r.at[4 + row, slot],
                    ring.flat(other),
                )
            )
        return keep, copies

    up_keep, up_moves = to_columns(R.guo, R.o_gu, 0)
    wo_sc.last()

    bias_d = params_row(7)

    def back_norm1(s):
        grad = d1[s].finish()
        normed, inv_dev = row_norm(R.xb[s].astype(f32))
        scaled = grad * gain1
        total = R.dr[s] + inv_dev * (
            scaled
            - jnp.mean(scaled, axis=-1, keepdims=True)
            - normed * jnp.mean(scaled * normed, axis=-1, keepdims=True)
        )
        R.igs[s] = total.astype(bf16)
        for row, item in ((4, grad * normed), (5, grad)):
            item = jnp.sum(item, axis=0, keepdims=True)
            sums[row] = sums[row] + item if row in sums else item

    back_norm1(0)
    back_norm1(1)
    for row in range(6):
        R.ev[row : row + 1, :] = sums[row]
    R.ev[6:8, :] = jnp.zeros((2, width), f32)
    save_ig = move(R.igs, R.o_ig, local.at[14])
    ev_moves = []
    for hop in range(1, 8):
        other = (col + hop) % 8
        ev_moves.append(
            send(
                R.ev.at[:, pl.ds(pl.multiple_of(other * head, head), head)],
                R.evr.at[hop - 1],
                R.es.at[hop - 1],
                R.er.at[hop - 1],
                ring.flat(other),
            )
        )
    for copy in z_q:
        copy.wait_recv()
    total = R.gq[:, layer].astype(f32)
    for k in range(3):
        total = total + R.zq[k].astype(f32)
    R.gqo[...] = total.astype(bf16)
    q_keep, q_moves = to_columns(R.gqo, R.o_gq, 1)
    for copy in ev_moves:
        copy.wait_recv()
    plane = R.ev[:, pl.ds(head_cols, head)]
    for k in range(7):
        plane = plane + R.evr[k]
    R.evp[...] = plane
    z_e = to_planes(R.evp, R.evz.at[layer], 14)
    go_rows = pl.ds(pl.multiple_of(layer * 32, 32), 32)
    own = wo_sc.finish()
    R.gws[...] = own.astype(bf16)
    z_o = to_planes_part(
        lambda other: R.gws.at[pl.ds(pl.multiple_of(other * 32, 32), 32)], R.zo, 15
    )
    for s in range(2):
        R.los[s] = (R.r1[s] + out_sc[s].finish() + bias_d).astype(bf16)
    save_lo = move(R.los, R.o_lo, local.at[15])
    for copy in z_e:
        copy.wait_recv()
    total = R.evp[...] + (R.evz[ring.up(1)] + R.evz[ring.up(2)] + R.evz[ring.up(3)])
    both = jnp.concatenate([total, R.bzs[...]], axis=0)
    picked = jnp.zeros((16, 32), f32)
    for k in range(4):
        picked = jnp.where(layer == k, both[:, k * 32 : (k + 1) * 32], picked)
    R.o_small[...] = picked
    for copy in z_o:
        copy.wait_recv()
    total = R.gws[go_rows].astype(f32)
    for k in range(3):
        total = total + R.zo[k].astype(f32)
    R.o_go[...] = total

    @pl.when(jnp.logical_not(at_home))
    def _():
        one, two = away()
        one.wait()
        two.wait()

    save_ig.wait()
    save_lo.wait()
    for keep, copies in ((up_keep, up_moves), (q_keep, q_moves)):
        keep.wait()
        for copy in copies:
            copy.wait()
    for group in (h1_gather, ct_gather, [wo_gather], d1, out_sc, [wo_sc]):
        for item in group:
            item.drain()
    for copies in (
        moved_o + moved_d + [send_par, send_q, send_o, send_u, send_d]
        + [z_down, z_up, z_q, z_b, z_e, z_o, ev_moves]
    ):
        for copy in copies:
            copy.wait_send()

def per_device_tp(
    layer_in,
    block_order,
    ln1_gain,
    ln1_shift,
    w_qkv,
    b_query,
    b_value,
    w_out,
    b_out,
    ln2_gain,
    ln2_shift,
    w_up,
    b_up,
    w_down,
    b_down,
    cotangent,
):
    f32, bf16, i32 = jnp.float32, jnp.bfloat16, jnp.int32
    seqs, tokens, width = layer_in.shape
    seq_len = tokens * 8
    ff = w_up.shape[1]
    hid = ff // 32
    params = jnp.concatenate(
        [
            jnp.stack([ln1_gain, ln1_shift, b_query, b_value, b_out, ln2_gain, ln2_shift, b_down]),
            b_up.reshape(4, -1),
            jnp.zeros((4, width // 4), bf16),
        ]
    ).astype(f32)
    anywhere = pl.BlockSpec(memory_space=pl.ANY)
    in_vmem = pl.BlockSpec(memory_space=pltpu.VMEM)
    inputs = dict(
        order=(block_order, pl.BlockSpec(memory_space=pltpu.SMEM)),
        params=(params, in_vmem),
        x=(layer_in, anywhere),
        cot=(cotangent, anywhere),
        w_qkv=(w_qkv, anywhere),
        w_out=(w_out, anywhere),
        w_up=(w_up, anywhere),
        w_down=(w_down, anywhere),
    )
    outputs = dict(
        o_lo=((seqs, tokens, width), bf16, anywhere),
        o_ig=((seqs, tokens, width), bf16, anywhere),
        o_gq=((8, 32, 3 * HEAD_DIM), bf16, anywhere),
        o_gu=((8, 32, 4 * hid), bf16, anywhere),
        o_gd=((hid, width), bf16, anywhere),
        o_go=((32, width), f32, in_vmem),
        o_small=((16, 32), f32, in_vmem),
        o_bu=((8, HEAD_DIM), f32, anywhere),
    )
    whole = (seqs, seq_len, width)
    heads = (seqs, seq_len, HEAD_DIM)
    turned = (seqs, HEAD_DIM, seq_len)
    own = (seqs, tokens, width)
    vmem, sems = pltpu.VMEM, pltpu.SemaphoreType.DMA
    scratch = dict(
        h1=vmem(whole, bf16),
        ct=vmem(whole, bf16),
        h2=vmem(whole, bf16),
        po=vmem(whole, bf16),
        pd=vmem(whole, bf16),
        wq=vmem((width, 3 * HEAD_DIM), bf16),
        wo=vmem((4, 8, 32, width), bf16),
        wu=vmem((width, 4 * hid), bf16),
        wd=vmem((4 * hid, width), bf16),
        q=vmem(heads, bf16),
        k=vmem(heads, bf16),
        v=vmem(heads, bf16),
        kt=vmem(turned, bf16),
        vt=vmem(turned, bf16),
        ol=vmem(heads, bf16),
        dh=vmem(heads, bf16),
        ob=vmem(own, bf16),
        db=vmem(own, bf16),
        xb=vmem(own, bf16),
        dz=vmem(own, bf16),
        igs=vmem(own, bf16),
        los=vmem(own, bf16),
        r1=vmem(own, f32),
        dr=vmem(own, f32),
        r_sib=vmem((5, 4, tokens, width), bf16),
        r_diag=vmem((5, 2, tokens // 2, width), bf16),
        r_side=vmem((5, 2, tokens, width), bf16),
        kpos=vmem(heads, i32),
        qpos=vmem((seqs, 1, seq_len), i32),
        lse=vmem((seqs, 1, seq_len), f32),
        act=vmem((seqs, seq_len, 4 * hid), bf16),
        du=vmem((seqs, seq_len, 4 * hid), bf16),
        dp=vmem((seqs, seq_len, 3 * HEAD_DIM), bf16),
        dka=vmem((seq_len, HEAD_DIM), f32),
        dva=vmem((seq_len, HEAD_DIM), f32),
        gd=vmem((4 * hid, width), bf16),
        gu=vmem((8, 4, 32, 4 * hid), bf16),
        gq=vmem((8, 4, 32, 3 * HEAD_DIM), bf16),
        gws=vmem((tokens, width), bf16),
        gdo=vmem((hid, width), bf16),
        guo=vmem((8, 32, 4 * hid), bf16),
        gqo=vmem((8, 32, 3 * HEAD_DIM), bf16),
        zd=vmem((3, hid, width), bf16),
        zu=vmem((3, 8, 32, 4 * hid), bf16),
        zq=vmem((3, 8, 32, 3 * HEAD_DIM), bf16),
        zo=vmem((3, 32, width), bf16),
        par=vmem((4, SMALL_ROWS, width // 4), f32),
        bz=vmem((8, HEAD_DIM), f32),
        bzs=vmem((8, HEAD_DIM), f32),
        bu=vmem((8, HEAD_DIM), f32),
        zb=vmem((4, 8, HEAD_DIM), f32),
        ev=vmem((8, width), f32),
        evr=vmem((7, 8, HEAD_DIM), f32),
        evp=vmem((8, HEAD_DIM), f32),
        evz=vmem((4, 8, HEAD_DIM), f32),
        lsem=sems((16,)),
        zs=sems((16, 3)),
        zr=sems((16, 3)),
        gs=sems((7, 8)),
        gr=sems((7, 8)),
        ss=sems((7, 8)),
        sr=sems((7, 8)),
        a_s=sems((6, 7)),
        a_r=sems((6, 7)),
        es=sems((7,)),
        er=sems((7,)),
        ps=sems((6,)),
    )
    names = list(inputs) + list(outputs) + list(scratch)

    def body(*refs):
        layer_kernel(HEAD_DIM ** (-0.5), types.SimpleNamespace(**dict(zip(names, refs))))

    results = pl.pallas_call(
        body,
        out_shape=[jax.ShapeDtypeStruct(shape, kind) for shape, kind, _ in outputs.values()],
        in_specs=[spec for _, spec in inputs.values()],
        out_specs=[spec for _, _, spec in outputs.values()],
        scratch_shapes=list(scratch.values()),
        compiler_params=pltpu.CompilerParams(
            collective_id=0, has_side_effects=True, vmem_limit_bytes=VMEM_BYTES
        ),
    )(*(item for item, _ in inputs.values()))
    got = types.SimpleNamespace(**dict(zip(outputs, results)))

    def by_columns(item, groups):
        item = item.reshape(8, 32, groups, -1).astype(f32)
        return jnp.transpose(item, (1, 2, 0, 3)).reshape(32, -1)

    small = got.o_small
    return (
        got.o_lo,
        got.o_ig,
        small[4],
        small[5],
        by_columns(got.o_gq, 3),
        small[8],
        small[9],
        got.o_go,
        small[0],
        small[1],
        small[2],
        by_columns(got.o_gu, 4),
        got.o_bu[0],
        got.o_gd.astype(f32),
        small[3],
    )


def solution(mesh):
    placed = (
        P("fsdp", "ctx", None),
        P("fsdp", None),
        P("fsdp"),
        P("fsdp"),
        P("fsdp", None),
        P("fsdp"),
        P("fsdp"),
        P("fsdp", None),
        P("fsdp"),
        P("fsdp"),
        P("fsdp"),
        P("fsdp", None),
        P("fsdp"),
        P("fsdp", None),
        P("fsdp"),
        P("fsdp", "ctx", None),
    )
    by_heads = mesh.shape["ctx"] == HEADS and mesh.shape["fsdp"] == 4
    return jax.shard_map(
        per_device_tp if by_heads else per_device_ctx,
        mesh=mesh,
        in_specs=placed,
        out_specs=(
            P("fsdp", "ctx", None),
            P("fsdp", "ctx", None),
            P(("ctx", "fsdp")),
            P(("ctx", "fsdp")),
            P(("ctx", "fsdp"), None),
            P(("ctx", "fsdp")),
            P(("ctx", "fsdp")),
            P(("ctx", "fsdp"), None),
            P(("ctx", "fsdp")),
            P(("ctx", "fsdp")),
            P(("ctx", "fsdp")),
            P(("ctx", "fsdp"), None),
            P(("ctx", "fsdp")),
            P(("ctx", "fsdp"), None),
            P(("ctx", "fsdp")),
        ),
        check_vma=False,
    )
```

```python
import math
import types

import jax
import jax.numpy as jnp
from jax import lax
from jax.experimental import pallas as pl
from jax.experimental.pallas import tpu as pltpu
from jax.sharding import PartitionSpec as P

D = 1024
HEADS = 8
HEAD_DIM = 128


EPSILON = 1e-05
NEG_LARGE = -1e30
GELU_C = math.sqrt(2.0 / math.pi)
GELU_K = 0.044715
VMEM_BYTES = 63 << 20


def gelu_tanh(values):
    inner = jnp.tanh(GELU_C * (values + GELU_K * values * values * values))
    return 0.5 * values * (1.0 + inner)


def gelu_slope(values):
    inner = jnp.tanh(GELU_C * (values + GELU_K * values * values * values))
    return 0.5 * (1.0 + inner) + 0.5 * values * (1.0 - inner * inner) * GELU_C * (
        1.0 + 3.0 * GELU_K * values * values
    )


def normalize(values, gain_vec, shift_vec):
    average = jnp.mean(values, axis=-1, keepdims=True)
    centered = values - average
    inv_dev = lax.rsqrt(jnp.mean(centered * centered, axis=-1, keepdims=True) + EPSILON)
    normed = centered * inv_dev
    return (normed * gain_vec + shift_vec, normed, inv_dev)


def normalize_back(grad, normed, inv_dev, gain_vec):
    scaled = grad * gain_vec
    return inv_dev * (
        scaled
        - jnp.mean(scaled, axis=-1, keepdims=True)
        - normed * jnp.mean(scaled * normed, axis=-1, keepdims=True)
    )


def token_positions(order_row, seq_len, half_rows):
    rows = jnp.arange(seq_len, dtype=jnp.int32)
    slots = jnp.arange(order_row.shape[0], dtype=jnp.int32)
    picked = jnp.sum(
        jnp.where((rows // half_rows)[:, None] == slots[None, :], order_row[None, :], 0), axis=1
    )
    return picked * half_rows + rows % half_rows


def block_probs(query_heads, key_heads, query_pos, key_pos, row_lse, scale):
    raw_scores = jnp.einsum(
        "qhd,khd->hqk", query_heads, key_heads, preferred_element_type=jnp.float32
    )
    allowed = (query_pos[:, None] >= key_pos[None, :])[None]
    shifted = jnp.where(allowed, raw_scores * scale - row_lse[:, :, None], NEG_LARGE)
    return jnp.where(allowed, jnp.exp(shifted), 0.0)


def score_grads(probs, grad_probs, row_delta, scale):
    return (probs * (grad_probs - row_delta[:, :, None]) * scale).astype(jnp.bfloat16)


def per_device_ctx(
    layer_in,
    block_order,
    ln1_gain,
    ln1_shift,
    w_qkv,
    b_query,
    b_value,
    w_out,
    b_out,
    ln2_gain,
    ln2_shift,
    w_up,
    b_up,
    w_down,
    b_down,
    cotangent,
):
    full = (
        lax.all_gather(ln1_gain, "fsdp", axis=0, tiled=True),
        lax.all_gather(ln1_shift, "fsdp", axis=0, tiled=True),
        lax.all_gather(w_qkv, "fsdp", axis=0, tiled=True),
        lax.all_gather(b_query, "fsdp", axis=0, tiled=True),
        lax.all_gather(b_value, "fsdp", axis=0, tiled=True),
        lax.all_gather(w_out, "fsdp", axis=0, tiled=True),
        lax.all_gather(b_out, "fsdp", axis=0, tiled=True),
        lax.all_gather(ln2_gain, "fsdp", axis=0, tiled=True),
        lax.all_gather(ln2_shift, "fsdp", axis=0, tiled=True),
        lax.all_gather(w_up, "fsdp", axis=0, tiled=True),
        lax.all_gather(b_up, "fsdp", axis=0, tiled=True),
        lax.all_gather(w_down, "fsdp", axis=0, tiled=True),
        lax.all_gather(b_down, "fsdp", axis=0, tiled=True),
    )
    qkv_full, out_full, up_full, down_full = (full[2], full[5], full[9], full[11])
    first_gain = full[0].astype(jnp.float32)
    first_shift = full[1].astype(jnp.float32)
    query_bias = full[3].astype(jnp.float32)
    value_bias = full[4].astype(jnp.float32)
    out_bias = full[6].astype(jnp.float32)
    second_gain = full[7].astype(jnp.float32)
    second_shift = full[8].astype(jnp.float32)
    up_bias = full[10].astype(jnp.float32)
    down_bias = full[12].astype(jnp.float32)
    micro = layer_in.shape[0]
    tokens = layer_in.shape[1]
    seq_len = tokens * lax.axis_size("ctx")
    half_rows = tokens // 2
    key_block = min(512, seq_len)
    blocks = seq_len // key_block
    scale = HEAD_DIM ** (-0.5)
    here = lax.axis_index("ctx")
    heads_shape = (blocks, key_block, HEADS, HEAD_DIM)
    totals = [jnp.zeros(item.shape, jnp.float32) for item in full]
    outputs_fwd = []
    outputs_grad = []
    for micro_step in range(micro):
        pos_all = token_positions(block_order[micro_step], seq_len, half_rows)
        pos_mine = lax.dynamic_slice_in_dim(pos_all, here * tokens, tokens)
        pos_blocks = pos_all.reshape(blocks, key_block)
        inputs = layer_in[micro_step].astype(jnp.float32)
        first_out, first_normed, first_inv = normalize(inputs, first_gain, first_shift)
        first_low = first_out.astype(jnp.bfloat16)
        projected = jnp.dot(first_low, qkv_full, preferred_element_type=jnp.float32)
        query_low = (projected[:, :D] + query_bias).astype(jnp.bfloat16)
        key_low = projected[:, D : 2 * D].astype(jnp.bfloat16)
        value_low = (projected[:, 2 * D :] + value_bias).astype(jnp.bfloat16)
        keys_all, values_all = (
            lax.all_gather(key_low, "ctx", axis=0, tiled=True),
            lax.all_gather(value_low, "ctx", axis=0, tiled=True),
        )
        query_heads = query_low.reshape(tokens, HEADS, HEAD_DIM)
        key_blocks = keys_all.reshape(heads_shape)
        value_blocks = values_all.reshape(heads_shape)

        def stats_step(carry, piece):
            run_max, run_sum = carry
            key_piece, key_pos = piece
            raw_scores = (
                jnp.einsum(
                    "qhd,khd->hqk", query_heads, key_piece, preferred_element_type=jnp.float32
                )
                * scale
            )
            allowed = (pos_mine[:, None] >= key_pos[None, :])[None]
            masked = jnp.where(allowed, raw_scores, NEG_LARGE)
            new_max = jnp.maximum(run_max, jnp.max(masked, axis=-1))
            weights = jnp.where(allowed, jnp.exp(masked - new_max[:, :, None]), 0.0)
            run_sum = run_sum * jnp.exp(run_max - new_max) + jnp.sum(weights, axis=-1)
            return ((new_max, run_sum), None)

        start_state = (
            jnp.full((HEADS, tokens), NEG_LARGE, jnp.float32),
            jnp.zeros((HEADS, tokens), jnp.float32),
        )
        (run_max, run_sum), unused = lax.scan(stats_step, start_state, (key_blocks, pos_blocks))
        row_lse = run_max + jnp.log(run_sum)

        def output_step(carry, piece):
            acc_low, acc_exact = carry
            key_piece, value_piece, key_pos = piece
            probs = block_probs(query_heads, key_piece, pos_mine, key_pos, row_lse, scale)
            acc_low = acc_low + jnp.einsum(
                "hqk,khd->hqd",
                probs.astype(jnp.bfloat16),
                value_piece,
                preferred_element_type=jnp.float32,
            )
            acc_exact = acc_exact + jnp.einsum(
                "hqk,khd->hqd",
                probs,
                value_piece.astype(jnp.float32),
                preferred_element_type=jnp.float32,
            )
            return ((acc_low, acc_exact), None)

        start_acc = (
            jnp.zeros((HEADS, tokens, HEAD_DIM), jnp.float32),
            jnp.zeros((HEADS, tokens, HEAD_DIM), jnp.float32),
        )
        (attn_heads, exact_heads), unused = lax.scan(
            output_step, start_acc, (key_blocks, value_blocks, pos_blocks)
        )
        attn_low = jnp.transpose(attn_heads, (1, 0, 2)).reshape(tokens, D).astype(jnp.bfloat16)
        resid = inputs + jnp.dot(attn_low, out_full, preferred_element_type=jnp.float32) + out_bias
        second_out, second_normed, second_inv = normalize(resid, second_gain, second_shift)
        second_low = second_out.astype(jnp.bfloat16)
        hidden = jnp.dot(second_low, up_full, preferred_element_type=jnp.float32) + up_bias
        active_low = gelu_tanh(hidden).astype(jnp.bfloat16)
        result = (
            resid + jnp.dot(active_low, down_full, preferred_element_type=jnp.float32) + down_bias
        )
        outputs_fwd.append(result.astype(jnp.bfloat16))
        grad_out = cotangent[micro_step]
        grad_outf = grad_out.astype(jnp.float32)
        term_down = jnp.einsum(
            "tf,td->fd", active_low, grad_out, preferred_element_type=jnp.float32
        )
        grad_active = jnp.einsum(
            "td,fd->tf", grad_out, down_full, preferred_element_type=jnp.float32
        )
        grad_hidden = (grad_active * gelu_slope(hidden)).astype(jnp.bfloat16)
        term_up = jnp.einsum(
            "td,tf->df", second_low, grad_hidden, preferred_element_type=jnp.float32
        )
        grad_second = jnp.einsum(
            "tf,df->td", grad_hidden, up_full, preferred_element_type=jnp.float32
        )
        grad_resid = grad_outf + normalize_back(grad_second, second_normed, second_inv, second_gain)
        grad_branch = grad_resid.astype(jnp.bfloat16)
        term_out = jnp.einsum(
            "td,te->de", attn_low, grad_branch, preferred_element_type=jnp.float32
        )
        grad_attn = jnp.einsum(
            "te,de->td", grad_branch, out_full, preferred_element_type=jnp.float32
        ).astype(jnp.bfloat16)
        grad_heads = grad_attn.reshape(tokens, HEADS, HEAD_DIM)
        row_delta = jnp.einsum("qhd,hqd->hq", grad_heads.astype(jnp.float32), exact_heads)

        def backward_step(grad_query, piece):
            key_piece, value_piece, key_pos = piece
            probs = block_probs(query_heads, key_piece, pos_mine, key_pos, row_lse, scale)
            grad_value = jnp.einsum(
                "hqk,qhd->khd",
                probs.astype(jnp.bfloat16),
                grad_heads,
                preferred_element_type=jnp.float32,
            )
            grad_probs = jnp.einsum(
                "qhd,khd->hqk", grad_heads, value_piece, preferred_element_type=jnp.float32
            )
            grad_scores = score_grads(probs, grad_probs, row_delta, scale)
            grad_query = grad_query + jnp.einsum(
                "hqk,khd->qhd", grad_scores, key_piece, preferred_element_type=jnp.float32
            )
            grad_key = jnp.einsum(
                "hqk,qhd->khd", grad_scores, query_heads, preferred_element_type=jnp.float32
            )
            rows_here = key_piece.shape[0]
            return (
                grad_query,
                jnp.concatenate(
                    [grad_key.reshape(rows_here, D), grad_value.reshape(rows_here, D)], axis=1
                ),
            )

        grad_query, key_terms = lax.scan(
            backward_step,
            jnp.zeros((tokens, HEADS, HEAD_DIM), jnp.float32),
            (key_blocks, value_blocks, pos_blocks),
        )
        key_sums = lax.psum_scatter(
            key_terms.reshape(seq_len, 2 * D), "ctx", scatter_dimension=0, tiled=True
        )
        grad_key_low = key_sums[:, :D].astype(jnp.bfloat16)
        grad_value_low = key_sums[:, D:].astype(jnp.bfloat16)
        grad_query_low = grad_query.reshape(tokens, D).astype(jnp.bfloat16)
        grad_projected = jnp.concatenate([grad_query_low, grad_key_low, grad_value_low], axis=1)
        term_qkv = jnp.einsum(
            "td,te->de", first_low, grad_projected, preferred_element_type=jnp.float32
        )
        grad_first = jnp.einsum(
            "te,de->td", grad_projected, qkv_full, preferred_element_type=jnp.float32
        )
        grad_input = grad_resid + normalize_back(grad_first, first_normed, first_inv, first_gain)
        outputs_grad.append(grad_input.astype(jnp.bfloat16))
        terms = (
            jnp.sum(grad_first * first_normed, axis=0),
            jnp.sum(grad_first, axis=0),
            term_qkv,
            jnp.sum(grad_query_low.astype(jnp.float32), axis=0),
            jnp.sum(grad_value_low.astype(jnp.float32), axis=0),
            term_out,
            jnp.sum(grad_branch.astype(jnp.float32), axis=0),
            jnp.sum(grad_second * second_normed, axis=0),
            jnp.sum(grad_second, axis=0),
            term_up,
            jnp.sum(grad_hidden.astype(jnp.float32), axis=0),
            term_down,
            jnp.sum(grad_outf, axis=0),
        )
        totals = [older + newer for older, newer in zip(totals, terms)]
    summed = (
        lax.psum_scatter(totals[0], ("ctx", "fsdp"), scatter_dimension=0, tiled=True),
        lax.psum_scatter(totals[1], ("ctx", "fsdp"), scatter_dimension=0, tiled=True),
        lax.psum_scatter(totals[2], ("ctx", "fsdp"), scatter_dimension=0, tiled=True),
        lax.psum_scatter(totals[3], ("ctx", "fsdp"), scatter_dimension=0, tiled=True),
        lax.psum_scatter(totals[4], ("ctx", "fsdp"), scatter_dimension=0, tiled=True),
        lax.psum_scatter(totals[5], ("ctx", "fsdp"), scatter_dimension=0, tiled=True),
        lax.psum_scatter(totals[6], ("ctx", "fsdp"), scatter_dimension=0, tiled=True),
        lax.psum_scatter(totals[7], ("ctx", "fsdp"), scatter_dimension=0, tiled=True),
        lax.psum_scatter(totals[8], ("ctx", "fsdp"), scatter_dimension=0, tiled=True),
        lax.psum_scatter(totals[9], ("ctx", "fsdp"), scatter_dimension=0, tiled=True),
        lax.psum_scatter(totals[10], ("ctx", "fsdp"), scatter_dimension=0, tiled=True),
        lax.psum_scatter(totals[11], ("ctx", "fsdp"), scatter_dimension=0, tiled=True),
        lax.psum_scatter(totals[12], ("ctx", "fsdp"), scatter_dimension=0, tiled=True),
    )
    return (
        jnp.stack(outputs_fwd),
        jnp.stack(outputs_grad),
        summed[0],
        summed[1],
        summed[2],
        summed[3],
        summed[4],
        summed[5],
        summed[6],
        summed[7],
        summed[8],
        summed[9],
        summed[10],
        summed[11],
        summed[12],
    )


LOG2E = 1.4426950408889634


def dot_as(left, right, left_dim, right_dim):
    return lax.dot_general(
        left, right, (((left_dim,), (right_dim,)), ((), ())), preferred_element_type=jnp.float32
    )


def dot_nn(left, right):
    return dot_as(left, right, 1, 0)


def dot_nt(left, right):
    return dot_as(left, right, 1, 1)


def dot_tn(left, right):
    return dot_as(left, right, 0, 0)


class Ring:
    def __init__(self):
        self.col = lax.axis_index("ctx")
        self.layer = lax.axis_index("fsdp")
        col = self.col
        self.sib = col + 1 - 2 * (col % 2)
        self.xnb = col + 2 - 4 * ((col // 2) % 2)
        self.ynb = col + 4 - 8 * (col // 4)
        self.diag = self.xnb + self.ynb - col
        self.xsib = self.xnb + self.sib - col
        self.ysib = self.ynb + self.sib - col
        self.dsib = self.diag + self.sib - col

    def flat(self, col):
        return (col, self.layer)

    def up(self, hop):
        return (self.layer + hop) % 4


class Wire:
    def __init__(self):
        self.all = []

    def send(self, src, dst, send_sem, recv_sem, where):
        copy = Sent(src, dst, send_sem, recv_sem, where)
        copy.start()
        self.all.append(copy)
        return copy

    def drain(self):
        for copy in self.all:
            copy.wait_send()


class Sent:
    def __init__(self, src, dst, send_sem, recv_sem, where):
        self.copy = pltpu.make_async_remote_copy(
            src_ref=src,
            dst_ref=dst,
            send_sem=send_sem,
            recv_sem=recv_sem,
            device_id=where,
            device_id_type=pl.DeviceIdType.MESH,
        )
        self.left = True
        self.came = False

    def start(self):
        self.copy.start()

    def copy_in(self):
        self.copy.wait_recv()

    def copy_out(self):
        self.copy.wait_send()

    def wait_recv(self):
        self.came = True
        self.copy.wait_recv()

    def wait_send(self):
        if self.left:
            self.left = False
            self.copy.wait_send()


def move(src, dst, sem):
    copy = pltpu.make_async_copy(src, dst, sem)
    copy.start()
    return copy


class Gather:
    def __init__(self, ring, wire, block, half, ssem, rsem):
        self.ring, self.wire, self.block, self.half = ring, wire, block, half
        self.ssem, self.rsem = ssem, rsem
        self.sent = []

    def go(self, ref, slot_s, slot_r, col):
        copy = self.wire.send(ref, ref, self.ssem.at[slot_s], self.rsem.at[slot_r], self.ring.flat(col))
        self.sent.append(copy)
        return copy

    def start(self):
        ring = self.ring
        own = self.block(ring.col)
        self.by_x = self.go(own, 0, 0, ring.xnb)
        self.by_y = self.go(own, 1, 1, ring.ynb)
        self.by_sib = self.go(own, 2, 2, ring.sib)

    def relay(self):
        ring = self.ring
        self.by_x.wait_recv()
        self.diag_y = self.go(self.half(ring.xnb, 0), 3, 3, ring.ynb)
        self.x_sib = self.go(self.block(ring.xnb), 4, 4, ring.sib)
        self.by_y.wait_recv()
        self.diag_x = self.go(self.half(ring.ynb, 1), 5, 5, ring.xnb)
        self.y_sib = self.go(self.block(ring.ynb), 6, 6, ring.sib)

    def relay_diag(self):
        ring = self.ring
        self.diag_y.wait_recv()
        self.diag_x.wait_recv()
        self.d_sib = self.go(self.block(ring.diag), 7, 7, ring.sib)

    def finish(self):
        self.by_sib.wait_recv()
        self.x_sib.wait_recv()
        self.y_sib.wait_recv()
        self.d_sib.wait_recv()

    def drain(self):
        for copy in self.sent:
            copy.wait_send()


class Scatter:
    def __init__(self, ring, wire, part, rows, from_sib, from_diag, from_side, ssem, rsem):
        self.ring, self.wire, self.part, self.rows = ring, wire, part, rows
        self.from_sib, self.from_diag, self.from_side = from_sib, from_diag, from_side
        self.chip = {}
        self.ssem, self.rsem = ssem, rsem
        self.sent = []

    def at(self, col, first=0, count=None):
        count = self.rows if count is None else count
        return pl.ds(pl.multiple_of(col * self.rows + first, count), count)

    def go(self, src, dst, slot, col):
        copy = self.wire.send(src, dst, self.ssem.at[slot], self.rsem.at[slot], self.ring.flat(col))
        self.sent.append(copy)
        return copy

    def start(self, slot):
        ring = self.ring
        col = (ring.sib, ring.xsib, ring.ysib, ring.dsib)[slot]
        self.chip[slot] = self.go(
            self.part.at[self.at(col)], self.from_sib.at[slot], slot, ring.sib
        )

    def add(self, col, extra, first=0, count=None):
        where = self.at(col, first, count)
        total = self.part[where].astype(jnp.float32)
        for item in extra:
            total = total + item.astype(jnp.float32)
        self.part[where] = total.astype(jnp.bfloat16)

    def middle(self):
        ring = self.ring
        half = self.rows // 2
        self.chip[3].wait_recv()
        self.add(ring.diag, [self.from_sib[3]])
        self.diag_x = self.go(
            self.part.at[self.at(ring.diag, 0, half)], self.from_diag.at[0], 4, ring.xnb
        )
        self.diag_y = self.go(
            self.part.at[self.at(ring.diag, half, half)], self.from_diag.at[1], 5, ring.ynb
        )

    def last(self):
        ring = self.ring
        half = self.rows // 2
        self.chip[1].wait_recv()
        self.chip[2].wait_recv()
        self.diag_x.wait_recv()
        self.add(ring.ynb, [self.from_sib[2, :half], self.from_diag[0]], 0, half)
        self.add(ring.ynb, [self.from_sib[2, half:]], half, half)
        self.side_y = self.go(self.part.at[self.at(ring.ynb)], self.from_side.at[1], 7, ring.ynb)
        self.diag_y.wait_recv()
        self.add(ring.xnb, [self.from_sib[1, :half]], 0, half)
        self.add(ring.xnb, [self.from_sib[1, half:], self.from_diag[1]], half, half)
        self.side_x = self.go(self.part.at[self.at(ring.xnb)], self.from_side.at[0], 6, ring.xnb)

    def finish(self):
        self.chip[0].wait_recv()
        self.side_y.wait_recv()
        self.side_x.wait_recv()
        total = self.part[self.at(self.ring.col)].astype(jnp.float32)
        total = total + self.from_sib[0].astype(jnp.float32)
        return (
            total + self.from_side[0].astype(jnp.float32) + self.from_side[1].astype(jnp.float32)
        )

    def drain(self):
        for copy in self.sent:
            copy.wait_send()


class Halve:
    def __init__(self, ring, wire, part, near, far, ssem, rsem):
        layer = ring.layer
        self.near_plane = layer + 1 - 2 * (layer % 2)
        self.far_plane = (layer + 2) % 4
        self.cross = (self.near_plane + 2) % 4
        self.ring, self.wire, self.part, self.near, self.far = ring, wire, part, near, far
        self.ssem, self.rsem = ssem, rsem

    def start(self):
        where = (self.ring.col, self.near_plane)
        self.one = self.wire.send(
            self.part(self.cross), self.near.at[0], self.ssem.at[0], self.rsem.at[0], where
        )
        self.two = self.wire.send(
            self.part(self.near_plane), self.near.at[1], self.ssem.at[1], self.rsem.at[1], where
        )

    def middle(self):
        self.one.wait_recv()
        ref = self.part(self.far_plane)
        total = ref[...].astype(jnp.float32) + self.near[0].astype(jnp.float32)
        ref[...] = total.astype(jnp.bfloat16)
        where = (self.ring.col, self.far_plane)
        self.last = self.wire.send(ref, self.far, self.ssem.at[2], self.rsem.at[2], where)

    def finish(self):
        self.two.wait_recv()
        total = self.part(self.ring.layer)[...].astype(jnp.float32)
        total = total + self.near[1].astype(jnp.float32)
        self.last.wait_recv()
        return total + self.far[...].astype(jnp.float32)


class Chain:
    def __init__(self, ring, block, ssem, rsem):
        layer, col = ring.layer, ring.col
        self.ways = []
        for way, step in ((0, 1), (1, -1)):
            inside = layer < 3 if step > 0 else layer > 0
            copies = []
            for k in range(3):
                item = block(ring.up(4 - k * step))
                copies.append(
                    Sent(item, item, ssem.at[way, k], rsem.at[way, k], (col, ring.up(4 + step)))
                )
            reach = [layer >= k if step > 0 else layer + k <= 3 for k in range(4)]
            self.ways.append((inside, reach, copies))

    def start(self):
        for inside, _, copies in self.ways:
            pl.when(inside)(copies[0].start)

    def pass_on(self, k):
        for inside, reach, copies in self.ways:

            @pl.when(reach[k])
            def _():
                copies[k - 1].copy_in()
                if k < 3:
                    pl.when(inside)(copies[k].start)

    def drain(self):
        for inside, reach, copies in self.ways:
            for k in range(3):

                @pl.when(jnp.logical_and(inside, reach[k]))
                def _():
                    copies[k].copy_out()


def row_norm(values):
    average = jnp.mean(values, axis=-1, keepdims=True)
    centered = values - average
    inv_dev = lax.rsqrt(jnp.mean(centered * centered, axis=-1, keepdims=True) + EPSILON)
    return centered * inv_dev, inv_dev


def layer_kernel(scale, refs):
    f32, bf16 = jnp.float32, jnp.bfloat16
    ring = Ring()
    wire = Wire()
    send = wire.send
    col, layer = ring.col, ring.layer
    seqs, tokens, width = refs.x.shape
    seq_len = tokens * 8
    head = HEAD_DIM
    rows_z = width // 4
    hid = refs.wu.shape[1] // 4
    step_c2 = scale * LOG2E
    R = refs
    mine = pl.ds(pl.multiple_of(col * tokens, tokens), tokens)
    head_cols = pl.multiple_of(col * head, head)

    barrier = pltpu.get_barrier_semaphore()
    me = col * 4 + layer
    for hop in range(1, 32):
        other = (me + hop) % 32
        pl.semaphore_signal(
            barrier, 1, device_id=(other // 4, other % 4), device_id_type=pl.DeviceIdType.MESH
        )
    local = R.lsem
    load_x = move(R.x, R.xb, local.at[0])
    load_ct = [move(R.cot.at[s], R.ct.at[s, mine], local.at[1 + s]) for s in range(seqs)]
    qkv_rows = pl.ds(pl.multiple_of(layer * rows_z, rows_z), rows_z)
    load_q = []
    for g in range(3):
        src = R.w_qkv.at[:, pl.ds(pl.multiple_of(g * width + col * head, head), head)]
        load_q.append(move(src, R.wq.at[qkv_rows, g * head : (g + 1) * head], local.at[3 + g]))
    small_rows = 32
    out_src = R.w_out.at[pl.ds(pl.multiple_of(col * small_rows, small_rows), small_rows)]
    load_o = move(out_src, R.wo.at[layer, col], local.at[6])
    load_u = []
    for g in range(4):
        src = R.w_up.at[:, pl.ds(pl.multiple_of(g * width + col * hid, hid), hid)]
        load_u.append(move(src, R.wu.at[qkv_rows, g * hid : (g + 1) * hid], local.at[7 + g]))
    down_src = R.w_down.at[pl.ds(pl.multiple_of(col * hid, hid), hid)]
    down_rows = pl.ds(pl.multiple_of(layer * hid, hid), hid)
    load_d = move(down_src, R.wd.at[down_rows], local.at[11])
    load_p = []
    for row, item in enumerate(R.vectors):
        load_p.append(move(item, R.pv.at[layer, row], local.at[12 + row]))
    load_b = move(R.b_up, R.pb.at[layer], local.at[11 + 9])
    for copy in load_p:
        copy.wait()
    load_b.wait()
    pl.semaphore_wait(barrier, 31)

    zs, zr = R.zs, R.zr

    def to_planes(src, dst, slot):
        return [
            send(src, dst, zs.at[slot, hop - 1], zr.at[slot, hop - 1], (col, ring.up(hop)))
            for hop in range(1, 4)
        ]

    send_par = to_planes(R.pv.at[layer], R.pv.at[layer], 0)
    send_par += to_planes(R.pb.at[layer], R.pb.at[layer], 1)

    def rows_of(ref, count):
        return lambda index: ref.at[pl.ds(pl.multiple_of(index * count, count), count)]

    chain_q, chain_u, chain_d = (
        Chain(ring, rows_of(ref, count), R.cs.at[slot], R.cr.at[slot])
        for slot, (ref, count) in enumerate(((R.wq, rows_z), (R.wu, rows_z), (R.wd, hid)))
    )
    for copy in load_q:
        copy.wait()
    chain_q.start()

    def gather_rows(ref, s, slot):

        def block(index):
            return ref.at[s, pl.ds(pl.multiple_of(index * tokens, tokens), tokens)]

        def half(index, part):
            count = tokens // 2
            first = pl.multiple_of(index * tokens + part * count, count)
            return ref.at[s, pl.ds(first, count)]

        return Gather(ring, wire, block, half, R.gs.at[slot], R.gr.at[slot])

    h1_gather = [gather_rows(R.h1, s, s) for s in range(seqs)]
    ct_gather = [gather_rows(R.ct, s, 2 + s) for s in range(seqs)]
    h2_gather = [gather_rows(R.h2, s, 4 + s) for s in range(seqs)]
    wo_gather = Gather(
        ring,
        wire,
        lambda index: R.wo.at[:, index],
        lambda index, part: R.wo.at[2 * part : 2 * part + 2, index],
        R.gs.at[6],
        R.gr.at[6],
    )

    load_x.wait()

    def params_row(row):
        pieces = []
        for plane in range(4):
            both = R.pv[plane, row].astype(f32)
            pieces += [both[0:1, :], both[1:2, :]]
        return jnp.concatenate(pieces, axis=1)

    def norm_one(s):
        return row_norm(R.xb[s].astype(f32))

    first = norm_one(0)
    for copy in send_par:
        copy.wait_recv()
    gain1, shift1 = params_row(0), params_row(1)
    R.h1[0, mine] = (first[0] * gain1 + shift1).astype(bf16)
    h1_gather[0].start()
    second = norm_one(1)
    R.h1[1, mine] = (second[0] * gain1 + shift1).astype(bf16)
    h1_gather[1].start()
    load_o.wait()
    send_o = to_planes(out_src, R.wo.at[layer, col], 4)
    for s in range(seqs):
        lane = lax.broadcasted_iota(jnp.int32, (1, seq_len), 1)
        half_rows = tokens // 2
        pos = jnp.zeros((1, seq_len), jnp.int32)
        down = lax.broadcasted_iota(jnp.int32, (half_rows, 128), 0)
        for j in range(seq_len // half_rows):
            start = R.order[s, j] * half_rows
            pos = jnp.where(lane // half_rows == j, start, pos)
            R.kpos[s, j * half_rows : (j + 1) * half_rows, :] = down + start
        R.qpos[s] = pos + lane % half_rows


    def chosen(rows):
        total = rows[0]
        for index, item in enumerate(rows[1:]):
            total = jnp.where(col == index + 1, item, total)
        return total

    def head_row(row):
        parts = [R.pv[plane, row].astype(f32) for plane in range(4)]
        return chosen([parts[j // 2][j % 2 : j % 2 + 1, :] for j in range(8)])

    bias_q, bias_v = head_row(2), head_row(3)
    pieces = []
    for plane in range(4):
        rows = R.pb[plane].astype(f32)
        pieces.append(chosen([rows[j : j + 1, :] for j in range(8)]))
    bias_u = jnp.concatenate(pieces, axis=1)
    tile = 256


    def span(chip):
        return pl.ds(pl.multiple_of(chip * tile, tile), tile)

    chips = [ring.diag // 2, ring.xnb // 2, ring.ynb // 2, col // 2]
    slots = (3, 1, 2, 0)

    def project(s):
        @pl.loop(0, 4)
        def _(t):
            r = span(t)
            both = dot_nn(R.h1[s, r, :], R.wq[...])
            R.q[s, r, :] = (both[:, :head] + bias_q).astype(bf16)
            R.k[s, r, :] = both[:, head : 2 * head].astype(bf16)
            R.v[s, r, :] = (both[:, 2 * head :] + bias_v).astype(bf16)

        R.kt[s] = R.k[s].T
        R.vt[s] = R.v[s].T

    def masked(s, r, scores, other):
        keys = jnp.concatenate([R.kpos[s]] * (tile // 128), axis=1)
        return jnp.where(R.qpos[s, :, r] >= keys, scores, other)

    def attend(s, t):
        r = span(t)
        raw = masked(s, r, dot_nt(R.k[s], R.q[s, r, :]), NEG_LARGE)
        top = jnp.max(raw, axis=0, keepdims=True)
        weights = jnp.exp2((raw - top) * step_c2)
        total = jnp.sum(weights, axis=0, keepdims=True)
        turned = dot_nn(R.vt[s], weights.astype(bf16)) * (1.0 / total)
        R.ol[s, r, :] = turned.T.astype(bf16)
        R.lse[s, :, r] = top * step_c2 + jnp.log2(total)

    others = (ring.dsib, ring.diag, ring.xsib, ring.xnb, ring.ysib, ring.ynb, ring.sib)

    def heads_to_rows(s):
        R.ob[s, :, pl.ds(head_cols, head)] = R.ol[s, mine, :]
        copies = []
        for slot, other in enumerate(others):
            src = R.ol.at[s, pl.ds(pl.multiple_of(other * tokens, tokens), tokens)]
            dst = R.ob.at[s, :, pl.ds(head_cols, head)]
            copies.append(
                send(src, dst, R.a_s.at[s, slot], R.a_r.at[s, slot], ring.flat(other))
            )
        return copies

    def rows_to_heads(s):
        R.dh[s, mine, :] = R.db[s, :, pl.ds(head_cols, head)]
        copies = []
        for slot, other in enumerate(others):
            src = R.db.at[s, :, pl.ds(pl.multiple_of(other * head, head), head)]
            dst = R.dh.at[s, mine]
            copies.append(
                send(src, dst, R.a_s.at[2 + s, slot], R.a_r.at[2 + s, slot], ring.flat(other))
            )
        return copies

    h1_gather[0].relay()
    h1_gather[1].relay()
    chain_q.pass_on(1)
    h1_gather[0].relay_diag()
    for copy in load_ct:
        copy.wait()
    ct_gather[0].start()
    chain_q.pass_on(2)
    h1_gather[1].relay_diag()
    h1_gather[0].finish()
    chain_q.pass_on(3)
    for copy in load_u + [load_d]:
        copy.wait()
    chain_u.start()
    for copy in send_o:
        copy.wait_recv()
    wo_gather.start()
    project(0)
    attend(0, 0)
    ct_gather[0].relay()
    attend(0, 1)
    chain_u.pass_on(1)
    attend(0, 2)
    wo_gather.relay()
    attend(0, 3)
    moved_o = [heads_to_rows(0)]
    h1_gather[1].finish()
    ct_gather[0].relay_diag()
    ct_gather[1].start()
    chain_d.start()
    project(1)
    wo_gather.relay_diag()
    chain_u.pass_on(2)
    attend(1, 0)
    attend(1, 1)
    wo_gather.finish()

    bias_o = params_row(4)
    gain2, shift2 = params_row(5), params_row(6)
    out_w = R.wo

    def out_project(s):
        for copy in moved_o[s]:
            copy.wait_recv()
        weight = out_w[...].reshape(width, width)
        resid = R.xb[s].astype(f32) + dot_nn(R.ob[s], weight) + bias_o
        R.r1[s] = resid
        normed, _ = row_norm(resid)
        R.h2[s, mine] = (normed * gain2 + shift2).astype(bf16)

    out_project(0)
    h2_gather[0].start()
    attend(1, 2)
    ct_gather[1].relay()
    attend(1, 3)
    moved_o.append(heads_to_rows(1))
    chain_u.pass_on(3)
    chain_d.pass_on(1)
    ct_gather[1].relay_diag()
    h2_gather[0].relay()
    out_project(1)
    h2_gather[1].start()
    h2_gather[0].relay_diag()
    chain_d.pass_on(2)
    ct_gather[0].finish()
    h2_gather[0].finish()
    chain_d.pass_on(3)

    def feed(s, chip):
        r = span(chip)
        hidden = dot_nn(R.h2[s, r, :], R.wu[...]) + bias_u
        square = hidden * hidden
        bend = jnp.tanh(hidden * (GELU_C + (GELU_C * GELU_K) * square))
        half = 0.5 * (1.0 + bend)
        active = (hidden * half).astype(bf16)
        slope = half + (0.5 * hidden) * (1.0 - bend * bend) * (
            GELU_C + (3.0 * GELU_C * GELU_K) * square
        )
        R.act[s, r, :] = active
        R.po[s, r, :] = dot_nn(active, R.wd[...]).astype(bf16)
        grad = dot_nt(R.ct[s, r, :], R.wd[...])
        grad = (grad * slope).astype(bf16)
        R.du[s, r, :] = grad
        R.pd[s, r, :] = dot_nt(grad, R.wu[...]).astype(bf16)
        up_sums.append(jnp.sum(grad.astype(f32), axis=0, keepdims=True))

    def scatter(part, s, recv, slot, rows=None):
        return Scatter(
            ring,
            wire,
            part,
            tokens,
            R.r_sib.at[recv],
            R.r_diag.at[recv],
            R.r_side.at[recv],
            R.ss.at[slot],
            R.sr.at[slot],
        )

    up_sums = []
    d2 = [scatter(R.pd.at[s], s, s, s) for s in range(2)]
    out_sc = [scatter(R.po.at[s], s, 2 + s, 2 + s) for s in range(2)]
    for t in range(4):
        feed(0, chips[t])
        d2[0].start(slots[t])
        out_sc[0].start(slots[t])
        if t == 0:
            h2_gather[1].relay()
        if t == 1:
            d2[0].middle()
        if t == 2:
            h2_gather[1].relay_diag()
    d2[0].last()
    h2_gather[1].finish()
    ct_gather[1].finish()
    for t in range(4):
        feed(1, chips[t])
        d2[1].start(slots[t])
        out_sc[1].start(slots[t])
        if t == 1:
            d2[1].middle()

    bz = R.bz
    for g in range(4):
        bz[2 + g : 3 + g, :] = sum(up_sums)[:, g * hid : (g + 1) * hid]

    down_slots, up_slots = [], []

    def grad_down():
        for j in range(2):
            cols = slice(j * 2 * hid, (j + 1) * 2 * hid)
            total = dot_tn(R.act[0, :, cols], R.ct[0])
            total = total + dot_tn(R.act[1, :, cols], R.ct[1])
            R.gd[cols, :] = total.astype(bf16)

    def grad_up():
        for j in range(2):
            cols = slice(j * 2 * hid, (j + 1) * 2 * hid)
            total = dot_tn(R.du[0, :, cols], R.h2[0])
            total = total + dot_tn(R.du[1, :, cols], R.h2[1])
            total = total.T.astype(bf16).reshape(8, 4, 32, 2 * hid)
            R.gu[:, :, :, cols] = total

    def to_planes_part(piece, dst, slot):
        return [
            send(
                piece(ring.up(hop)),
                dst.at[hop - 1],
                zs.at[slot, hop - 1],
                zr.at[slot, hop - 1],
                (col, ring.up(hop)),
            )
            for hop in range(1, 4)
        ]

    sums = {}

    def back_norm2(s):
        grad = d2[s].finish()
        normed, inv_dev = row_norm(R.r1[s])
        cot = R.ct[s, mine].astype(f32)
        scaled = grad * gain2
        resid = cot + inv_dev * (
            scaled
            - jnp.mean(scaled, axis=-1, keepdims=True)
            - normed * jnp.mean(scaled * normed, axis=-1, keepdims=True)
        )
        R.dr[s] = resid
        low = resid.astype(bf16)
        R.dz[s] = low
        lowf = low.astype(f32)
        parts = (
            jnp.sum(lowf, axis=0, keepdims=True),
            jnp.sum(grad * normed, axis=0, keepdims=True),
            jnp.sum(grad, axis=0, keepdims=True),
            jnp.sum(cot, axis=0, keepdims=True),
        )
        for row, item in enumerate(parts):
            sums[row] = sums[row] + item if row in sums else item
        R.db[s] = dot_nt(low, out_w[...].reshape(width, width)).astype(bf16)

    def attend_back(s, t):
        r = span(t)
        query, dout = R.q[s, r, :], R.dh[s, r, :]
        raw = dot_nt(R.k[s], query)
        probs = masked(s, r, jnp.exp2(raw * step_c2 - R.lse[s, :, r]), 0.0)
        grad = dot_nt(R.v[s], dout)
        part_v = dot_nn(probs.astype(bf16), dout)
        delta = jnp.sum(probs * grad, axis=0, keepdims=True)
        low = (probs * ((grad - delta) * scale)).astype(bf16)
        part_k = dot_nn(low, query)
        R.dp[s, r, :head] = dot_nn(R.kt[s], low).T.astype(bf16)
        R.dva[s] += part_v
        R.dka[s] += part_k

    def close_back(s):
        R.dp[s, :, head : 2 * head] = R.dka[s].astype(bf16)
        R.dp[s, :, 2 * head :] = R.dva[s].astype(bf16)

    def first_part(s, chip):
        r = span(chip)
        R.pd[s, r, :] = dot_nt(R.dp[s, r, :], R.wq[...]).astype(bf16)

    d2[1].last()
    back_norm2(0)
    moved_d = [rows_to_heads(0)]
    grad_down()
    z_down = Halve(ring, wire, rows_of(R.gd, hid), R.zd.at[0:2], R.zd.at[2], zs.at[10], zr.at[10])
    z_down.start()
    out_sc[0].middle()
    grad_up()
    z_up = Halve(
        ring, wire, lambda other: R.gu.at[:, other], R.zu.at[0:2], R.zu.at[2], zs.at[11], zr.at[11]
    )
    z_up.start()
    out_sc[0].last()
    back_norm2(1)
    moved_d.append(rows_to_heads(1))
    out_sc[1].middle()
    for copy in moved_d[0]:
        copy.wait_recv()
    R.dva[...] = jnp.zeros_like(R.dva)
    R.dka[...] = jnp.zeros_like(R.dka)

    @pl.loop(0, 4)
    def _(t):
        attend_back(0, t)

    close_back(0)
    d2[0].drain()
    d1 = [scatter(R.pd.at[s], s, s, 4 + s) for s in range(2)]
    for t in range(4):
        first_part(0, chips[t])
        d1[0].start(slots[t])
    z_down.middle()
    for copy in moved_d[1]:
        copy.wait_recv()
    attend_back(1, 0)
    d1[0].middle()

    @pl.loop(1, 3)
    def _(t):
        attend_back(1, t)

    d1[0].last()
    z_up.middle()
    attend_back(1, 3)
    close_back(1)
    d2[1].drain()
    for t in range(4):
        first_part(1, chips[t])
        d1[1].start(slots[t])
    for g in range(3):
        cols = slice(g * head, (g + 1) * head)
        total = dot_tn(R.dp[0, :, cols], R.h1[0]) + dot_tn(R.dp[1, :, cols], R.h1[1])
        R.gq[:, :, :, cols] = total.T.astype(bf16).reshape(8, 4, 32, head)
    z_q = Halve(
        ring, wire, lambda other: R.gq.at[:, other], R.zq.at[0:2], R.zq.at[2], zs.at[12], zr.at[12]
    )
    z_q.start()
    d1[1].middle()
    proj_sums = jnp.sum(R.dp[0].astype(f32), axis=0, keepdims=True) + jnp.sum(
        R.dp[1].astype(f32), axis=0, keepdims=True
    )
    bz[0:1, :] = proj_sums[:, :head]
    bz[1:2, :] = proj_sums[:, 2 * head :]
    bz[6:8, :] = jnp.zeros((2, head), f32)
    z_b = to_planes(bz, R.zb.at[layer], 13)
    d1[1].last()

    h2_flat = R.h2.at[0]
    for copies in (h2_gather[0], h2_gather[1]):
        copies.drain()
    h2_flat[...] = (
        dot_tn(R.ob[0], R.dz[0]) + dot_tn(R.ob[1], R.dz[1])
    ).astype(bf16)
    wo_sc = scatter(h2_flat, 0, 4, 6)
    for slot in slots:
        wo_sc.start(slot)

    out_sc[1].last()
    z_q.middle()

    owner_col, owner_layer = 2 * layer + col // 4, col % 4
    at_home = owner_col * 4 + owner_layer == me
    R.gdo[...] = z_down.finish().astype(bf16)
    wo_sc.middle()
    for copy in z_b:
        copy.wait_recv()
    bz_all = bz[...] + (R.zb[ring.up(1)] + R.zb[ring.up(2)] + R.zb[ring.up(3)])
    R.bzs[...] = bz_all
    own_up = jnp.zeros((1, head), f32)
    for k in range(4):
        own_up = jnp.where(layer == k, bz_all[2 + k : 3 + k, :], own_up)
    R.bu[...] = jnp.broadcast_to(own_up, (8, head))
    psem = R.ps

    home_copies = (
        (R.gdo, R.o_gd, psem.at[0], psem.at[2], psem.at[3]),
        (R.bu, R.o_bu, psem.at[1], psem.at[4], psem.at[5]),
    )

    @pl.when(at_home)
    def _():
        for src, dst, sem, _, _ in home_copies:
            move(src, dst, sem).wait()

    away = [
        Sent(src, dst, ssem, rsem, (owner_col, owner_layer))
        for src, dst, _, ssem, rsem in home_copies
    ]

    @pl.when(jnp.logical_not(at_home))
    def _():
        for copy in away:
            copy.start()

    R.guo[...] = z_up.finish().astype(bf16)

    def to_columns(src, dst, row):
        keep = move(src.at[col], dst.at[col], local.at[21 + row])
        copies = []
        for slot, other in enumerate(others):
            copies.append(
                send(
                    src.at[other],
                    dst.at[col],
                    R.a_s.at[4 + row, slot],
                    R.a_r.at[4 + row, slot],
                    ring.flat(other),
                )
            )
        return keep, copies

    up_keep, up_moves = to_columns(R.guo, R.o_gu, 0)
    wo_sc.last()

    bias_d = params_row(7)

    def back_norm1(s):
        grad = d1[s].finish()
        normed, inv_dev = row_norm(R.xb[s].astype(f32))
        scaled = grad * gain1
        total = R.dr[s] + inv_dev * (
            scaled
            - jnp.mean(scaled, axis=-1, keepdims=True)
            - normed * jnp.mean(scaled * normed, axis=-1, keepdims=True)
        )
        R.igs[s] = total.astype(bf16)
        for row, item in ((4, grad * normed), (5, grad)):
            item = jnp.sum(item, axis=0, keepdims=True)
            sums[row] = sums[row] + item if row in sums else item

    back_norm1(0)
    back_norm1(1)
    for row in range(6):
        R.ev[row : row + 1, :] = sums[row]
    R.ev[6:8, :] = jnp.zeros((2, width), f32)
    save_ig = move(R.igs, R.o_ig, local.at[23])
    ev_moves = []
    for hop in range(1, 8):
        other = (col + hop) % 8
        ev_moves.append(
            send(
                R.ev.at[:, pl.ds(pl.multiple_of(other * head, head), head)],
                R.evr.at[hop - 1],
                R.es.at[hop - 1],
                R.er.at[hop - 1],
                ring.flat(other),
            )
        )
    R.gqo[...] = z_q.finish().astype(bf16)
    q_keep, q_moves = to_columns(R.gqo, R.o_gq, 1)
    for copy in ev_moves:
        copy.wait_recv()
    plane = R.ev[:, pl.ds(head_cols, head)]
    for k in range(7):
        plane = plane + R.evr[k]
    R.evp[...] = plane
    z_e = to_planes(R.evp, R.evz.at[layer], 14)
    go_rows = pl.ds(pl.multiple_of(layer * 32, 32), 32)
    own = wo_sc.finish()
    R.gws[...] = own.astype(bf16)
    z_o = to_planes_part(
        lambda other: R.gws.at[pl.ds(pl.multiple_of(other * 32, 32), 32)], R.zo, 15
    )
    for s in range(2):
        R.los[s] = (R.r1[s] + out_sc[s].finish() + bias_d).astype(bf16)
    save_lo = move(R.los, R.o_lo, local.at[24])
    for copy in z_e:
        copy.wait_recv()
    total = R.evp[...] + (R.evz[ring.up(1)] + R.evz[ring.up(2)] + R.evz[ring.up(3)])
    both = jnp.concatenate([total, R.bzs[...]], axis=0)
    picked = jnp.zeros((16, 32), f32)
    for k in range(4):
        picked = jnp.where(layer == k, both[:, k * 32 : (k + 1) * 32], picked)
    R.o_small[...] = picked
    for copy in z_o:
        copy.wait_recv()
    total = R.gws[go_rows].astype(f32)
    for k in range(3):
        total = total + R.zo[k].astype(f32)
    R.o_go[...] = total

    @pl.when(jnp.logical_not(at_home))
    def _():
        for copy in away:
            copy.wait_recv()
            copy.wait_send()

    save_ig.wait()
    save_lo.wait()
    for keep, copies in ((up_keep, up_moves), (q_keep, q_moves)):
        keep.wait()
        for copy in copies:
            copy.wait_recv()
    wire.drain()
    for chain in (chain_q, chain_u, chain_d):
        chain.drain()


def closing_kernel(refs):
    R = refs
    f32 = jnp.float32
    head = HEAD_DIM
    sem = R.sem
    plan = (
        (R.gd, R.vd, R.td, R.f_gd),
        (R.gu, R.vu, R.tu, R.f_gu),
        (R.gq, R.vq, R.tq, R.f_gq),
        (R.lo, R.vl, R.vl, R.f_lo),
        (R.ig, R.vi, R.vi, R.f_ig),
        (R.go, R.vo, R.vo, R.f_go),
    )
    loads = [move(src, held, sem.at[slot]) for slot, (src, held, _, _) in enumerate(plan)]
    waits = []
    for slot, (_, held, wide, dst) in enumerate(plan):
        loads[slot].wait()
        if slot == 0:
            wide[...] = held[...].astype(f32)
        elif slot < 3:
            groups = held.shape[2] // head
            for g in range(groups):
                for c in range(8):
                    first = (g * 8 + c) * head
                    piece = held[c, :, g * head : (g + 1) * head]
                    wide[:, first : first + head] = piece.astype(f32)
        waits.append(move(wide, dst, sem.at[6 + slot]))
    for row, ref in R.rows:
        ref[...] = R.small[row]
    R.f_bu[...] = R.bu[0]
    for copy in waits:
        copy.wait()

def per_device_tp(
    layer_in,
    block_order,
    ln1_gain,
    ln1_shift,
    w_qkv,
    b_query,
    b_value,
    w_out,
    b_out,
    ln2_gain,
    ln2_shift,
    w_up,
    b_up,
    w_down,
    b_down,
    cotangent,
):
    f32, bf16, i32 = jnp.float32, jnp.bfloat16, jnp.int32
    seqs, tokens, width = layer_in.shape
    seq_len = tokens * 8
    ff = w_up.shape[1]
    hid = ff // 32
    vectors = [
        item.reshape(2, -1)
        for item in (ln1_gain, ln1_shift, b_query, b_value, b_out, ln2_gain, ln2_shift, b_down)
    ]
    anywhere = pl.BlockSpec(memory_space=pl.ANY)
    in_vmem = pl.BlockSpec(memory_space=pltpu.VMEM)
    inputs = dict(
        order=(block_order, pl.BlockSpec(memory_space=pltpu.SMEM)),
        b_up=(b_up.reshape(8, -1), anywhere),
        x=(layer_in, anywhere),
        cot=(cotangent, anywhere),
        w_qkv=(w_qkv, anywhere),
        w_out=(w_out, anywhere),
        w_up=(w_up, anywhere),
        w_down=(w_down, anywhere),
    )
    outputs = dict(
        o_lo=((seqs, tokens, width), bf16, anywhere),
        o_ig=((seqs, tokens, width), bf16, anywhere),
        o_gq=((8, 32, 3 * HEAD_DIM), bf16, anywhere),
        o_gu=((8, 32, 4 * hid), bf16, anywhere),
        o_gd=((hid, width), bf16, anywhere),
        o_go=((32, width), f32, in_vmem),
        o_small=((16, 32), f32, in_vmem),
        o_bu=((8, HEAD_DIM), f32, anywhere),
    )
    whole = (seqs, seq_len, width)
    heads = (seqs, seq_len, HEAD_DIM)
    turned = (seqs, HEAD_DIM, seq_len)
    own = (seqs, tokens, width)
    vmem, sems = pltpu.VMEM, pltpu.SemaphoreType.DMA
    scratch = dict(
        h1=vmem(whole, bf16),
        ct=vmem(whole, bf16),
        h2=vmem(whole, bf16),
        po=vmem(whole, bf16),
        pd=vmem(whole, bf16),
        wq=vmem((width, 3 * HEAD_DIM), bf16),
        wo=vmem((4, 8, 32, width), bf16),
        wu=vmem((width, 4 * hid), bf16),
        wd=vmem((4 * hid, width), bf16),
        q=vmem(heads, bf16),
        k=vmem(heads, bf16),
        v=vmem(heads, bf16),
        kt=vmem(turned, bf16),
        vt=vmem(turned, bf16),
        ol=vmem(heads, bf16),
        dh=vmem(heads, bf16),
        ob=vmem(own, bf16),
        db=vmem(own, bf16),
        xb=vmem(own, bf16),
        dz=vmem(own, bf16),
        igs=vmem(own, bf16),
        los=vmem(own, bf16),
        r1=vmem(own, f32),
        dr=vmem(own, f32),
        r_sib=vmem((5, 4, tokens, width), bf16),
        r_diag=vmem((5, 2, tokens // 2, width), bf16),
        r_side=vmem((5, 2, tokens, width), bf16),
        kpos=vmem(heads, i32),
        qpos=vmem((seqs, 1, seq_len), i32),
        lse=vmem((seqs, 1, seq_len), f32),
        act=vmem((seqs, seq_len, 4 * hid), bf16),
        du=vmem((seqs, seq_len, 4 * hid), bf16),
        dp=vmem((seqs, seq_len, 3 * HEAD_DIM), bf16),
        dka=vmem(heads, f32),
        dva=vmem(heads, f32),
        gd=vmem((4 * hid, width), bf16),
        gu=vmem((8, 4, 32, 4 * hid), bf16),
        gq=vmem((8, 4, 32, 3 * HEAD_DIM), bf16),
        gws=vmem((tokens, width), bf16),
        gdo=vmem((hid, width), bf16),
        guo=vmem((8, 32, 4 * hid), bf16),
        gqo=vmem((8, 32, 3 * HEAD_DIM), bf16),
        zd=vmem((3, hid, width), bf16),
        zu=vmem((3, 8, 32, 4 * hid), bf16),
        zq=vmem((3, 8, 32, 3 * HEAD_DIM), bf16),
        zo=vmem((3, 32, width), bf16),
        pv=vmem((4, 8, 2, HEAD_DIM), bf16),
        pb=vmem((4, 8, HEAD_DIM), bf16),
        bz=vmem((8, HEAD_DIM), f32),
        bzs=vmem((8, HEAD_DIM), f32),
        bu=vmem((8, HEAD_DIM), f32),
        zb=vmem((4, 8, HEAD_DIM), f32),
        ev=vmem((8, width), f32),
        evr=vmem((7, 8, HEAD_DIM), f32),
        evp=vmem((8, HEAD_DIM), f32),
        evz=vmem((4, 8, HEAD_DIM), f32),
        lsem=sems((25,)),
        zs=sems((16, 3)),
        zr=sems((16, 3)),
        cs=sems((3, 2, 3)),
        cr=sems((3, 2, 3)),
        gs=sems((7, 8)),
        gr=sems((7, 8)),
        ss=sems((7, 8)),
        sr=sems((7, 8)),
        a_s=sems((6, 7)),
        a_r=sems((6, 7)),
        es=sems((7,)),
        er=sems((7,)),
        ps=sems((6,)),
    )
    names = list(inputs) + list(outputs) + list(scratch)

    def body(*refs):
        space = types.SimpleNamespace(**dict(zip(names, refs[8:])))
        space.vectors = refs[:8]
        layer_kernel(HEAD_DIM ** (-0.5), space)

    results = pl.pallas_call(
        body,
        out_shape=[jax.ShapeDtypeStruct(shape, kind) for shape, kind, _ in outputs.values()],
        in_specs=[anywhere] * 8 + [spec for _, spec in inputs.values()],
        out_specs=[spec for _, _, spec in outputs.values()],
        scratch_shapes=list(scratch.values()),
        compiler_params=pltpu.CompilerParams(
            collective_id=0, has_side_effects=True, vmem_limit_bytes=VMEM_BYTES
        ),
    )(*vectors, *(item for item, _ in inputs.values()))
    finals = dict(
        f_lo=((seqs, tokens, width), bf16, anywhere),
        f_ig=((seqs, tokens, width), bf16, anywhere),
        f_g1=((32,), f32, in_vmem),
        f_s1=((32,), f32, in_vmem),
        f_gq=((32, 3 * width), f32, anywhere),
        f_bq=((32,), f32, in_vmem),
        f_bv=((32,), f32, in_vmem),
        f_go=((32, width), f32, anywhere),
        f_bo=((32,), f32, in_vmem),
        f_g2=((32,), f32, in_vmem),
        f_s2=((32,), f32, in_vmem),
        f_gu=((32, ff), f32, anywhere),
        f_bu=((HEAD_DIM,), f32, in_vmem),
        f_gd=((hid, width), f32, anywhere),
        f_bd=((32,), f32, in_vmem),
    )
    held = dict(
        vd=vmem((hid, width), bf16),
        vu=vmem((8, 32, 4 * hid), bf16),
        vq=vmem((8, 32, 3 * HEAD_DIM), bf16),
        td=vmem((hid, width), f32),
        tu=vmem((32, ff), f32),
        tq=vmem((32, 3 * width), f32),
        vl=vmem(own, bf16),
        vi=vmem(own, bf16),
        vo=vmem((32, width), f32),
        sem=sems((12,)),
    )
    last_names = [item[2:] for item in outputs] + list(finals) + list(held)

    def last_body(*refs):
        space = types.SimpleNamespace(**dict(zip(last_names, refs)))
        space.rows = (
            (4, space.f_g1),
            (5, space.f_s1),
            (8, space.f_bq),
            (9, space.f_bv),
            (0, space.f_bo),
            (1, space.f_g2),
            (2, space.f_s2),
            (3, space.f_bd),
        )
        closing_kernel(space)

    return tuple(
        pl.pallas_call(
            last_body,
            out_shape=[jax.ShapeDtypeStruct(shape, kind) for shape, kind, _ in finals.values()],
            in_specs=[anywhere] * 6 + [in_vmem] * 2,
            out_specs=[spec for _, _, spec in finals.values()],
            scratch_shapes=list(held.values()),
        )(*results)
    )


def solution(mesh):
    placed = (
        P("fsdp", "ctx", None),
        P("fsdp", None),
        P("fsdp"),
        P("fsdp"),
        P("fsdp", None),
        P("fsdp"),
        P("fsdp"),
        P("fsdp", None),
        P("fsdp"),
        P("fsdp"),
        P("fsdp"),
        P("fsdp", None),
        P("fsdp"),
        P("fsdp", None),
        P("fsdp"),
        P("fsdp", "ctx", None),
    )
    by_heads = mesh.shape["ctx"] == HEADS and mesh.shape["fsdp"] == 4
    return jax.shard_map(
        per_device_tp if by_heads else per_device_ctx,
        mesh=mesh,
        in_specs=placed,
        out_specs=(
            P("fsdp", "ctx", None),
            P("fsdp", "ctx", None),
            P(("ctx", "fsdp")),
            P(("ctx", "fsdp")),
            P(("ctx", "fsdp"), None),
            P(("ctx", "fsdp")),
            P(("ctx", "fsdp")),
            P(("ctx", "fsdp"), None),
            P(("ctx", "fsdp")),
            P(("ctx", "fsdp")),
            P(("ctx", "fsdp")),
            P(("ctx", "fsdp"), None),
            P(("ctx", "fsdp")),
            P(("ctx", "fsdp"), None),
            P(("ctx", "fsdp")),
        ),
        check_vma=False,
    )
```

```python
import math
import types

import jax
import jax.numpy as jnp
from jax import lax
from jax.experimental import pallas as pl
from jax.experimental.pallas import tpu as pltpu
from jax.sharding import PartitionSpec as P

D = 1024
HEADS = 8
HEAD_DIM = 128


EPSILON = 1e-05
NEG_LARGE = -1e30
GELU_C = math.sqrt(2.0 / math.pi)
GELU_K = 0.044715
VMEM_BYTES = 63 << 20


def gelu_tanh(values):
    inner = jnp.tanh(GELU_C * (values + GELU_K * values * values * values))
    return 0.5 * values * (1.0 + inner)


def gelu_slope(values):
    inner = jnp.tanh(GELU_C * (values + GELU_K * values * values * values))
    return 0.5 * (1.0 + inner) + 0.5 * values * (1.0 - inner * inner) * GELU_C * (
        1.0 + 3.0 * GELU_K * values * values
    )


def normalize(values, gain_vec, shift_vec):
    average = jnp.mean(values, axis=-1, keepdims=True)
    centered = values - average
    inv_dev = lax.rsqrt(jnp.mean(centered * centered, axis=-1, keepdims=True) + EPSILON)
    normed = centered * inv_dev
    return (normed * gain_vec + shift_vec, normed, inv_dev)


def normalize_back(grad, normed, inv_dev, gain_vec):
    scaled = grad * gain_vec
    return inv_dev * (
        scaled
        - jnp.mean(scaled, axis=-1, keepdims=True)
        - normed * jnp.mean(scaled * normed, axis=-1, keepdims=True)
    )


def token_positions(order_row, seq_len, half_rows):
    rows = jnp.arange(seq_len, dtype=jnp.int32)
    slots = jnp.arange(order_row.shape[0], dtype=jnp.int32)
    picked = jnp.sum(
        jnp.where((rows // half_rows)[:, None] == slots[None, :], order_row[None, :], 0), axis=1
    )
    return picked * half_rows + rows % half_rows


def block_probs(query_heads, key_heads, query_pos, key_pos, row_lse, scale):
    raw_scores = jnp.einsum(
        "qhd,khd->hqk", query_heads, key_heads, preferred_element_type=jnp.float32
    )
    allowed = (query_pos[:, None] >= key_pos[None, :])[None]
    shifted = jnp.where(allowed, raw_scores * scale - row_lse[:, :, None], NEG_LARGE)
    return jnp.where(allowed, jnp.exp(shifted), 0.0)


def score_grads(probs, grad_probs, row_delta, scale):
    return (probs * (grad_probs - row_delta[:, :, None]) * scale).astype(jnp.bfloat16)


def per_device_ctx(
    layer_in,
    block_order,
    ln1_gain,
    ln1_shift,
    w_qkv,
    b_query,
    b_value,
    w_out,
    b_out,
    ln2_gain,
    ln2_shift,
    w_up,
    b_up,
    w_down,
    b_down,
    cotangent,
):
    full = (
        lax.all_gather(ln1_gain, "fsdp", axis=0, tiled=True),
        lax.all_gather(ln1_shift, "fsdp", axis=0, tiled=True),
        lax.all_gather(w_qkv, "fsdp", axis=0, tiled=True),
        lax.all_gather(b_query, "fsdp", axis=0, tiled=True),
        lax.all_gather(b_value, "fsdp", axis=0, tiled=True),
        lax.all_gather(w_out, "fsdp", axis=0, tiled=True),
        lax.all_gather(b_out, "fsdp", axis=0, tiled=True),
        lax.all_gather(ln2_gain, "fsdp", axis=0, tiled=True),
        lax.all_gather(ln2_shift, "fsdp", axis=0, tiled=True),
        lax.all_gather(w_up, "fsdp", axis=0, tiled=True),
        lax.all_gather(b_up, "fsdp", axis=0, tiled=True),
        lax.all_gather(w_down, "fsdp", axis=0, tiled=True),
        lax.all_gather(b_down, "fsdp", axis=0, tiled=True),
    )
    qkv_full, out_full, up_full, down_full = (full[2], full[5], full[9], full[11])
    first_gain = full[0].astype(jnp.float32)
    first_shift = full[1].astype(jnp.float32)
    query_bias = full[3].astype(jnp.float32)
    value_bias = full[4].astype(jnp.float32)
    out_bias = full[6].astype(jnp.float32)
    second_gain = full[7].astype(jnp.float32)
    second_shift = full[8].astype(jnp.float32)
    up_bias = full[10].astype(jnp.float32)
    down_bias = full[12].astype(jnp.float32)
    micro = layer_in.shape[0]
    tokens = layer_in.shape[1]
    seq_len = tokens * lax.axis_size("ctx")
    half_rows = tokens // 2
    key_block = min(512, seq_len)
    blocks = seq_len // key_block
    scale = HEAD_DIM ** (-0.5)
    here = lax.axis_index("ctx")
    heads_shape = (blocks, key_block, HEADS, HEAD_DIM)
    totals = [jnp.zeros(item.shape, jnp.float32) for item in full]
    outputs_fwd = []
    outputs_grad = []
    for micro_step in range(micro):
        pos_all = token_positions(block_order[micro_step], seq_len, half_rows)
        pos_mine = lax.dynamic_slice_in_dim(pos_all, here * tokens, tokens)
        pos_blocks = pos_all.reshape(blocks, key_block)
        inputs = layer_in[micro_step].astype(jnp.float32)
        first_out, first_normed, first_inv = normalize(inputs, first_gain, first_shift)
        first_low = first_out.astype(jnp.bfloat16)
        projected = jnp.dot(first_low, qkv_full, preferred_element_type=jnp.float32)
        query_low = (projected[:, :D] + query_bias).astype(jnp.bfloat16)
        key_low = projected[:, D : 2 * D].astype(jnp.bfloat16)
        value_low = (projected[:, 2 * D :] + value_bias).astype(jnp.bfloat16)
        keys_all, values_all = (
            lax.all_gather(key_low, "ctx", axis=0, tiled=True),
            lax.all_gather(value_low, "ctx", axis=0, tiled=True),
        )
        query_heads = query_low.reshape(tokens, HEADS, HEAD_DIM)
        key_blocks = keys_all.reshape(heads_shape)
        value_blocks = values_all.reshape(heads_shape)

        def stats_step(carry, piece):
            run_max, run_sum = carry
            key_piece, key_pos = piece
            raw_scores = (
                jnp.einsum(
                    "qhd,khd->hqk", query_heads, key_piece, preferred_element_type=jnp.float32
                )
                * scale
            )
            allowed = (pos_mine[:, None] >= key_pos[None, :])[None]
            masked = jnp.where(allowed, raw_scores, NEG_LARGE)
            new_max = jnp.maximum(run_max, jnp.max(masked, axis=-1))
            weights = jnp.where(allowed, jnp.exp(masked - new_max[:, :, None]), 0.0)
            run_sum = run_sum * jnp.exp(run_max - new_max) + jnp.sum(weights, axis=-1)
            return ((new_max, run_sum), None)

        start_state = (
            jnp.full((HEADS, tokens), NEG_LARGE, jnp.float32),
            jnp.zeros((HEADS, tokens), jnp.float32),
        )
        (run_max, run_sum), unused = lax.scan(stats_step, start_state, (key_blocks, pos_blocks))
        row_lse = run_max + jnp.log(run_sum)

        def output_step(carry, piece):
            acc_low, acc_exact = carry
            key_piece, value_piece, key_pos = piece
            probs = block_probs(query_heads, key_piece, pos_mine, key_pos, row_lse, scale)
            acc_low = acc_low + jnp.einsum(
                "hqk,khd->hqd",
                probs.astype(jnp.bfloat16),
                value_piece,
                preferred_element_type=jnp.float32,
            )
            acc_exact = acc_exact + jnp.einsum(
                "hqk,khd->hqd",
                probs,
                value_piece.astype(jnp.float32),
                preferred_element_type=jnp.float32,
            )
            return ((acc_low, acc_exact), None)

        start_acc = (
            jnp.zeros((HEADS, tokens, HEAD_DIM), jnp.float32),
            jnp.zeros((HEADS, tokens, HEAD_DIM), jnp.float32),
        )
        (attn_heads, exact_heads), unused = lax.scan(
            output_step, start_acc, (key_blocks, value_blocks, pos_blocks)
        )
        attn_low = jnp.transpose(attn_heads, (1, 0, 2)).reshape(tokens, D).astype(jnp.bfloat16)
        resid = inputs + jnp.dot(attn_low, out_full, preferred_element_type=jnp.float32) + out_bias
        second_out, second_normed, second_inv = normalize(resid, second_gain, second_shift)
        second_low = second_out.astype(jnp.bfloat16)
        hidden = jnp.dot(second_low, up_full, preferred_element_type=jnp.float32) + up_bias
        active_low = gelu_tanh(hidden).astype(jnp.bfloat16)
        result = (
            resid + jnp.dot(active_low, down_full, preferred_element_type=jnp.float32) + down_bias
        )
        outputs_fwd.append(result.astype(jnp.bfloat16))
        grad_out = cotangent[micro_step]
        grad_outf = grad_out.astype(jnp.float32)
        term_down = jnp.einsum(
            "tf,td->fd", active_low, grad_out, preferred_element_type=jnp.float32
        )
        grad_active = jnp.einsum(
            "td,fd->tf", grad_out, down_full, preferred_element_type=jnp.float32
        )
        grad_hidden = (grad_active * gelu_slope(hidden)).astype(jnp.bfloat16)
        term_up = jnp.einsum(
            "td,tf->df", second_low, grad_hidden, preferred_element_type=jnp.float32
        )
        grad_second = jnp.einsum(
            "tf,df->td", grad_hidden, up_full, preferred_element_type=jnp.float32
        )
        grad_resid = grad_outf + normalize_back(grad_second, second_normed, second_inv, second_gain)
        grad_branch = grad_resid.astype(jnp.bfloat16)
        term_out = jnp.einsum(
            "td,te->de", attn_low, grad_branch, preferred_element_type=jnp.float32
        )
        grad_attn = jnp.einsum(
            "te,de->td", grad_branch, out_full, preferred_element_type=jnp.float32
        ).astype(jnp.bfloat16)
        grad_heads = grad_attn.reshape(tokens, HEADS, HEAD_DIM)
        row_delta = jnp.einsum("qhd,hqd->hq", grad_heads.astype(jnp.float32), exact_heads)

        def backward_step(grad_query, piece):
            key_piece, value_piece, key_pos = piece
            probs = block_probs(query_heads, key_piece, pos_mine, key_pos, row_lse, scale)
            grad_value = jnp.einsum(
                "hqk,qhd->khd",
                probs.astype(jnp.bfloat16),
                grad_heads,
                preferred_element_type=jnp.float32,
            )
            grad_probs = jnp.einsum(
                "qhd,khd->hqk", grad_heads, value_piece, preferred_element_type=jnp.float32
            )
            grad_scores = score_grads(probs, grad_probs, row_delta, scale)
            grad_query = grad_query + jnp.einsum(
                "hqk,khd->qhd", grad_scores, key_piece, preferred_element_type=jnp.float32
            )
            grad_key = jnp.einsum(
                "hqk,qhd->khd", grad_scores, query_heads, preferred_element_type=jnp.float32
            )
            rows_here = key_piece.shape[0]
            return (
                grad_query,
                jnp.concatenate(
                    [grad_key.reshape(rows_here, D), grad_value.reshape(rows_here, D)], axis=1
                ),
            )

        grad_query, key_terms = lax.scan(
            backward_step,
            jnp.zeros((tokens, HEADS, HEAD_DIM), jnp.float32),
            (key_blocks, value_blocks, pos_blocks),
        )
        key_sums = lax.psum_scatter(
            key_terms.reshape(seq_len, 2 * D), "ctx", scatter_dimension=0, tiled=True
        )
        grad_key_low = key_sums[:, :D].astype(jnp.bfloat16)
        grad_value_low = key_sums[:, D:].astype(jnp.bfloat16)
        grad_query_low = grad_query.reshape(tokens, D).astype(jnp.bfloat16)
        grad_projected = jnp.concatenate([grad_query_low, grad_key_low, grad_value_low], axis=1)
        term_qkv = jnp.einsum(
            "td,te->de", first_low, grad_projected, preferred_element_type=jnp.float32
        )
        grad_first = jnp.einsum(
            "te,de->td", grad_projected, qkv_full, preferred_element_type=jnp.float32
        )
        grad_input = grad_resid + normalize_back(grad_first, first_normed, first_inv, first_gain)
        outputs_grad.append(grad_input.astype(jnp.bfloat16))
        terms = (
            jnp.sum(grad_first * first_normed, axis=0),
            jnp.sum(grad_first, axis=0),
            term_qkv,
            jnp.sum(grad_query_low.astype(jnp.float32), axis=0),
            jnp.sum(grad_value_low.astype(jnp.float32), axis=0),
            term_out,
            jnp.sum(grad_branch.astype(jnp.float32), axis=0),
            jnp.sum(grad_second * second_normed, axis=0),
            jnp.sum(grad_second, axis=0),
            term_up,
            jnp.sum(grad_hidden.astype(jnp.float32), axis=0),
            term_down,
            jnp.sum(grad_outf, axis=0),
        )
        totals = [older + newer for older, newer in zip(totals, terms)]
    summed = (
        lax.psum_scatter(totals[0], ("ctx", "fsdp"), scatter_dimension=0, tiled=True),
        lax.psum_scatter(totals[1], ("ctx", "fsdp"), scatter_dimension=0, tiled=True),
        lax.psum_scatter(totals[2], ("ctx", "fsdp"), scatter_dimension=0, tiled=True),
        lax.psum_scatter(totals[3], ("ctx", "fsdp"), scatter_dimension=0, tiled=True),
        lax.psum_scatter(totals[4], ("ctx", "fsdp"), scatter_dimension=0, tiled=True),
        lax.psum_scatter(totals[5], ("ctx", "fsdp"), scatter_dimension=0, tiled=True),
        lax.psum_scatter(totals[6], ("ctx", "fsdp"), scatter_dimension=0, tiled=True),
        lax.psum_scatter(totals[7], ("ctx", "fsdp"), scatter_dimension=0, tiled=True),
        lax.psum_scatter(totals[8], ("ctx", "fsdp"), scatter_dimension=0, tiled=True),
        lax.psum_scatter(totals[9], ("ctx", "fsdp"), scatter_dimension=0, tiled=True),
        lax.psum_scatter(totals[10], ("ctx", "fsdp"), scatter_dimension=0, tiled=True),
        lax.psum_scatter(totals[11], ("ctx", "fsdp"), scatter_dimension=0, tiled=True),
        lax.psum_scatter(totals[12], ("ctx", "fsdp"), scatter_dimension=0, tiled=True),
    )
    return (
        jnp.stack(outputs_fwd),
        jnp.stack(outputs_grad),
        summed[0],
        summed[1],
        summed[2],
        summed[3],
        summed[4],
        summed[5],
        summed[6],
        summed[7],
        summed[8],
        summed[9],
        summed[10],
        summed[11],
        summed[12],
    )


LOG2E = 1.4426950408889634


def dot_as(left, right, left_dim, right_dim):
    return lax.dot_general(
        left, right, (((left_dim,), (right_dim,)), ((), ())), preferred_element_type=jnp.float32
    )


def dot_nn(left, right):
    return dot_as(left, right, 1, 0)


def dot_nt(left, right):
    return dot_as(left, right, 1, 1)


def dot_tn(left, right):
    return dot_as(left, right, 0, 0)


class Ring:
    def __init__(self):
        self.col = lax.axis_index("ctx")
        self.layer = lax.axis_index("fsdp")
        col = self.col
        self.sib = col + 1 - 2 * (col % 2)
        self.xnb = col + 2 - 4 * ((col // 2) % 2)
        self.ynb = col + 4 - 8 * (col // 4)
        self.diag = self.xnb + self.ynb - col
        self.xsib = self.xnb + self.sib - col
        self.ysib = self.ynb + self.sib - col
        self.dsib = self.diag + self.sib - col

    def flat(self, col):
        return (col, self.layer)

    def up(self, hop):
        return (self.layer + hop) % 4


class Wire:
    def __init__(self):
        self.all = []

    def plan(self, src, dst, send_sem, recv_sem, where):
        copy = Sent(src, dst, send_sem, recv_sem, where)
        self.all.append(copy)
        return copy

    def send(self, src, dst, send_sem, recv_sem, where):
        copy = self.plan(src, dst, send_sem, recv_sem, where)
        copy.start()
        return copy

    def drain(self):
        for copy in self.all:
            copy.wait_send()


class Sent:
    def __init__(self, src, dst, send_sem, recv_sem, where):
        self.copy = pltpu.make_async_remote_copy(
            src_ref=src,
            dst_ref=dst,
            send_sem=send_sem,
            recv_sem=recv_sem,
            device_id=where,
            device_id_type=pl.DeviceIdType.MESH,
        )
        self.left = True
        self.came = False

    def start(self):
        self.copy.start()

    def copy_in(self):
        self.copy.wait_recv()

    def copy_out(self):
        self.copy.wait_send()

    def wait_recv(self):
        self.came = True
        self.copy.wait_recv()

    def wait_send(self):
        if self.left:
            self.left = False
            self.copy.wait_send()


def move(src, dst, sem):
    copy = pltpu.make_async_copy(src, dst, sem)
    copy.start()
    return copy


class Gather:
    def __init__(self, ring, wire, block, half, ssem, rsem):
        plan = (
            (half(ring.col, 0), ring.xnb),
            (half(ring.col, 1), ring.ynb),
            (block(ring.col), ring.sib),
            (half(ring.xnb, 0), ring.ynb),
            (block(ring.xnb), ring.sib),
            (half(ring.ynb, 1), ring.xnb),
            (block(ring.ynb), ring.sib),
            (block(ring.diag), ring.sib),
            (half(ring.col, 1), ring.xnb),
            (half(ring.col, 0), ring.ynb),
        )
        self.sent = [
            wire.plan(ref, ref, ssem.at[slot], rsem.at[slot], ring.flat(col))
            for slot, (ref, col) in enumerate(plan)
        ]

    def start(self):
        for slot in (0, 1, 8, 9, 2):
            self.sent[slot].start()

    def relay(self):
        self.sent[0].wait_recv()
        self.sent[3].start()
        self.sent[1].wait_recv()
        self.sent[5].start()
        self.sent[8].wait_recv()
        self.sent[4].start()
        self.sent[9].wait_recv()
        self.sent[6].start()

    def relay_diag(self):
        self.sent[3].wait_recv()
        self.sent[5].wait_recv()
        self.sent[7].start()

    def finish(self):
        for slot in (2, 4, 6, 7):
            self.sent[slot].wait_recv()

    def drain(self):
        for copy in self.sent:
            copy.wait_send()


class Scatter:
    def __init__(self, ring, wire, part, rows, from_sib, from_diag, from_side, ssem, rsem):
        self.ring, self.part, self.rows = ring, part, rows
        self.from_sib, self.from_diag, self.from_side = from_sib, from_diag, from_side
        self.ssem, self.rsem = ssem, rsem
        self.core = ring.sib % 2
        half = rows // 2
        plan = [
            (part.at[self.at(col)], from_sib.at[slot], ring.sib)
            for slot, col in enumerate((ring.sib, ring.xsib, ring.ysib, ring.dsib))
        ]
        plan += [
            (part.at[self.at(ring.diag, 0, half)], from_diag.at[0], ring.xnb),
            (part.at[self.at(ring.diag, half, half)], from_diag.at[1], ring.ynb),
            (part.at[self.at(ring.xnb, 0, half)], from_side.at[0, 0:half], ring.xnb),
            (part.at[self.at(ring.ynb, half, half)], from_side.at[1, half:rows], ring.ynb),
            (part.at[self.at(ring.xnb, half, half)], from_side.at[0, half:rows], ring.xnb),
            (part.at[self.at(ring.ynb, 0, half)], from_side.at[1, 0:half], ring.ynb),
        ]
        self.sent = [
            wire.plan(src, dst, ssem.at[slot], rsem.at[slot], ring.flat(col))
            for slot, (src, dst, col) in enumerate(plan)
        ]

    def at(self, col, first=0, count=None):
        count = self.rows if count is None else count
        return pl.ds(pl.multiple_of(col * self.rows + first, count), count)

    def start_of(self, chip, slot):
        ring = self.ring
        col = chip * 2 + self.core
        Sent(
            self.part.at[self.at(col)],
            self.from_sib.at[slot],
            self.ssem.at[slot],
            self.rsem.at[slot],
            ring.flat(ring.sib),
        ).start()

    def start(self):
        for slot in (3, 1, 2, 0):
            self.sent[slot].start()

    def add(self, col, extra, first=0, count=None):
        where = self.at(col, first, count)
        total = self.part[where].astype(jnp.float32)
        for item in extra:
            total = total + item.astype(jnp.float32)
        self.part[where] = total.astype(jnp.bfloat16)

    def middle(self):
        self.sent[3].wait_recv()
        self.add(self.ring.diag, [self.from_sib[3]])
        self.sent[4].start()
        self.sent[5].start()

    def early(self):
        half = self.rows // 2
        self.sent[1].wait_recv()
        self.add(self.ring.xnb, [self.from_sib[1, :half]], 0, half)
        self.sent[6].start()
        self.sent[2].wait_recv()
        self.add(self.ring.ynb, [self.from_sib[2, half:]], half, half)
        self.sent[7].start()

    def last(self):
        half = self.rows // 2
        self.sent[4].wait_recv()
        self.add(self.ring.ynb, [self.from_sib[2, :half], self.from_diag[0]], 0, half)
        self.sent[9].start()
        self.sent[5].wait_recv()
        self.add(self.ring.xnb, [self.from_sib[1, half:], self.from_diag[1]], half, half)
        self.sent[8].start()

    def finish(self):
        for slot in (0, 6, 7, 8, 9):
            self.sent[slot].wait_recv()
        total = self.part[self.at(self.ring.col)].astype(jnp.float32)
        total = total + self.from_sib[0].astype(jnp.float32)
        return (
            total + self.from_side[0].astype(jnp.float32) + self.from_side[1].astype(jnp.float32)
        )

    def drain(self):
        for copy in self.sent:
            copy.wait_send()


class Halve:
    def __init__(self, ring, wire, part, near, far, ssem, rsem):
        layer = ring.layer
        self.near_plane = layer + 1 - 2 * (layer % 2)
        self.far_plane = (layer + 2) % 4
        cross = (self.near_plane + 2) % 4
        self.ring, self.part, self.near, self.far = ring, part, near, far
        plan = (
            (part(cross), near.at[0], self.near_plane),
            (part(self.near_plane), near.at[1], self.near_plane),
            (part(self.far_plane), far, self.far_plane),
        )
        self.one, self.two, self.last = (
            wire.plan(src, dst, ssem.at[slot], rsem.at[slot], (ring.col, plane))
            for slot, (src, dst, plane) in enumerate(plan)
        )

    def start(self):
        self.one.start()
        self.two.start()

    def middle(self):
        self.one.wait_recv()
        ref = self.part(self.far_plane)
        total = ref[...].astype(jnp.float32) + self.near[0].astype(jnp.float32)
        ref[...] = total.astype(jnp.bfloat16)
        self.last.start()

    def finish(self):
        self.two.wait_recv()
        total = self.part(self.ring.layer)[...].astype(jnp.float32)
        total = total + self.near[1].astype(jnp.float32)
        self.last.wait_recv()
        return total + self.far[...].astype(jnp.float32)


class Chain:
    def __init__(self, ring, block, ssem, rsem):
        layer, col = ring.layer, ring.col
        self.ways = []
        for way, step in ((0, 1), (1, -1)):
            inside = layer < 3 if step > 0 else layer > 0
            copies = []
            for k in range(3):
                item = block(ring.up(4 - k * step))
                copies.append(
                    Sent(item, item, ssem.at[way, k], rsem.at[way, k], (col, ring.up(4 + step)))
                )
            reach = [layer >= k if step > 0 else layer + k <= 3 for k in range(4)]
            self.ways.append((inside, reach, copies))

    def start(self):
        for inside, _, copies in self.ways:
            pl.when(inside)(copies[0].start)

    def pass_on(self, k):
        for inside, reach, copies in self.ways:

            @pl.when(reach[k])
            def _():
                copies[k - 1].copy_in()
                if k < 3:
                    pl.when(inside)(copies[k].start)

    def drain(self):
        for inside, reach, copies in self.ways:
            for k in range(3):

                @pl.when(jnp.logical_and(inside, reach[k]))
                def _():
                    copies[k].copy_out()


def row_norm(values):
    average = jnp.mean(values, axis=-1, keepdims=True)
    centered = values - average
    inv_dev = lax.rsqrt(jnp.mean(centered * centered, axis=-1, keepdims=True) + EPSILON)
    return centered * inv_dev, inv_dev


def layer_kernel(scale, refs):
    f32, bf16 = jnp.float32, jnp.bfloat16
    ring = Ring()
    wire = Wire()
    send = wire.send
    col, layer = ring.col, ring.layer
    seqs, tokens, width = refs.x.shape
    seq_len = tokens * 8
    head = HEAD_DIM
    rows_z = width // 4
    hid = refs.wu.shape[1] // 4
    step_c2 = scale * LOG2E
    R = refs
    mine = pl.ds(pl.multiple_of(col * tokens, tokens), tokens)
    head_cols = pl.multiple_of(col * head, head)

    barrier = pltpu.get_barrier_semaphore()
    me = col * 4 + layer
    owner_col, owner_layer = 2 * layer + col // 4, col % 4
    at_home = owner_col * 4 + owner_layer == me
    for hop in range(1, 32):
        other = (me + hop) % 32
        pl.semaphore_signal(
            barrier, 1, device_id=(other // 4, other % 4), device_id_type=pl.DeviceIdType.MESH
        )
    local = R.lsem
    load_x = move(R.x, R.xb, local.at[0])
    load_ct = [move(R.cot.at[s], R.ct.at[s, mine], local.at[1 + s]) for s in range(seqs)]
    qkv_rows = pl.ds(pl.multiple_of(layer * rows_z, rows_z), rows_z)
    load_q = []
    for g in range(3):
        src = R.w_qkv.at[:, pl.ds(pl.multiple_of(g * width + col * head, head), head)]
        load_q.append(move(src, R.wq.at[qkv_rows, g * head : (g + 1) * head], local.at[3 + g]))
    small_rows = 32
    out_src = R.w_out.at[pl.ds(pl.multiple_of(col * small_rows, small_rows), small_rows)]
    load_o = move(out_src, R.wo.at[layer, col], local.at[6])
    load_u = []
    for g in range(4):
        src = R.w_up.at[:, pl.ds(pl.multiple_of(g * width + col * hid, hid), hid)]
        load_u.append(move(src, R.wu.at[qkv_rows, g * hid : (g + 1) * hid], local.at[7 + g]))
    down_src = R.w_down.at[pl.ds(pl.multiple_of(col * hid, hid), hid)]
    down_rows = pl.ds(pl.multiple_of(layer * hid, hid), hid)
    load_d = move(down_src, R.wd.at[down_rows], local.at[11])
    load_p = []
    for row, item in enumerate(R.vectors):
        load_p.append(move(item, R.pv.at[layer, row], local.at[12 + row]))
    load_b = move(R.b_up, R.pb.at[layer], local.at[11 + 9])
    load_x.wait()
    first, second = (row_norm(R.xb[s].astype(f32))[0] for s in range(2))
    R.r1[0] = first
    R.r1[1] = second
    for s in range(seqs):
        lane = lax.broadcasted_iota(jnp.int32, (1, seq_len), 1)
        half_rows = tokens // 2
        pos = jnp.zeros((1, seq_len), jnp.int32)
        down = lax.broadcasted_iota(jnp.int32, (half_rows, 128), 0)
        for j in range(seq_len // half_rows):
            start = R.order[s, j] * half_rows
            pos = jnp.where(lane // half_rows == j, start, pos)
            R.kpos[s, j * half_rows : (j + 1) * half_rows, :] = down + start
        R.qpos[s] = pos + lane % half_rows
    for copy in load_p:
        copy.wait()
    load_b.wait()
    pl.semaphore_wait(barrier, 31)

    zs, zr = R.zs, R.zr

    def to_planes(src, dst, slot):
        return [
            send(src, dst, zs.at[slot, hop - 1], zr.at[slot, hop - 1], (col, ring.up(hop)))
            for hop in range(1, 4)
        ]

    send_par = to_planes(R.pv.at[layer], R.pv.at[layer], 0)
    send_par += to_planes(R.pb.at[layer], R.pb.at[layer], 1)

    def rows_of(ref, count):
        return lambda index: ref.at[pl.ds(pl.multiple_of(index * count, count), count)]

    chain_q, chain_u, chain_d = (
        Chain(ring, rows_of(ref, count), R.cs.at[slot], R.cr.at[slot])
        for slot, (ref, count) in enumerate(((R.wq, rows_z), (R.wu, rows_z), (R.wd, hid)))
    )
    for copy in load_q:
        copy.wait()
    chain_q.start()

    def gather_rows(ref, s, slot):

        def block(index):
            return ref.at[s, pl.ds(pl.multiple_of(index * tokens, tokens), tokens)]

        def half(index, part):
            count = tokens // 2
            first = pl.multiple_of(index * tokens + part * count, count)
            return ref.at[s, pl.ds(first, count)]

        return Gather(ring, wire, block, half, R.gs.at[slot], R.gr.at[slot])

    h1_gather = [gather_rows(R.h1, s, s) for s in range(seqs)]
    ct_gather = [gather_rows(R.ct, s, 2 + s) for s in range(seqs)]
    h2_gather = [gather_rows(R.h2, s, 4 + s) for s in range(seqs)]
    wo_gather = Gather(
        ring,
        wire,
        lambda index: R.wo.at[:, index],
        lambda index, part: R.wo.at[2 * part : 2 * part + 2, index],
        R.gs.at[6],
        R.gr.at[6],
    )

    for copy in load_ct:
        copy.wait()
    ct_gather[0].start()


    def params_row(row):
        pieces = []
        for plane in range(4):
            both = R.pv[plane, row].astype(f32)
            pieces += [both[0:1, :], both[1:2, :]]
        return jnp.concatenate(pieces, axis=1)

    for copy in send_par:
        copy.wait_recv()
    gain1, shift1 = params_row(0), params_row(1)
    R.h1[0, mine] = (R.r1[0] * gain1 + shift1).astype(bf16)
    h1_gather[0].start()
    R.h1[1, mine] = (R.r1[1] * gain1 + shift1).astype(bf16)
    h1_gather[1].start()
    for copy in load_u:
        copy.wait()
    chain_u.start()
    load_o.wait()
    send_o = to_planes(out_src, R.wo.at[layer, col], 4)

    def chosen(rows):
        total = rows[0]
        for index, item in enumerate(rows[1:]):
            total = jnp.where(col == index + 1, item, total)
        return total

    def head_row(row):
        parts = [R.pv[plane, row].astype(f32) for plane in range(4)]
        return chosen([parts[j // 2][j % 2 : j % 2 + 1, :] for j in range(8)])

    bias_q, bias_v = head_row(2), head_row(3)
    pieces = []
    for plane in range(4):
        rows = R.pb[plane].astype(f32)
        pieces.append(chosen([rows[j : j + 1, :] for j in range(8)]))
    bias_u = jnp.concatenate(pieces, axis=1)
    tile = 256


    def span(chip):
        return pl.ds(pl.multiple_of(chip * tile, tile), tile)

    chip_x, chip_y = (col // 2) % 2, col // 4

    def order(t):
        flip_x, flip_y = 1 - t[0], 1 - t[1]
        place_x = chip_x + flip_x - 2 * chip_x * flip_x
        place_y = chip_y + flip_y - 2 * chip_y * flip_y
        return place_x + 2 * place_y, flip_x + 2 * flip_y

    def tiles(body, **between):
        @pl.loop(0, 2)
        def _(high):
            @pl.loop(0, 2)
            def _(low):
                body((high, low))
                t = 2 * high + low
                for name, action in between.items():
                    pl.when(t == int(name[1:]))(action)

    def project(s):
        @pl.loop(0, 4)
        def _(t):
            r = span(t)
            both = dot_nn(R.h1[s, r, :], R.wq[...])
            R.q[s, r, :] = (both[:, :head] + bias_q).astype(bf16)
            R.k[s, r, :] = both[:, head : 2 * head].astype(bf16)
            R.v[s, r, :] = (both[:, 2 * head :] + bias_v).astype(bf16)

        R.kt[s] = R.k[s].T
        R.vt[s] = R.v[s].T

    def masked(s, r, scores, other):
        keys = jnp.concatenate([R.kpos[s]] * (tile // 128), axis=1)
        return jnp.where(R.qpos[s, :, r] >= keys, scores, other)

    def attend(s, t):
        r = span(2 * t[0] + t[1])
        raw = masked(s, r, dot_nt(R.k[s], R.q[s, r, :]), NEG_LARGE)
        top = jnp.max(raw, axis=0, keepdims=True)
        weights = jnp.exp2((raw - top) * step_c2)
        total = jnp.sum(weights, axis=0, keepdims=True)
        turned = dot_nn(R.vt[s], weights.astype(bf16)) * (1.0 / total)
        R.ol[s, r, :] = turned.T.astype(bf16)
        R.lse[s, :, r] = top * step_c2 + jnp.log2(total)

    others = (ring.dsib, ring.diag, ring.xsib, ring.xnb, ring.ysib, ring.ynb, ring.sib)

    def heads_to_rows(s):
        R.ob[s, :, pl.ds(head_cols, head)] = R.ol[s, mine, :]
        copies = []
        for slot, other in enumerate(others):
            src = R.ol.at[s, pl.ds(pl.multiple_of(other * tokens, tokens), tokens)]
            dst = R.ob.at[s, :, pl.ds(head_cols, head)]
            copies.append(
                send(src, dst, R.a_s.at[s, slot], R.a_r.at[s, slot], ring.flat(other))
            )
        return copies

    def rows_to_heads(s):
        R.dh[s, mine, :] = R.db[s, :, pl.ds(head_cols, head)]
        copies = []
        for slot, other in enumerate(others):
            src = R.db.at[s, :, pl.ds(pl.multiple_of(other * head, head), head)]
            dst = R.dh.at[s, mine]
            copies.append(
                send(src, dst, R.a_s.at[2 + s, slot], R.a_r.at[2 + s, slot], ring.flat(other))
            )
        return copies

    bias_o = params_row(4)
    gain2, shift2 = params_row(5), params_row(6)
    out_w = R.wo

    def out_project(s):
        for copy in moved_o[s]:
            copy.wait_recv()
        weight = out_w[...].reshape(width, width)
        resid = R.xb[s].astype(f32) + dot_nn(R.ob[s], weight) + bias_o
        R.r1[s] = resid
        normed, _ = row_norm(resid)
        R.h2[s, mine] = (normed * gain2 + shift2).astype(bf16)

    def many(*actions):
        def run():
            for action in actions:
                action()

        return run

    ct_gather[0].relay()
    h1_gather[0].relay()
    chain_q.pass_on(1)
    h1_gather[1].relay()
    h1_gather[0].relay_diag()
    ct_gather[0].relay_diag()
    ct_gather[1].start()
    chain_q.pass_on(2)
    load_d.wait()
    chain_d.start()
    h1_gather[0].finish()
    chain_q.pass_on(3)
    project(0)
    chain_u.pass_on(1)
    h1_gather[1].relay_diag()
    for copy in send_o:
        copy.wait_recv()
    wo_gather.start()
    tiles(lambda t: attend(0, t), t2=wo_gather.relay)
    moved_o = [heads_to_rows(0)]
    h1_gather[1].finish()
    ct_gather[1].relay()
    project(1)
    wo_gather.relay_diag()
    chain_u.pass_on(2)

    def first_rows():
        out_project(0)
        h2_gather[0].start()

    tiles(
        lambda t: attend(1, t),
        t0=lambda: chain_d.pass_on(1),
        t1=many(wo_gather.finish, first_rows),
        t2=ct_gather[1].relay_diag,
    )
    moved_o.append(heads_to_rows(1))
    h2_gather[0].relay()
    chain_u.pass_on(3)
    out_project(1)
    h2_gather[1].start()
    chain_d.pass_on(2)
    h2_gather[0].relay_diag()
    ct_gather[0].finish()
    h2_gather[0].finish()
    chain_d.pass_on(3)

    def feed(s, t):
        chip, slot = order(t)
        r = span(chip)
        hidden = dot_nn(R.h2[s, r, :], R.wu[...]) + bias_u
        square = hidden * hidden
        bend = jnp.tanh(hidden * (GELU_C + (GELU_C * GELU_K) * square))
        half = 0.5 * (1.0 + bend)
        active = (hidden * half).astype(bf16)
        slope = half + (0.5 * hidden) * (1.0 - bend * bend) * (
            GELU_C + (3.0 * GELU_C * GELU_K) * square
        )
        R.act[s, r, :] = active
        R.po[s, r, :] = dot_nn(active, R.wd[...]).astype(bf16)
        grad = dot_nt(R.ct[s, r, :], R.wd[...])
        grad = (grad * slope).astype(bf16)
        R.du[s, r, :] = grad
        R.pd[s, r, :] = dot_nt(grad, R.wu[...]).astype(bf16)
        R.us[...] += jnp.sum(grad.astype(f32), axis=0, keepdims=True)
        d2[s].start_of(chip, slot)
        out_sc[s].start_of(chip, slot)

    def scatter(part, s, recv, slot, rows=None):
        return Scatter(
            ring,
            wire,
            part,
            tokens,
            R.r_sib.at[recv],
            R.r_diag.at[recv],
            R.r_side.at[recv],
            R.ss.at[slot],
            R.sr.at[slot],
        )

    R.us[...] = jnp.zeros_like(R.us)
    d2 = [scatter(R.pd.at[s], s, s, s) for s in range(2)]
    out_sc = [scatter(R.po.at[s], s, 2 + s, 2 + s) for s in range(2)]
    tiles(
        lambda t: feed(0, t),
        t0=h2_gather[1].relay,
        t1=d2[0].middle,
        t2=h2_gather[1].relay_diag,
        t3=d2[0].early,
    )
    d2[0].last()
    h2_gather[1].finish()
    ct_gather[1].finish()
    tiles(lambda t: feed(1, t), t1=d2[1].middle, t3=d2[1].early)

    bz = R.bz
    for g in range(4):
        bz[2 + g : 3 + g, :] = R.us[:, g * hid : (g + 1) * hid]


    def grad_down():
        for j in range(2):
            cols = slice(j * 2 * hid, (j + 1) * 2 * hid)
            total = dot_tn(R.act[0, :, cols], R.ct[0])
            total = total + dot_tn(R.act[1, :, cols], R.ct[1])
            R.gd[cols, :] = total.astype(bf16)

    def grad_up():
        for j in range(2):
            cols = slice(j * 2 * hid, (j + 1) * 2 * hid)
            total = dot_tn(R.du[0, :, cols], R.h2[0])
            total = total + dot_tn(R.du[1, :, cols], R.h2[1])
            total = total.T.astype(bf16).reshape(8, 4, 32, 2 * hid)
            R.gu[:, :, :, cols] = total

    def to_planes_part(piece, dst, slot):
        return [
            send(
                piece(ring.up(hop)),
                dst.at[hop - 1],
                zs.at[slot, hop - 1],
                zr.at[slot, hop - 1],
                (col, ring.up(hop)),
            )
            for hop in range(1, 4)
        ]

    sums = {}

    def back_norm2(s):
        grad = d2[s].finish()
        normed, inv_dev = row_norm(R.r1[s])
        cot = R.ct[s, mine].astype(f32)
        scaled = grad * gain2
        resid = cot + inv_dev * (
            scaled
            - jnp.mean(scaled, axis=-1, keepdims=True)
            - normed * jnp.mean(scaled * normed, axis=-1, keepdims=True)
        )
        R.dr[s] = resid
        low = resid.astype(bf16)
        R.dz[s] = low
        lowf = low.astype(f32)
        parts = (
            jnp.sum(lowf, axis=0, keepdims=True),
            jnp.sum(grad * normed, axis=0, keepdims=True),
            jnp.sum(grad, axis=0, keepdims=True),
            jnp.sum(cot, axis=0, keepdims=True),
        )
        for row, item in enumerate(parts):
            sums[row] = sums[row] + item if row in sums else item
        R.db[s] = dot_nt(low, out_w[...].reshape(width, width)).astype(bf16)

    def attend_back(s, t):
        r = span(2 * t[0] + t[1])
        query, dout = R.q[s, r, :], R.dh[s, r, :]
        raw = dot_nt(R.k[s], query)
        probs = masked(s, r, jnp.exp2(raw * step_c2 - R.lse[s, :, r]), 0.0)
        grad = dot_nt(R.v[s], dout)
        part_v = dot_nn(probs.astype(bf16), dout)
        delta = jnp.sum(probs * grad, axis=0, keepdims=True)
        low = (probs * ((grad - delta) * scale)).astype(bf16)
        part_k = dot_nn(low, query)
        R.dp[s, r, :head] = dot_nn(R.kt[s], low).T.astype(bf16)
        R.dva[s] += part_v
        R.dka[s] += part_k

    def close_back(s):
        R.dp[s, :, head : 2 * head] = R.dka[s].astype(bf16)
        R.dp[s, :, 2 * head :] = R.dva[s].astype(bf16)

    def first_part(s, t):
        chip, slot = order(t)
        r = span(chip)
        R.pd[s, r, :] = dot_nt(R.dp[s, r, :], R.wq[...]).astype(bf16)
        d1[s].start_of(chip, slot)

    back_norm2(0)
    moved_d = [rows_to_heads(0)]
    d2[1].last()
    grad_down()
    z_down = Halve(ring, wire, rows_of(R.gd, hid), R.zd.at[0:2], R.zd.at[2], zs.at[10], zr.at[10])
    z_down.start()
    out_sc[0].middle()
    grad_up()
    z_up = Halve(
        ring, wire, lambda other: R.gu.at[:, other], R.zu.at[0:2], R.zu.at[2], zs.at[11], zr.at[11]
    )
    z_up.start()
    back_norm2(1)
    moved_d.append(rows_to_heads(1))
    out_sc[0].early()
    out_sc[0].last()

    h2_flat = R.h2.at[0]
    for gather in h2_gather:
        gather.drain()
    h2_flat[...] = (dot_tn(R.ob[0], R.dz[0]) + dot_tn(R.ob[1], R.dz[1])).astype(bf16)
    wo_sc = scatter(h2_flat, 0, 4, 6)
    wo_sc.start()
    R.dva[...] = jnp.zeros_like(R.dva)
    R.dka[...] = jnp.zeros_like(R.dka)
    for copy in moved_d[0]:
        copy.wait_recv()
    tiles(lambda t: attend_back(0, t), t1=wo_sc.middle)
    close_back(0)
    d2[0].drain()
    d1 = [scatter(R.pd.at[s], s, s, 4 + s) for s in range(2)]
    tiles(lambda t: first_part(0, t))
    z_down.middle()
    for copy in moved_d[1]:
        copy.wait_recv()
    tiles(
        lambda t: attend_back(1, t),
        t0=many(d1[0].middle, d1[0].early, out_sc[1].middle),
        t2=many(d1[0].last, z_up.middle),
        t3=many(wo_sc.early, wo_sc.last),
    )
    close_back(1)
    d2[1].drain()
    tiles(lambda t: first_part(1, t), t2=d1[1].middle)
    proj_sums = jnp.sum(R.dp[0].astype(f32), axis=0, keepdims=True) + jnp.sum(
        R.dp[1].astype(f32), axis=0, keepdims=True
    )
    bz[0:1, :] = proj_sums[:, :head]
    bz[1:2, :] = proj_sums[:, 2 * head :]
    bz[6:8, :] = jnp.zeros((2, head), f32)
    z_b = to_planes(bz, R.zb.at[layer], 13)
    for g in range(3):
        cols = slice(g * head, (g + 1) * head)
        total = dot_tn(R.dp[0, :, cols], R.h1[0]) + dot_tn(R.dp[1, :, cols], R.h1[1])
        R.gq[:, :, :, cols] = total.T.astype(bf16).reshape(8, 4, 32, head)
    z_q = Halve(
        ring, wire, lambda other: R.gq.at[:, other], R.zq.at[0:2], R.zq.at[2], zs.at[12], zr.at[12]
    )
    z_q.start()
    d1[1].early()
    d1[1].last()
    out_sc[1].early()
    out_sc[1].last()
    R.gws[...] = wo_sc.finish().astype(bf16)
    z_o = to_planes_part(
        lambda other: R.gws.at[pl.ds(pl.multiple_of(other * 32, 32), 32)], R.zo, 15
    )

    R.gdo[...] = z_down.finish().astype(bf16)
    for copy in z_b:
        copy.wait_recv()
    bz_all = bz[...] + (R.zb[ring.up(1)] + R.zb[ring.up(2)] + R.zb[ring.up(3)])
    R.bzs[...] = bz_all
    own_up = jnp.zeros((1, head), f32)
    for k in range(4):
        own_up = jnp.where(layer == k, bz_all[2 + k : 3 + k, :], own_up)
    R.bu[...] = jnp.broadcast_to(own_up, (8, head))
    psem = R.ps
    home_copies = (
        (R.gdo, R.o_gd, psem.at[0], psem.at[2], psem.at[3]),
        (R.bu, R.o_bu, psem.at[1], psem.at[4], psem.at[5]),
    )

    @pl.when(at_home)
    def _():
        for src, dst, sem, _, _ in home_copies:
            move(src, dst, sem).wait()

    away = [
        Sent(src, dst, ssem, rsem, (owner_col, owner_layer))
        for src, dst, _, ssem, rsem in home_copies
    ]

    @pl.when(jnp.logical_not(at_home))
    def _():
        for copy in away:
            copy.start()

    def to_columns(src, dst, row):
        keep = move(src.at[col], dst.at[col], local.at[21 + row])
        copies = []
        for slot, other in enumerate(others):
            copies.append(
                send(
                    src.at[other],
                    dst.at[col],
                    R.a_s.at[4 + row, slot],
                    R.a_r.at[4 + row, slot],
                    ring.flat(other),
                )
            )
        return keep, copies

    R.guo[...] = z_up.finish().astype(bf16)
    up_keep, up_moves = to_columns(R.guo, R.o_gu, 0)

    bias_d = params_row(7)
    for s in range(2):
        R.los[s] = (R.r1[s] + out_sc[s].finish() + bias_d).astype(bf16)
    save_lo = move(R.los, R.o_lo, local.at[24])

    def back_norm1(s):
        grad = d1[s].finish()
        normed, inv_dev = row_norm(R.xb[s].astype(f32))
        scaled = grad * gain1
        total = R.dr[s] + inv_dev * (
            scaled
            - jnp.mean(scaled, axis=-1, keepdims=True)
            - normed * jnp.mean(scaled * normed, axis=-1, keepdims=True)
        )
        R.igs[s] = total.astype(bf16)
        for row, item in ((4, grad * normed), (5, grad)):
            item = jnp.sum(item, axis=0, keepdims=True)
            sums[row] = sums[row] + item if row in sums else item

    back_norm1(0)
    z_q.middle()
    back_norm1(1)
    save_ig = move(R.igs, R.o_ig, local.at[23])
    for row in range(6):
        R.ev[row : row + 1, :] = sums[row]
    R.ev[6:8, :] = jnp.zeros((2, width), f32)
    ev_moves = []
    for hop in range(1, 8):
        other = (col + hop) % 8
        ev_moves.append(
            send(
                R.ev.at[:, pl.ds(pl.multiple_of(other * head, head), head)],
                R.evr.at[hop - 1],
                R.es.at[hop - 1],
                R.er.at[hop - 1],
                ring.flat(other),
            )
        )
    R.gqo[...] = z_q.finish().astype(bf16)
    q_keep, q_moves = to_columns(R.gqo, R.o_gq, 1)
    for copy in ev_moves:
        copy.wait_recv()
    plane = R.ev[:, pl.ds(head_cols, head)]
    for k in range(7):
        plane = plane + R.evr[k]
    R.evp[...] = plane
    z_e = to_planes(R.evp, R.evz.at[layer], 14)
    for copy in z_o:
        copy.wait_recv()
    go_rows = pl.ds(pl.multiple_of(layer * 32, 32), 32)
    total = R.gws[go_rows].astype(f32)
    for k in range(3):
        total = total + R.zo[k].astype(f32)
    R.o_go[...] = total
    for copy in z_e:
        copy.wait_recv()
    total = R.evp[...] + (R.evz[ring.up(1)] + R.evz[ring.up(2)] + R.evz[ring.up(3)])
    both = jnp.concatenate([total, R.bzs[...]], axis=0)
    picked = jnp.zeros((16, 32), f32)
    for k in range(4):
        picked = jnp.where(layer == k, both[:, k * 32 : (k + 1) * 32], picked)
    R.o_small[...] = picked

    @pl.when(jnp.logical_not(at_home))
    def _():
        for copy in away:
            copy.wait_recv()
            copy.wait_send()

    save_ig.wait()
    save_lo.wait()
    for keep, copies in ((up_keep, up_moves), (q_keep, q_moves)):
        keep.wait()
        for copy in copies:
            copy.wait_recv()
    wire.drain()
    for chain in (chain_q, chain_u, chain_d):
        chain.drain()


def closing_kernel(refs):
    R = refs
    f32 = jnp.float32
    head = HEAD_DIM
    sem = R.sem
    plan = (
        (R.gd, R.vd, R.td, R.f_gd),
        (R.gu, R.vu, R.tu, R.f_gu),
        (R.gq, R.vq, R.tq, R.f_gq),
        (R.lo, R.vl, R.vl, R.f_lo),
        (R.ig, R.vi, R.vi, R.f_ig),
        (R.go, R.vo, R.vo, R.f_go),
    )
    loads = [move(src, held, sem.at[slot]) for slot, (src, held, _, _) in enumerate(plan)]
    waits = []
    for slot, (_, held, wide, dst) in enumerate(plan):
        loads[slot].wait()
        if slot == 0:
            wide[...] = held[...].astype(f32)
        elif slot < 3:
            groups = held.shape[2] // head
            for g in range(groups):
                for c in range(8):
                    first = (g * 8 + c) * head
                    piece = held[c, :, g * head : (g + 1) * head]
                    wide[:, first : first + head] = piece.astype(f32)
        waits.append(move(wide, dst, sem.at[6 + slot]))
    for row, ref in R.rows:
        ref[...] = R.small[row]
    R.f_bu[...] = R.bu[0]
    for copy in waits:
        copy.wait()

def per_device_tp(
    layer_in,
    block_order,
    ln1_gain,
    ln1_shift,
    w_qkv,
    b_query,
    b_value,
    w_out,
    b_out,
    ln2_gain,
    ln2_shift,
    w_up,
    b_up,
    w_down,
    b_down,
    cotangent,
):
    f32, bf16, i32 = jnp.float32, jnp.bfloat16, jnp.int32
    seqs, tokens, width = layer_in.shape
    seq_len = tokens * 8
    ff = w_up.shape[1]
    hid = ff // 32
    vectors = [
        item.reshape(2, -1)
        for item in (ln1_gain, ln1_shift, b_query, b_value, b_out, ln2_gain, ln2_shift, b_down)
    ]
    anywhere = pl.BlockSpec(memory_space=pl.ANY)
    in_vmem = pl.BlockSpec(memory_space=pltpu.VMEM)
    inputs = dict(
        order=(block_order, pl.BlockSpec(memory_space=pltpu.SMEM)),
        b_up=(b_up.reshape(8, -1), anywhere),
        x=(layer_in, anywhere),
        cot=(cotangent, anywhere),
        w_qkv=(w_qkv, anywhere),
        w_out=(w_out, anywhere),
        w_up=(w_up, anywhere),
        w_down=(w_down, anywhere),
    )
    outputs = dict(
        o_lo=((seqs, tokens, width), bf16, anywhere),
        o_ig=((seqs, tokens, width), bf16, anywhere),
        o_gq=((8, 32, 3 * HEAD_DIM), bf16, anywhere),
        o_gu=((8, 32, 4 * hid), bf16, anywhere),
        o_gd=((hid, width), bf16, anywhere),
        o_go=((32, width), f32, in_vmem),
        o_small=((16, 32), f32, in_vmem),
        o_bu=((8, HEAD_DIM), f32, anywhere),
    )
    whole = (seqs, seq_len, width)
    heads = (seqs, seq_len, HEAD_DIM)
    turned = (seqs, HEAD_DIM, seq_len)
    own = (seqs, tokens, width)
    vmem, sems = pltpu.VMEM, pltpu.SemaphoreType.DMA
    scratch = dict(
        h1=vmem(whole, bf16),
        ct=vmem(whole, bf16),
        h2=vmem(whole, bf16),
        po=vmem(whole, bf16),
        pd=vmem(whole, bf16),
        wq=vmem((width, 3 * HEAD_DIM), bf16),
        wo=vmem((4, 8, 32, width), bf16),
        wu=vmem((width, 4 * hid), bf16),
        wd=vmem((4 * hid, width), bf16),
        q=vmem(heads, bf16),
        k=vmem(heads, bf16),
        v=vmem(heads, bf16),
        kt=vmem(turned, bf16),
        vt=vmem(turned, bf16),
        ol=vmem(heads, bf16),
        dh=vmem(heads, bf16),
        ob=vmem(own, bf16),
        db=vmem(own, bf16),
        xb=vmem(own, bf16),
        dz=vmem(own, bf16),
        igs=vmem(own, bf16),
        los=vmem(own, bf16),
        r1=vmem(own, f32),
        dr=vmem(own, f32),
        r_sib=vmem((5, 4, tokens, width), bf16),
        r_diag=vmem((5, 2, tokens // 2, width), bf16),
        r_side=vmem((5, 2, tokens, width), bf16),
        kpos=vmem(heads, i32),
        qpos=vmem((seqs, 1, seq_len), i32),
        lse=vmem((seqs, 1, seq_len), f32),
        act=vmem((seqs, seq_len, 4 * hid), bf16),
        du=vmem((seqs, seq_len, 4 * hid), bf16),
        dp=vmem((seqs, seq_len, 3 * HEAD_DIM), bf16),
        dka=vmem(heads, f32),
        dva=vmem(heads, f32),
        gd=vmem((4 * hid, width), bf16),
        gu=vmem((8, 4, 32, 4 * hid), bf16),
        gq=vmem((8, 4, 32, 3 * HEAD_DIM), bf16),
        gws=vmem((tokens, width), bf16),
        gdo=vmem((hid, width), bf16),
        guo=vmem((8, 32, 4 * hid), bf16),
        gqo=vmem((8, 32, 3 * HEAD_DIM), bf16),
        zd=vmem((3, hid, width), bf16),
        zu=vmem((3, 8, 32, 4 * hid), bf16),
        zq=vmem((3, 8, 32, 3 * HEAD_DIM), bf16),
        zo=vmem((3, 32, width), bf16),
        pv=vmem((4, 8, 2, HEAD_DIM), bf16),
        pb=vmem((4, 8, HEAD_DIM), bf16),
        us=vmem((1, 4 * hid), f32),
        bz=vmem((8, HEAD_DIM), f32),
        bzs=vmem((8, HEAD_DIM), f32),
        bu=vmem((8, HEAD_DIM), f32),
        zb=vmem((4, 8, HEAD_DIM), f32),
        ev=vmem((8, width), f32),
        evr=vmem((7, 8, HEAD_DIM), f32),
        evp=vmem((8, HEAD_DIM), f32),
        evz=vmem((4, 8, HEAD_DIM), f32),
        lsem=sems((25,)),
        zs=sems((16, 3)),
        zr=sems((16, 3)),
        cs=sems((3, 2, 3)),
        cr=sems((3, 2, 3)),
        gs=sems((7, 10)),
        gr=sems((7, 10)),
        ss=sems((7, 10)),
        sr=sems((7, 10)),
        a_s=sems((6, 7)),
        a_r=sems((6, 7)),
        es=sems((7,)),
        er=sems((7,)),
        ps=sems((6,)),
    )
    names = list(inputs) + list(outputs) + list(scratch)

    def body(*refs):
        space = types.SimpleNamespace(**dict(zip(names, refs[8:])))
        space.vectors = refs[:8]
        layer_kernel(HEAD_DIM ** (-0.5), space)

    results = pl.pallas_call(
        body,
        out_shape=[jax.ShapeDtypeStruct(shape, kind) for shape, kind, _ in outputs.values()],
        in_specs=[anywhere] * 8 + [spec for _, spec in inputs.values()],
        out_specs=[spec for _, _, spec in outputs.values()],
        scratch_shapes=list(scratch.values()),
        compiler_params=pltpu.CompilerParams(
            collective_id=0, has_side_effects=True, vmem_limit_bytes=VMEM_BYTES
        ),
    )(*vectors, *(item for item, _ in inputs.values()))
    finals = dict(
        f_lo=((seqs, tokens, width), bf16, anywhere),
        f_ig=((seqs, tokens, width), bf16, anywhere),
        f_g1=((32,), f32, in_vmem),
        f_s1=((32,), f32, in_vmem),
        f_gq=((32, 3 * width), f32, anywhere),
        f_bq=((32,), f32, in_vmem),
        f_bv=((32,), f32, in_vmem),
        f_go=((32, width), f32, anywhere),
        f_bo=((32,), f32, in_vmem),
        f_g2=((32,), f32, in_vmem),
        f_s2=((32,), f32, in_vmem),
        f_gu=((32, ff), f32, anywhere),
        f_bu=((HEAD_DIM,), f32, in_vmem),
        f_gd=((hid, width), f32, anywhere),
        f_bd=((32,), f32, in_vmem),
    )
    held = dict(
        vd=vmem((hid, width), bf16),
        vu=vmem((8, 32, 4 * hid), bf16),
        vq=vmem((8, 32, 3 * HEAD_DIM), bf16),
        td=vmem((hid, width), f32),
        tu=vmem((32, ff), f32),
        tq=vmem((32, 3 * width), f32),
        vl=vmem(own, bf16),
        vi=vmem(own, bf16),
        vo=vmem((32, width), f32),
        sem=sems((12,)),
    )
    last_names = [item[2:] for item in outputs] + list(finals) + list(held)

    def last_body(*refs):
        space = types.SimpleNamespace(**dict(zip(last_names, refs)))
        space.rows = (
            (4, space.f_g1),
            (5, space.f_s1),
            (8, space.f_bq),
            (9, space.f_bv),
            (0, space.f_bo),
            (1, space.f_g2),
            (2, space.f_s2),
            (3, space.f_bd),
        )
        closing_kernel(space)

    return tuple(
        pl.pallas_call(
            last_body,
            out_shape=[jax.ShapeDtypeStruct(shape, kind) for shape, kind, _ in finals.values()],
            in_specs=[anywhere] * 6 + [in_vmem] * 2,
            out_specs=[spec for _, _, spec in finals.values()],
            scratch_shapes=list(held.values()),
        )(*results)
    )


def solution(mesh):
    placed = (
        P("fsdp", "ctx", None),
        P("fsdp", None),
        P("fsdp"),
        P("fsdp"),
        P("fsdp", None),
        P("fsdp"),
        P("fsdp"),
        P("fsdp", None),
        P("fsdp"),
        P("fsdp"),
        P("fsdp"),
        P("fsdp", None),
        P("fsdp"),
        P("fsdp", None),
        P("fsdp"),
        P("fsdp", "ctx", None),
    )
    by_heads = mesh.shape["ctx"] == HEADS and mesh.shape["fsdp"] == 4
    return jax.shard_map(
        per_device_tp if by_heads else per_device_ctx,
        mesh=mesh,
        in_specs=placed,
        out_specs=(
            P("fsdp", "ctx", None),
            P("fsdp", "ctx", None),
            P(("ctx", "fsdp")),
            P(("ctx", "fsdp")),
            P(("ctx", "fsdp"), None),
            P(("ctx", "fsdp")),
            P(("ctx", "fsdp")),
            P(("ctx", "fsdp"), None),
            P(("ctx", "fsdp")),
            P(("ctx", "fsdp")),
            P(("ctx", "fsdp")),
            P(("ctx", "fsdp"), None),
            P(("ctx", "fsdp")),
            P(("ctx", "fsdp"), None),
            P(("ctx", "fsdp")),
        ),
        check_vma=False,
    )
```

```python
import math
import types

import jax
import jax.numpy as jnp
from jax import lax
from jax.experimental import pallas as pl
from jax.experimental.pallas import tpu as pltpu
from jax.sharding import PartitionSpec as P

D = 1024
HEADS = 8
HEAD_DIM = 128


EPSILON = 1e-05
NEG_LARGE = -1e30
GELU_C = math.sqrt(2.0 / math.pi)
GELU_K = 0.044715
VMEM_BYTES = 63 << 20


def gelu_tanh(values):
    inner = jnp.tanh(GELU_C * (values + GELU_K * values * values * values))
    return 0.5 * values * (1.0 + inner)


def gelu_slope(values):
    inner = jnp.tanh(GELU_C * (values + GELU_K * values * values * values))
    return 0.5 * (1.0 + inner) + 0.5 * values * (1.0 - inner * inner) * GELU_C * (
        1.0 + 3.0 * GELU_K * values * values
    )


def normalize(values, gain_vec, shift_vec):
    average = jnp.mean(values, axis=-1, keepdims=True)
    centered = values - average
    inv_dev = lax.rsqrt(jnp.mean(centered * centered, axis=-1, keepdims=True) + EPSILON)
    normed = centered * inv_dev
    return (normed * gain_vec + shift_vec, normed, inv_dev)


def normalize_back(grad, normed, inv_dev, gain_vec):
    scaled = grad * gain_vec
    return inv_dev * (
        scaled
        - jnp.mean(scaled, axis=-1, keepdims=True)
        - normed * jnp.mean(scaled * normed, axis=-1, keepdims=True)
    )


def token_positions(order_row, seq_len, half_rows):
    rows = jnp.arange(seq_len, dtype=jnp.int32)
    slots = jnp.arange(order_row.shape[0], dtype=jnp.int32)
    picked = jnp.sum(
        jnp.where((rows // half_rows)[:, None] == slots[None, :], order_row[None, :], 0), axis=1
    )
    return picked * half_rows + rows % half_rows


def block_probs(query_heads, key_heads, query_pos, key_pos, row_lse, scale):
    raw_scores = jnp.einsum(
        "qhd,khd->hqk", query_heads, key_heads, preferred_element_type=jnp.float32
    )
    allowed = (query_pos[:, None] >= key_pos[None, :])[None]
    shifted = jnp.where(allowed, raw_scores * scale - row_lse[:, :, None], NEG_LARGE)
    return jnp.where(allowed, jnp.exp(shifted), 0.0)


def score_grads(probs, grad_probs, row_delta, scale):
    return (probs * (grad_probs - row_delta[:, :, None]) * scale).astype(jnp.bfloat16)


def per_device_ctx(
    layer_in,
    block_order,
    ln1_gain,
    ln1_shift,
    w_qkv,
    b_query,
    b_value,
    w_out,
    b_out,
    ln2_gain,
    ln2_shift,
    w_up,
    b_up,
    w_down,
    b_down,
    cotangent,
):
    full = (
        lax.all_gather(ln1_gain, "fsdp", axis=0, tiled=True),
        lax.all_gather(ln1_shift, "fsdp", axis=0, tiled=True),
        lax.all_gather(w_qkv, "fsdp", axis=0, tiled=True),
        lax.all_gather(b_query, "fsdp", axis=0, tiled=True),
        lax.all_gather(b_value, "fsdp", axis=0, tiled=True),
        lax.all_gather(w_out, "fsdp", axis=0, tiled=True),
        lax.all_gather(b_out, "fsdp", axis=0, tiled=True),
        lax.all_gather(ln2_gain, "fsdp", axis=0, tiled=True),
        lax.all_gather(ln2_shift, "fsdp", axis=0, tiled=True),
        lax.all_gather(w_up, "fsdp", axis=0, tiled=True),
        lax.all_gather(b_up, "fsdp", axis=0, tiled=True),
        lax.all_gather(w_down, "fsdp", axis=0, tiled=True),
        lax.all_gather(b_down, "fsdp", axis=0, tiled=True),
    )
    qkv_full, out_full, up_full, down_full = (full[2], full[5], full[9], full[11])
    first_gain = full[0].astype(jnp.float32)
    first_shift = full[1].astype(jnp.float32)
    query_bias = full[3].astype(jnp.float32)
    value_bias = full[4].astype(jnp.float32)
    out_bias = full[6].astype(jnp.float32)
    second_gain = full[7].astype(jnp.float32)
    second_shift = full[8].astype(jnp.float32)
    up_bias = full[10].astype(jnp.float32)
    down_bias = full[12].astype(jnp.float32)
    micro = layer_in.shape[0]
    tokens = layer_in.shape[1]
    seq_len = tokens * lax.axis_size("ctx")
    half_rows = tokens // 2
    key_block = min(512, seq_len)
    blocks = seq_len // key_block
    scale = HEAD_DIM ** (-0.5)
    here = lax.axis_index("ctx")
    heads_shape = (blocks, key_block, HEADS, HEAD_DIM)
    totals = [jnp.zeros(item.shape, jnp.float32) for item in full]
    outputs_fwd = []
    outputs_grad = []
    for micro_step in range(micro):
        pos_all = token_positions(block_order[micro_step], seq_len, half_rows)
        pos_mine = lax.dynamic_slice_in_dim(pos_all, here * tokens, tokens)
        pos_blocks = pos_all.reshape(blocks, key_block)
        inputs = layer_in[micro_step].astype(jnp.float32)
        first_out, first_normed, first_inv = normalize(inputs, first_gain, first_shift)
        first_low = first_out.astype(jnp.bfloat16)
        projected = jnp.dot(first_low, qkv_full, preferred_element_type=jnp.float32)
        query_low = (projected[:, :D] + query_bias).astype(jnp.bfloat16)
        key_low = projected[:, D : 2 * D].astype(jnp.bfloat16)
        value_low = (projected[:, 2 * D :] + value_bias).astype(jnp.bfloat16)
        keys_all, values_all = (
            lax.all_gather(key_low, "ctx", axis=0, tiled=True),
            lax.all_gather(value_low, "ctx", axis=0, tiled=True),
        )
        query_heads = query_low.reshape(tokens, HEADS, HEAD_DIM)
        key_blocks = keys_all.reshape(heads_shape)
        value_blocks = values_all.reshape(heads_shape)

        def stats_step(carry, piece):
            run_max, run_sum = carry
            key_piece, key_pos = piece
            raw_scores = (
                jnp.einsum(
                    "qhd,khd->hqk", query_heads, key_piece, preferred_element_type=jnp.float32
                )
                * scale
            )
            allowed = (pos_mine[:, None] >= key_pos[None, :])[None]
            masked = jnp.where(allowed, raw_scores, NEG_LARGE)
            new_max = jnp.maximum(run_max, jnp.max(masked, axis=-1))
            weights = jnp.where(allowed, jnp.exp(masked - new_max[:, :, None]), 0.0)
            run_sum = run_sum * jnp.exp(run_max - new_max) + jnp.sum(weights, axis=-1)
            return ((new_max, run_sum), None)

        start_state = (
            jnp.full((HEADS, tokens), NEG_LARGE, jnp.float32),
            jnp.zeros((HEADS, tokens), jnp.float32),
        )
        (run_max, run_sum), unused = lax.scan(stats_step, start_state, (key_blocks, pos_blocks))
        row_lse = run_max + jnp.log(run_sum)

        def output_step(carry, piece):
            acc_low, acc_exact = carry
            key_piece, value_piece, key_pos = piece
            probs = block_probs(query_heads, key_piece, pos_mine, key_pos, row_lse, scale)
            acc_low = acc_low + jnp.einsum(
                "hqk,khd->hqd",
                probs.astype(jnp.bfloat16),
                value_piece,
                preferred_element_type=jnp.float32,
            )
            acc_exact = acc_exact + jnp.einsum(
                "hqk,khd->hqd",
                probs,
                value_piece.astype(jnp.float32),
                preferred_element_type=jnp.float32,
            )
            return ((acc_low, acc_exact), None)

        start_acc = (
            jnp.zeros((HEADS, tokens, HEAD_DIM), jnp.float32),
            jnp.zeros((HEADS, tokens, HEAD_DIM), jnp.float32),
        )
        (attn_heads, exact_heads), unused = lax.scan(
            output_step, start_acc, (key_blocks, value_blocks, pos_blocks)
        )
        attn_low = jnp.transpose(attn_heads, (1, 0, 2)).reshape(tokens, D).astype(jnp.bfloat16)
        resid = inputs + jnp.dot(attn_low, out_full, preferred_element_type=jnp.float32) + out_bias
        second_out, second_normed, second_inv = normalize(resid, second_gain, second_shift)
        second_low = second_out.astype(jnp.bfloat16)
        hidden = jnp.dot(second_low, up_full, preferred_element_type=jnp.float32) + up_bias
        active_low = gelu_tanh(hidden).astype(jnp.bfloat16)
        result = (
            resid + jnp.dot(active_low, down_full, preferred_element_type=jnp.float32) + down_bias
        )
        outputs_fwd.append(result.astype(jnp.bfloat16))
        grad_out = cotangent[micro_step]
        grad_outf = grad_out.astype(jnp.float32)
        term_down = jnp.einsum(
            "tf,td->fd", active_low, grad_out, preferred_element_type=jnp.float32
        )
        grad_active = jnp.einsum(
            "td,fd->tf", grad_out, down_full, preferred_element_type=jnp.float32
        )
        grad_hidden = (grad_active * gelu_slope(hidden)).astype(jnp.bfloat16)
        term_up = jnp.einsum(
            "td,tf->df", second_low, grad_hidden, preferred_element_type=jnp.float32
        )
        grad_second = jnp.einsum(
            "tf,df->td", grad_hidden, up_full, preferred_element_type=jnp.float32
        )
        grad_resid = grad_outf + normalize_back(grad_second, second_normed, second_inv, second_gain)
        grad_branch = grad_resid.astype(jnp.bfloat16)
        term_out = jnp.einsum(
            "td,te->de", attn_low, grad_branch, preferred_element_type=jnp.float32
        )
        grad_attn = jnp.einsum(
            "te,de->td", grad_branch, out_full, preferred_element_type=jnp.float32
        ).astype(jnp.bfloat16)
        grad_heads = grad_attn.reshape(tokens, HEADS, HEAD_DIM)
        row_delta = jnp.einsum("qhd,hqd->hq", grad_heads.astype(jnp.float32), exact_heads)

        def backward_step(grad_query, piece):
            key_piece, value_piece, key_pos = piece
            probs = block_probs(query_heads, key_piece, pos_mine, key_pos, row_lse, scale)
            grad_value = jnp.einsum(
                "hqk,qhd->khd",
                probs.astype(jnp.bfloat16),
                grad_heads,
                preferred_element_type=jnp.float32,
            )
            grad_probs = jnp.einsum(
                "qhd,khd->hqk", grad_heads, value_piece, preferred_element_type=jnp.float32
            )
            grad_scores = score_grads(probs, grad_probs, row_delta, scale)
            grad_query = grad_query + jnp.einsum(
                "hqk,khd->qhd", grad_scores, key_piece, preferred_element_type=jnp.float32
            )
            grad_key = jnp.einsum(
                "hqk,qhd->khd", grad_scores, query_heads, preferred_element_type=jnp.float32
            )
            rows_here = key_piece.shape[0]
            return (
                grad_query,
                jnp.concatenate(
                    [grad_key.reshape(rows_here, D), grad_value.reshape(rows_here, D)], axis=1
                ),
            )

        grad_query, key_terms = lax.scan(
            backward_step,
            jnp.zeros((tokens, HEADS, HEAD_DIM), jnp.float32),
            (key_blocks, value_blocks, pos_blocks),
        )
        key_sums = lax.psum_scatter(
            key_terms.reshape(seq_len, 2 * D), "ctx", scatter_dimension=0, tiled=True
        )
        grad_key_low = key_sums[:, :D].astype(jnp.bfloat16)
        grad_value_low = key_sums[:, D:].astype(jnp.bfloat16)
        grad_query_low = grad_query.reshape(tokens, D).astype(jnp.bfloat16)
        grad_projected = jnp.concatenate([grad_query_low, grad_key_low, grad_value_low], axis=1)
        term_qkv = jnp.einsum(
            "td,te->de", first_low, grad_projected, preferred_element_type=jnp.float32
        )
        grad_first = jnp.einsum(
            "te,de->td", grad_projected, qkv_full, preferred_element_type=jnp.float32
        )
        grad_input = grad_resid + normalize_back(grad_first, first_normed, first_inv, first_gain)
        outputs_grad.append(grad_input.astype(jnp.bfloat16))
        terms = (
            jnp.sum(grad_first * first_normed, axis=0),
            jnp.sum(grad_first, axis=0),
            term_qkv,
            jnp.sum(grad_query_low.astype(jnp.float32), axis=0),
            jnp.sum(grad_value_low.astype(jnp.float32), axis=0),
            term_out,
            jnp.sum(grad_branch.astype(jnp.float32), axis=0),
            jnp.sum(grad_second * second_normed, axis=0),
            jnp.sum(grad_second, axis=0),
            term_up,
            jnp.sum(grad_hidden.astype(jnp.float32), axis=0),
            term_down,
            jnp.sum(grad_outf, axis=0),
        )
        totals = [older + newer for older, newer in zip(totals, terms)]
    summed = (
        lax.psum_scatter(totals[0], ("ctx", "fsdp"), scatter_dimension=0, tiled=True),
        lax.psum_scatter(totals[1], ("ctx", "fsdp"), scatter_dimension=0, tiled=True),
        lax.psum_scatter(totals[2], ("ctx", "fsdp"), scatter_dimension=0, tiled=True),
        lax.psum_scatter(totals[3], ("ctx", "fsdp"), scatter_dimension=0, tiled=True),
        lax.psum_scatter(totals[4], ("ctx", "fsdp"), scatter_dimension=0, tiled=True),
        lax.psum_scatter(totals[5], ("ctx", "fsdp"), scatter_dimension=0, tiled=True),
        lax.psum_scatter(totals[6], ("ctx", "fsdp"), scatter_dimension=0, tiled=True),
        lax.psum_scatter(totals[7], ("ctx", "fsdp"), scatter_dimension=0, tiled=True),
        lax.psum_scatter(totals[8], ("ctx", "fsdp"), scatter_dimension=0, tiled=True),
        lax.psum_scatter(totals[9], ("ctx", "fsdp"), scatter_dimension=0, tiled=True),
        lax.psum_scatter(totals[10], ("ctx", "fsdp"), scatter_dimension=0, tiled=True),
        lax.psum_scatter(totals[11], ("ctx", "fsdp"), scatter_dimension=0, tiled=True),
        lax.psum_scatter(totals[12], ("ctx", "fsdp"), scatter_dimension=0, tiled=True),
    )
    return (
        jnp.stack(outputs_fwd),
        jnp.stack(outputs_grad),
        summed[0],
        summed[1],
        summed[2],
        summed[3],
        summed[4],
        summed[5],
        summed[6],
        summed[7],
        summed[8],
        summed[9],
        summed[10],
        summed[11],
        summed[12],
    )


LOG2E = 1.4426950408889634


def dot_as(left, right, left_dim, right_dim):
    return lax.dot_general(
        left, right, (((left_dim,), (right_dim,)), ((), ())), preferred_element_type=jnp.float32
    )


def dot_nn(left, right):
    return dot_as(left, right, 1, 0)


def dot_nt(left, right):
    return dot_as(left, right, 1, 1)


def dot_tn(left, right):
    return dot_as(left, right, 0, 0)


class Ring:
    def __init__(self):
        self.col = lax.axis_index("ctx")
        self.layer = lax.axis_index("fsdp")
        col = self.col
        self.sib = col + 1 - 2 * (col % 2)
        self.xnb = col + 2 - 4 * ((col // 2) % 2)
        self.ynb = col + 4 - 8 * (col // 4)
        self.diag = self.xnb + self.ynb - col
        self.xsib = self.xnb + self.sib - col
        self.ysib = self.ynb + self.sib - col
        self.dsib = self.diag + self.sib - col

    def flat(self, col):
        return (col, self.layer)

    def up(self, hop):
        return (self.layer + hop) % 4


class Wire:
    def __init__(self):
        self.all = []

    def plan(self, src, dst, send_sem, recv_sem, where):
        copy = Sent(src, dst, send_sem, recv_sem, where)
        self.all.append(copy)
        return copy

    def send(self, src, dst, send_sem, recv_sem, where):
        copy = self.plan(src, dst, send_sem, recv_sem, where)
        copy.start()
        return copy

    def drain(self):
        for copy in self.all:
            copy.wait_send()


class Sent:
    def __init__(self, src, dst, send_sem, recv_sem, where):
        self.copy = pltpu.make_async_remote_copy(
            src_ref=src,
            dst_ref=dst,
            send_sem=send_sem,
            recv_sem=recv_sem,
            device_id=where,
            device_id_type=pl.DeviceIdType.MESH,
        )
        self.left = True
        self.came = False

    def start(self):
        self.copy.start()

    def copy_in(self):
        self.copy.wait_recv()

    def copy_out(self):
        self.copy.wait_send()

    def wait_recv(self):
        self.came = True
        self.copy.wait_recv()

    def wait_send(self):
        if self.left:
            self.left = False
            self.copy.wait_send()


def move(src, dst, sem):
    copy = pltpu.make_async_copy(src, dst, sem)
    copy.start()
    return copy


class Gather:
    def __init__(self, ring, wire, block, half, ssem, rsem):
        plan = (
            (half(ring.col, 0), ring.xnb),
            (half(ring.col, 1), ring.ynb),
            (block(ring.col), ring.sib),
            (half(ring.xnb, 0), ring.ynb),
            (block(ring.xnb), ring.sib),
            (half(ring.ynb, 1), ring.xnb),
            (block(ring.ynb), ring.sib),
            (block(ring.diag), ring.sib),
            (half(ring.col, 1), ring.xnb),
            (half(ring.col, 0), ring.ynb),
        )
        self.sent = [
            wire.plan(ref, ref, ssem.at[slot], rsem.at[slot], ring.flat(col))
            for slot, (ref, col) in enumerate(plan)
        ]

    def start(self):
        for slot in (0, 1, 8, 9, 2):
            self.sent[slot].start()

    def relay(self):
        self.sent[0].wait_recv()
        self.sent[3].start()
        self.sent[1].wait_recv()
        self.sent[5].start()
        self.sent[8].wait_recv()
        self.sent[4].start()
        self.sent[9].wait_recv()
        self.sent[6].start()

    def relay_diag(self):
        self.sent[3].wait_recv()
        self.sent[5].wait_recv()
        self.sent[7].start()

    def finish(self):
        for slot in (2, 4, 6, 7):
            self.sent[slot].wait_recv()

    def drain(self):
        for copy in self.sent:
            copy.wait_send()


class Scatter:
    def __init__(self, ring, wire, part, rows, from_sib, from_diag, from_side, ssem, rsem):
        self.ring, self.part, self.rows = ring, part, rows
        self.from_sib, self.from_diag, self.from_side = from_sib, from_diag, from_side
        self.ssem, self.rsem = ssem, rsem
        self.core = ring.sib % 2
        half = rows // 2
        plan = [
            (part.at[self.at(col)], from_sib.at[slot], ring.sib)
            for slot, col in enumerate((ring.sib, ring.xsib, ring.ysib, ring.dsib))
        ]
        plan += [
            (part.at[self.at(ring.diag, 0, half)], from_diag.at[0], ring.xnb),
            (part.at[self.at(ring.diag, half, half)], from_diag.at[1], ring.ynb),
            (part.at[self.at(ring.xnb, 0, half)], from_side.at[0, 0:half], ring.xnb),
            (part.at[self.at(ring.ynb, half, half)], from_side.at[1, half:rows], ring.ynb),
            (part.at[self.at(ring.xnb, half, half)], from_side.at[0, half:rows], ring.xnb),
            (part.at[self.at(ring.ynb, 0, half)], from_side.at[1, 0:half], ring.ynb),
        ]
        self.sent = [
            wire.plan(src, dst, ssem.at[slot], rsem.at[slot], ring.flat(col))
            for slot, (src, dst, col) in enumerate(plan)
        ]

    def at(self, col, first=0, count=None):
        count = self.rows if count is None else count
        return pl.ds(pl.multiple_of(col * self.rows + first, count), count)

    def start_of(self, chip, slot):
        ring = self.ring
        col = chip * 2 + self.core
        Sent(
            self.part.at[self.at(col)],
            self.from_sib.at[slot],
            self.ssem.at[slot],
            self.rsem.at[slot],
            ring.flat(ring.sib),
        ).start()

    def start(self):
        for slot in (3, 1, 2, 0):
            self.sent[slot].start()

    def add(self, col, extra, first=0, count=None):
        where = self.at(col, first, count)
        total = self.part[where].astype(jnp.float32)
        for item in extra:
            total = total + item.astype(jnp.float32)
        self.part[where] = total.astype(jnp.bfloat16)

    def middle(self):
        self.sent[3].wait_recv()
        self.add(self.ring.diag, [self.from_sib[3]])
        self.sent[4].start()
        self.sent[5].start()

    def early(self):
        half = self.rows // 2
        self.sent[1].wait_recv()
        self.add(self.ring.xnb, [self.from_sib[1, :half]], 0, half)
        self.sent[6].start()
        self.sent[2].wait_recv()
        self.add(self.ring.ynb, [self.from_sib[2, half:]], half, half)
        self.sent[7].start()

    def last(self):
        half = self.rows // 2
        self.sent[4].wait_recv()
        self.add(self.ring.ynb, [self.from_sib[2, :half], self.from_diag[0]], 0, half)
        self.sent[9].start()
        self.sent[5].wait_recv()
        self.add(self.ring.xnb, [self.from_sib[1, half:], self.from_diag[1]], half, half)
        self.sent[8].start()

    def finish(self):
        for slot in (0, 6, 7, 8, 9):
            self.sent[slot].wait_recv()
        total = self.part[self.at(self.ring.col)].astype(jnp.float32)
        total = total + self.from_sib[0].astype(jnp.float32)
        return (
            total + self.from_side[0].astype(jnp.float32) + self.from_side[1].astype(jnp.float32)
        )

    def drain(self):
        for copy in self.sent:
            copy.wait_send()


class Halve:
    def __init__(self, ring, wire, part, near, far, ssem, rsem):
        layer = ring.layer
        self.near_plane = layer + 1 - 2 * (layer % 2)
        self.far_plane = (layer + 2) % 4
        cross = (self.near_plane + 2) % 4
        self.ring, self.part, self.near, self.far = ring, part, near, far
        plan = (
            (part(cross), near.at[0], self.near_plane),
            (part(self.near_plane), near.at[1], self.near_plane),
            (part(self.far_plane), far, self.far_plane),
        )
        self.one, self.two, self.last = (
            wire.plan(src, dst, ssem.at[slot], rsem.at[slot], (ring.col, plane))
            for slot, (src, dst, plane) in enumerate(plan)
        )

    def start(self):
        self.one.start()
        self.two.start()

    def middle(self):
        self.one.wait_recv()
        ref = self.part(self.far_plane)
        total = ref[...].astype(jnp.float32) + self.near[0].astype(jnp.float32)
        ref[...] = total.astype(jnp.bfloat16)
        self.last.start()

    def finish(self):
        self.two.wait_recv()
        total = self.part(self.ring.layer)[...].astype(jnp.float32)
        total = total + self.near[1].astype(jnp.float32)
        self.last.wait_recv()
        return total + self.far[...].astype(jnp.float32)


class Chain:
    def __init__(self, ring, block, ssem, rsem):
        layer, col = ring.layer, ring.col
        self.ways = []
        for way, step in ((0, 1), (1, -1)):
            inside = layer < 3 if step > 0 else layer > 0
            copies = []
            for k in range(3):
                item = block(ring.up(4 - k * step))
                copies.append(
                    Sent(item, item, ssem.at[way, k], rsem.at[way, k], (col, ring.up(4 + step)))
                )
            reach = [layer >= k if step > 0 else layer + k <= 3 for k in range(4)]
            self.ways.append((inside, reach, copies))

    def start(self):
        for inside, _, copies in self.ways:
            pl.when(inside)(copies[0].start)

    def pass_on(self, k):
        for inside, reach, copies in self.ways:

            @pl.when(reach[k])
            def _():
                copies[k - 1].copy_in()
                if k < 3:
                    pl.when(inside)(copies[k].start)

    def drain(self):
        for inside, reach, copies in self.ways:
            for k in range(3):

                @pl.when(jnp.logical_and(inside, reach[k]))
                def _():
                    copies[k].copy_out()


def row_norm(values):
    average = jnp.mean(values, axis=-1, keepdims=True)
    centered = values - average
    inv_dev = lax.rsqrt(jnp.mean(centered * centered, axis=-1, keepdims=True) + EPSILON)
    return centered * inv_dev, inv_dev


def layer_kernel(scale, refs):
    f32, bf16 = jnp.float32, jnp.bfloat16
    ring = Ring()
    wire = Wire()
    send = wire.send
    col, layer = ring.col, ring.layer
    seqs, tokens, width = refs.x.shape
    seq_len = tokens * 8
    head = HEAD_DIM
    rows_z = width // 4
    hid = refs.wu.shape[1] // 4
    step_c2 = scale * LOG2E
    R = refs
    mine = pl.ds(pl.multiple_of(col * tokens, tokens), tokens)
    head_cols = pl.multiple_of(col * head, head)

    barrier = pltpu.get_barrier_semaphore()
    me = col * 4 + layer
    owner_col, owner_layer = 2 * layer + col // 4, col % 4
    at_home = owner_col * 4 + owner_layer == me
    giver = (col % 2 * 4 + layer) * 4 + col // 2
    moved = ((owner_col * 4 + owner_layer - me + 32) % 32 + 31) // 32
    peers = [((col + hop) % 8, layer) for hop in range(1, 8)]
    peers += [(col, ring.up(hop)) for hop in range(1, 4)]
    for other in (owner_col * 4 + owner_layer, giver):
        other = moved * other + (1 - moved) * (31 - me)
        peers.append((other // 4, other % 4))
    for where in peers:
        pl.semaphore_signal(barrier, 1, device_id=where, device_id_type=pl.DeviceIdType.MESH)
    local = R.lsem
    load_x = move(R.x, R.xb, local.at[0])
    load_ct = [move(R.cot.at[s], R.ct.at[s, mine], local.at[1 + s]) for s in range(seqs)]
    qkv_rows = pl.ds(pl.multiple_of(layer * rows_z, rows_z), rows_z)
    load_q = []
    for g in range(3):
        src = R.w_qkv.at[:, pl.ds(pl.multiple_of(g * width + col * head, head), head)]
        load_q.append(move(src, R.wq.at[qkv_rows, g * head : (g + 1) * head], local.at[3 + g]))
    small_rows = 32
    out_src = R.w_out.at[pl.ds(pl.multiple_of(col * small_rows, small_rows), small_rows)]
    load_o = move(out_src, R.wo.at[layer, col], local.at[6])
    load_u = []
    for g in range(4):
        src = R.w_up.at[:, pl.ds(pl.multiple_of(g * width + col * hid, hid), hid)]
        load_u.append(move(src, R.wu.at[qkv_rows, g * hid : (g + 1) * hid], local.at[7 + g]))
    down_src = R.w_down.at[pl.ds(pl.multiple_of(col * hid, hid), hid)]
    down_rows = pl.ds(pl.multiple_of(layer * hid, hid), hid)
    load_d = move(down_src, R.wd.at[down_rows], local.at[11])
    load_p = []
    for row, item in enumerate(R.vectors):
        load_p.append(move(item, R.pv.at[layer, row], local.at[12 + row]))
    load_b = move(R.b_up, R.pb.at[layer], local.at[11 + 9])
    load_x.wait()
    first, second = (row_norm(R.xb[s].astype(f32))[0] for s in range(2))
    R.r1[0] = first
    R.r1[1] = second
    for s in range(seqs):
        lane = lax.broadcasted_iota(jnp.int32, (1, seq_len), 1)
        half_rows = tokens // 2
        pos = jnp.zeros((1, seq_len), jnp.int32)
        down = lax.broadcasted_iota(jnp.int32, (half_rows, 128), 0)
        for j in range(seq_len // half_rows):
            start = R.order[s, j] * half_rows
            pos = jnp.where(lane // half_rows == j, start, pos)
            R.kpos[s, j * half_rows : (j + 1) * half_rows, :] = down + start
        R.qpos[s] = pos + lane % half_rows
    for copy in load_p:
        copy.wait()
    load_b.wait()
    pl.semaphore_wait(barrier, 12)

    zs, zr = R.zs, R.zr

    def to_planes(src, dst, slot):
        return [
            send(src, dst, zs.at[slot, hop - 1], zr.at[slot, hop - 1], (col, ring.up(hop)))
            for hop in range(1, 4)
        ]

    send_par = to_planes(R.pv.at[layer], R.pv.at[layer], 0)
    send_par += to_planes(R.pb.at[layer], R.pb.at[layer], 1)

    def rows_of(ref, count):
        return lambda index: ref.at[pl.ds(pl.multiple_of(index * count, count), count)]

    chain_q, chain_u, chain_d = (
        Chain(ring, rows_of(ref, count), R.cs.at[slot], R.cr.at[slot])
        for slot, (ref, count) in enumerate(((R.wq, rows_z), (R.wu, rows_z), (R.wd, hid)))
    )
    for copy in load_q:
        copy.wait()
    chain_q.start()

    def gather_rows(ref, s, slot):

        def block(index):
            return ref.at[s, pl.ds(pl.multiple_of(index * tokens, tokens), tokens)]

        def half(index, part):
            count = tokens // 2
            first = pl.multiple_of(index * tokens + part * count, count)
            return ref.at[s, pl.ds(first, count)]

        return Gather(ring, wire, block, half, R.gs.at[slot], R.gr.at[slot])

    h1_gather = [gather_rows(R.h1, s, s) for s in range(seqs)]
    ct_gather = [gather_rows(R.ct, s, 2 + s) for s in range(seqs)]
    h2_gather = [gather_rows(R.h2, s, 4 + s) for s in range(seqs)]
    wo_gather = Gather(
        ring,
        wire,
        lambda index: R.wo.at[:, index],
        lambda index, part: R.wo.at[2 * part : 2 * part + 2, index],
        R.gs.at[6],
        R.gr.at[6],
    )

    for copy in load_ct:
        copy.wait()
    ct_gather[0].start()


    def params_row(row):
        pieces = []
        for plane in range(4):
            both = R.pv[plane, row].astype(f32)
            pieces += [both[0:1, :], both[1:2, :]]
        return jnp.concatenate(pieces, axis=1)

    for copy in send_par:
        copy.wait_recv()
    gain1, shift1 = params_row(0), params_row(1)
    R.h1[0, mine] = (R.r1[0] * gain1 + shift1).astype(bf16)
    h1_gather[0].start()
    R.h1[1, mine] = (R.r1[1] * gain1 + shift1).astype(bf16)
    h1_gather[1].start()
    for copy in load_u:
        copy.wait()
    chain_u.start()
    load_o.wait()
    send_o = to_planes(out_src, R.wo.at[layer, col], 4)

    def chosen(rows):
        total = rows[0]
        for index, item in enumerate(rows[1:]):
            total = jnp.where(col == index + 1, item, total)
        return total

    def head_row(row):
        parts = [R.pv[plane, row].astype(f32) for plane in range(4)]
        return chosen([parts[j // 2][j % 2 : j % 2 + 1, :] for j in range(8)])

    bias_q, bias_v = head_row(2), head_row(3)
    pieces = []
    for plane in range(4):
        rows = R.pb[plane].astype(f32)
        pieces.append(chosen([rows[j : j + 1, :] for j in range(8)]))
    bias_u = jnp.concatenate(pieces, axis=1)
    tile = 256


    def span(chip):
        return pl.ds(pl.multiple_of(chip * tile, tile), tile)

    chip_x, chip_y = (col // 2) % 2, col // 4

    def order(t):
        flip_x, flip_y = 1 - t[0], 1 - t[1]
        place_x = chip_x + flip_x - 2 * chip_x * flip_x
        place_y = chip_y + flip_y - 2 * chip_y * flip_y
        return place_x + 2 * place_y, flip_x + 2 * flip_y

    def pairs(body, **between):
        @pl.loop(0, 2)
        def _(high):
            body((high, 0))
            body((high, 1))
            for name, action in between.items():
                pl.when(high == int(name[1:]))(action)

    def tiles(body, **between):
        @pl.loop(0, 2)
        def _(high):
            @pl.loop(0, 2)
            def _(low):
                body((high, low))
                t = 2 * high + low
                for name, action in between.items():
                    pl.when(t == int(name[1:]))(action)

    def project(s):
        @pl.loop(0, 4)
        def _(t):
            r = span(t)
            both = dot_nn(R.h1[s, r, :], R.wq[...])
            R.q[s, r, :] = (both[:, :head] + bias_q).astype(bf16)
            R.k[s, r, :] = both[:, head : 2 * head].astype(bf16)
            R.v[s, r, :] = (both[:, 2 * head :] + bias_v).astype(bf16)

        R.kt[s] = R.k[s].T
        R.vt[s] = R.v[s].T

    def masked(s, r, scores, other):
        keys = jnp.concatenate([R.kpos[s]] * (tile // 128), axis=1)
        return jnp.where(R.qpos[s, :, r] >= keys, scores, other)

    def attend(s, t):
        r = span(2 * t[0] + t[1])
        raw = masked(s, r, dot_nt(R.k[s], R.q[s, r, :]), NEG_LARGE)
        top = jnp.max(raw, axis=0, keepdims=True)
        weights = jnp.exp2((raw - top) * step_c2)
        total = jnp.sum(weights, axis=0, keepdims=True)
        turned = dot_nn(R.vt[s], weights.astype(bf16)) * (1.0 / total)
        R.ol[s, r, :] = turned.T.astype(bf16)
        R.lse[s, :, r] = top * step_c2 + jnp.log2(total)

    others = (ring.dsib, ring.diag, ring.xsib, ring.xnb, ring.ysib, ring.ynb, ring.sib)

    def heads_to_rows(s):
        R.ob[s, :, pl.ds(head_cols, head)] = R.ol[s, mine, :]
        copies = []
        for slot, other in enumerate(others):
            src = R.ol.at[s, pl.ds(pl.multiple_of(other * tokens, tokens), tokens)]
            dst = R.ob.at[s, :, pl.ds(head_cols, head)]
            copies.append(
                send(src, dst, R.a_s.at[s, slot], R.a_r.at[s, slot], ring.flat(other))
            )
        return copies

    def rows_to_heads(s):
        R.dh[s, mine, :] = R.db[s, :, pl.ds(head_cols, head)]
        copies = []
        for slot, other in enumerate(others):
            src = R.db.at[s, :, pl.ds(pl.multiple_of(other * head, head), head)]
            dst = R.dh.at[s, mine]
            copies.append(
                send(src, dst, R.a_s.at[2 + s, slot], R.a_r.at[2 + s, slot], ring.flat(other))
            )
        return copies

    bias_o = params_row(4)
    gain2, shift2 = params_row(5), params_row(6)
    out_w = R.wo

    def out_project(s):
        for copy in moved_o[s]:
            copy.wait_recv()
        weight = out_w[...].reshape(width, width)
        resid = R.xb[s].astype(f32) + dot_nn(R.ob[s], weight) + bias_o
        R.r1[s] = resid
        normed, _ = row_norm(resid)
        R.h2[s, mine] = (normed * gain2 + shift2).astype(bf16)

    def many(*actions):
        def run():
            for action in actions:
                action()

        return run

    ct_gather[0].relay()
    h1_gather[0].relay()
    chain_q.pass_on(1)
    h1_gather[1].relay()
    h1_gather[0].relay_diag()
    ct_gather[0].relay_diag()
    ct_gather[1].start()
    chain_q.pass_on(2)
    load_d.wait()
    chain_d.start()
    h1_gather[0].finish()
    chain_q.pass_on(3)
    project(0)
    chain_u.pass_on(1)
    h1_gather[1].relay_diag()
    for copy in send_o:
        copy.wait_recv()
    wo_gather.start()
    pairs(lambda t: attend(0, t), t0=wo_gather.relay)
    moved_o = [heads_to_rows(0)]
    h1_gather[1].finish()
    ct_gather[1].relay()
    project(1)
    wo_gather.relay_diag()
    chain_u.pass_on(2)

    def first_rows():
        out_project(0)
        h2_gather[0].start()

    tiles(
        lambda t: attend(1, t),
        t0=lambda: chain_d.pass_on(1),
        t1=many(wo_gather.finish, first_rows),
        t2=ct_gather[1].relay_diag,
    )
    moved_o.append(heads_to_rows(1))
    h2_gather[0].relay()
    chain_u.pass_on(3)
    out_project(1)
    h2_gather[1].start()
    chain_d.pass_on(2)
    h2_gather[0].relay_diag()
    ct_gather[0].finish()
    h2_gather[0].finish()
    chain_d.pass_on(3)

    def feed(s, t):
        chip, slot = order(t)
        r = span(chip)
        hidden = dot_nn(R.h2[s, r, :], R.wu[...]) + bias_u
        grad = dot_nt(R.ct[s, r, :], R.wd[...])
        square = hidden * hidden
        bend = jnp.tanh(hidden * (GELU_C + (GELU_C * GELU_K) * square))
        half = 0.5 * (1.0 + bend)
        active = (hidden * half).astype(bf16)
        slope = half + (0.5 * hidden) * (1.0 - bend * bend) * (
            GELU_C + (3.0 * GELU_C * GELU_K) * square
        )
        R.act[s, r, :] = active
        grad = (grad * slope).astype(bf16)
        R.du[s, r, :] = grad
        R.pd[s, r, :] = dot_nt(grad, R.wu[...]).astype(bf16)
        R.po[s, r, :] = dot_nn(active, R.wd[...]).astype(bf16)
        R.us[...] += jnp.sum(grad.astype(f32), axis=0, keepdims=True)
        d2[s].start_of(chip, slot)
        out_sc[s].start_of(chip, slot)

    def scatter(part, s, recv, slot, rows=None):
        return Scatter(
            ring,
            wire,
            part,
            tokens,
            R.r_sib.at[recv],
            R.r_diag.at[recv],
            R.r_side.at[recv],
            R.ss.at[slot],
            R.sr.at[slot],
        )

    R.us[...] = jnp.zeros_like(R.us)
    d2 = [scatter(R.pd.at[s], s, s, s) for s in range(2)]
    out_sc = [scatter(R.po.at[s], s, 2 + s, 2 + s) for s in range(2)]
    pairs(
        lambda t: feed(0, t),
        t0=many(h2_gather[1].relay, d2[0].middle),
        t1=many(h2_gather[1].relay_diag, d2[0].early),
    )
    d2[0].last()
    h2_gather[1].finish()
    ct_gather[1].finish()
    pairs(lambda t: feed(1, t), t0=d2[1].middle, t1=d2[1].early)

    bz = R.bz
    for g in range(4):
        bz[2 + g : 3 + g, :] = R.us[:, g * hid : (g + 1) * hid]


    def grad_down():
        for j in range(2):
            cols = slice(j * 2 * hid, (j + 1) * 2 * hid)
            total = dot_tn(R.act[0, :, cols], R.ct[0])
            total = total + dot_tn(R.act[1, :, cols], R.ct[1])
            R.gd[cols, :] = total.astype(bf16)

    def grad_up():
        for j in range(2):
            cols = slice(j * 2 * hid, (j + 1) * 2 * hid)
            total = dot_tn(R.du[0, :, cols], R.h2[0])
            total = total + dot_tn(R.du[1, :, cols], R.h2[1])
            total = total.T.astype(bf16).reshape(8, 4, 32, 2 * hid)
            R.gu[:, :, :, cols] = total

    def to_planes_part(piece, dst, slot):
        return [
            send(
                piece(ring.up(hop)),
                dst.at[hop - 1],
                zs.at[slot, hop - 1],
                zr.at[slot, hop - 1],
                (col, ring.up(hop)),
            )
            for hop in range(1, 4)
        ]

    sums = {}

    def back_norm2(s):
        grad = d2[s].finish()
        normed, inv_dev = row_norm(R.r1[s])
        cot = R.ct[s, mine].astype(f32)
        scaled = grad * gain2
        resid = cot + inv_dev * (
            scaled
            - jnp.mean(scaled, axis=-1, keepdims=True)
            - normed * jnp.mean(scaled * normed, axis=-1, keepdims=True)
        )
        R.dr[s] = resid
        low = resid.astype(bf16)
        R.dz[s] = low
        lowf = low.astype(f32)
        parts = (
            jnp.sum(lowf, axis=0, keepdims=True),
            jnp.sum(grad * normed, axis=0, keepdims=True),
            jnp.sum(grad, axis=0, keepdims=True),
            jnp.sum(cot, axis=0, keepdims=True),
        )
        for row, item in enumerate(parts):
            sums[row] = sums[row] + item if row in sums else item
        R.db[s] = dot_nt(low, out_w[...].reshape(width, width)).astype(bf16)

    def attend_back(s, t):
        r = span(2 * t[0] + t[1])
        query, dout = R.q[s, r, :], R.dh[s, r, :]
        raw = dot_nt(R.k[s], query)
        probs = masked(s, r, jnp.exp2(raw * step_c2 - R.lse[s, :, r]), 0.0)
        grad = dot_nt(R.v[s], dout)
        part_v = dot_nn(probs.astype(bf16), dout)
        delta = jnp.sum(probs * grad, axis=0, keepdims=True)
        low = (probs * ((grad - delta) * scale)).astype(bf16)
        part_k = dot_nn(low, query)
        R.dp[s, r, :head] = dot_nn(R.kt[s], low).T.astype(bf16)
        R.dva[s] += part_v
        R.dka[s] += part_k

    def close_back(s):
        R.dp[s, :, head : 2 * head] = R.dka[s].astype(bf16)
        R.dp[s, :, 2 * head :] = R.dva[s].astype(bf16)

    def first_part(s, t):
        chip, slot = order(t)
        r = span(chip)
        R.pd[s, r, :] = dot_nt(R.dp[s, r, :], R.wq[...]).astype(bf16)
        d1[s].start_of(chip, slot)

    back_norm2(0)
    moved_d = [rows_to_heads(0)]
    d2[1].last()
    grad_down()
    z_down = Halve(ring, wire, rows_of(R.gd, hid), R.zd.at[0:2], R.zd.at[2], zs.at[10], zr.at[10])
    z_down.start()
    out_sc[0].middle()
    grad_up()
    z_up = Halve(
        ring, wire, lambda other: R.gu.at[:, other], R.zu.at[0:2], R.zu.at[2], zs.at[11], zr.at[11]
    )
    z_up.start()
    back_norm2(1)
    moved_d.append(rows_to_heads(1))
    out_sc[0].early()
    out_sc[0].last()

    h2_flat = R.h2.at[0]
    for gather in h2_gather:
        gather.drain()
    h2_flat[...] = (dot_tn(R.ob[0], R.dz[0]) + dot_tn(R.ob[1], R.dz[1])).astype(bf16)
    wo_sc = scatter(h2_flat, 0, 4, 6)
    wo_sc.start()
    R.dva[...] = jnp.zeros_like(R.dva)
    R.dka[...] = jnp.zeros_like(R.dka)
    for copy in moved_d[0]:
        copy.wait_recv()
    pairs(lambda t: attend_back(0, t), t0=wo_sc.middle)
    close_back(0)
    d2[0].drain()
    d1 = [scatter(R.pd.at[s], s, s, 4 + s) for s in range(2)]
    tiles(lambda t: first_part(0, t))
    z_down.middle()
    for copy in moved_d[1]:
        copy.wait_recv()
    tiles(
        lambda t: attend_back(1, t),
        t0=many(d1[0].middle, d1[0].early, out_sc[1].middle),
        t2=many(d1[0].last, z_up.middle),
        t3=many(wo_sc.early, wo_sc.last),
    )
    close_back(1)
    d2[1].drain()
    tiles(lambda t: first_part(1, t), t2=d1[1].middle)
    proj_sums = jnp.sum(R.dp[0].astype(f32), axis=0, keepdims=True) + jnp.sum(
        R.dp[1].astype(f32), axis=0, keepdims=True
    )
    bz[0:1, :] = proj_sums[:, :head]
    bz[1:2, :] = proj_sums[:, 2 * head :]
    bz[6:8, :] = jnp.zeros((2, head), f32)
    z_b = to_planes(bz, R.zb.at[layer], 13)
    for g in range(3):
        cols = slice(g * head, (g + 1) * head)
        total = dot_tn(R.dp[0, :, cols], R.h1[0]) + dot_tn(R.dp[1, :, cols], R.h1[1])
        R.gq[:, :, :, cols] = total.T.astype(bf16).reshape(8, 4, 32, head)
    z_q = Halve(
        ring, wire, lambda other: R.gq.at[:, other], R.zq.at[0:2], R.zq.at[2], zs.at[12], zr.at[12]
    )
    z_q.start()
    d1[1].early()
    d1[1].last()
    out_sc[1].early()
    out_sc[1].last()
    R.gws[...] = wo_sc.finish().astype(bf16)
    z_o = to_planes_part(
        lambda other: R.gws.at[pl.ds(pl.multiple_of(other * 32, 32), 32)], R.zo, 15
    )

    R.gdo[...] = z_down.finish().astype(bf16)
    for copy in z_b:
        copy.wait_recv()
    bz_all = bz[...] + (R.zb[ring.up(1)] + R.zb[ring.up(2)] + R.zb[ring.up(3)])
    R.bzs[...] = bz_all
    own_up = jnp.zeros((1, head), f32)
    for k in range(4):
        own_up = jnp.where(layer == k, bz_all[2 + k : 3 + k, :], own_up)
    R.bu[...] = jnp.broadcast_to(own_up, (8, head))
    psem = R.ps
    home_copies = (
        (R.gdo, R.o_gd, psem.at[0], psem.at[2], psem.at[3]),
        (R.bu, R.o_bu, psem.at[1], psem.at[4], psem.at[5]),
    )

    @pl.when(at_home)
    def _():
        for src, dst, sem, _, _ in home_copies:
            move(src, dst, sem).wait()

    away = [
        Sent(src, dst, ssem, rsem, (owner_col, owner_layer))
        for src, dst, _, ssem, rsem in home_copies
    ]

    @pl.when(jnp.logical_not(at_home))
    def _():
        for copy in away:
            copy.start()

    def to_columns(src, dst, row):
        keep = move(src.at[col], dst.at[col], local.at[21 + row])
        copies = []
        for slot, other in enumerate(others):
            copies.append(
                send(
                    src.at[other],
                    dst.at[col],
                    R.a_s.at[4 + row, slot],
                    R.a_r.at[4 + row, slot],
                    ring.flat(other),
                )
            )
        return keep, copies

    R.guo[...] = z_up.finish().astype(bf16)
    up_keep, up_moves = to_columns(R.guo, R.o_gu, 0)

    bias_d = params_row(7)
    for s in range(2):
        R.los[s] = (R.r1[s] + out_sc[s].finish() + bias_d).astype(bf16)
    save_lo = move(R.los, R.o_lo, local.at[24])

    def back_norm1(s):
        grad = d1[s].finish()
        normed, inv_dev = row_norm(R.xb[s].astype(f32))
        scaled = grad * gain1
        total = R.dr[s] + inv_dev * (
            scaled
            - jnp.mean(scaled, axis=-1, keepdims=True)
            - normed * jnp.mean(scaled * normed, axis=-1, keepdims=True)
        )
        R.igs[s] = total.astype(bf16)
        for row, item in ((4, grad * normed), (5, grad)):
            item = jnp.sum(item, axis=0, keepdims=True)
            sums[row] = sums[row] + item if row in sums else item

    back_norm1(0)
    z_q.middle()
    back_norm1(1)
    save_ig = move(R.igs, R.o_ig, local.at[23])
    for row in range(6):
        R.ev[row : row + 1, :] = sums[row]
    R.ev[6:8, :] = jnp.zeros((2, width), f32)
    ev_moves = []
    for hop in range(1, 8):
        other = (col + hop) % 8
        ev_moves.append(
            send(
                R.ev.at[:, pl.ds(pl.multiple_of(other * head, head), head)],
                R.evr.at[hop - 1],
                R.es.at[hop - 1],
                R.er.at[hop - 1],
                ring.flat(other),
            )
        )
    R.gqo[...] = z_q.finish().astype(bf16)
    q_keep, q_moves = to_columns(R.gqo, R.o_gq, 1)
    for copy in ev_moves:
        copy.wait_recv()
    plane = R.ev[:, pl.ds(head_cols, head)]
    for k in range(7):
        plane = plane + R.evr[k]
    R.evp[...] = plane
    z_e = to_planes(R.evp, R.evz.at[layer], 14)
    for copy in z_o:
        copy.wait_recv()
    go_rows = pl.ds(pl.multiple_of(layer * 32, 32), 32)
    total = R.gws[go_rows].astype(f32)
    for k in range(3):
        total = total + R.zo[k].astype(f32)
    R.o_go[...] = total
    for copy in z_e:
        copy.wait_recv()
    total = R.evp[...] + (R.evz[ring.up(1)] + R.evz[ring.up(2)] + R.evz[ring.up(3)])
    both = jnp.concatenate([total, R.bzs[...]], axis=0)
    picked = jnp.zeros((16, 32), f32)
    for k in range(4):
        picked = jnp.where(layer == k, both[:, k * 32 : (k + 1) * 32], picked)
    R.o_small[...] = picked

    @pl.when(jnp.logical_not(at_home))
    def _():
        for copy in away:
            copy.wait_recv()
            copy.wait_send()

    save_ig.wait()
    save_lo.wait()
    for keep, copies in ((up_keep, up_moves), (q_keep, q_moves)):
        keep.wait()
        for copy in copies:
            copy.wait_recv()
    wire.drain()
    for chain in (chain_q, chain_u, chain_d):
        chain.drain()


def closing_kernel(refs):
    R = refs
    f32 = jnp.float32
    head = HEAD_DIM
    sem = R.sem
    plan = (
        (R.gd, R.vd, R.td, R.f_gd),
        (R.gu, R.vu, R.tu, R.f_gu),
        (R.gq, R.vq, R.tq, R.f_gq),
        (R.lo, R.vl, R.vl, R.f_lo),
        (R.ig, R.vi, R.vi, R.f_ig),
        (R.go, R.vo, R.vo, R.f_go),
    )
    loads = [move(src, held, sem.at[slot]) for slot, (src, held, _, _) in enumerate(plan)]
    waits = []
    for slot, (_, held, wide, dst) in enumerate(plan):
        loads[slot].wait()
        if slot == 0:
            wide[...] = held[...].astype(f32)
        elif slot < 3:
            groups = held.shape[2] // head
            for g in range(groups):
                for c in range(8):
                    first = (g * 8 + c) * head
                    piece = held[c, :, g * head : (g + 1) * head]
                    wide[:, first : first + head] = piece.astype(f32)
        waits.append(move(wide, dst, sem.at[6 + slot]))
    for row, ref in R.rows:
        ref[...] = R.small[row]
    R.f_bu[...] = R.bu[0]
    for copy in waits:
        copy.wait()

def per_device_tp(
    layer_in,
    block_order,
    ln1_gain,
    ln1_shift,
    w_qkv,
    b_query,
    b_value,
    w_out,
    b_out,
    ln2_gain,
    ln2_shift,
    w_up,
    b_up,
    w_down,
    b_down,
    cotangent,
):
    f32, bf16, i32 = jnp.float32, jnp.bfloat16, jnp.int32
    seqs, tokens, width = layer_in.shape
    seq_len = tokens * 8
    ff = w_up.shape[1]
    hid = ff // 32
    vectors = [
        item.reshape(2, -1)
        for item in (ln1_gain, ln1_shift, b_query, b_value, b_out, ln2_gain, ln2_shift, b_down)
    ]
    anywhere = pl.BlockSpec(memory_space=pl.ANY)
    in_vmem = pl.BlockSpec(memory_space=pltpu.VMEM)
    inputs = dict(
        order=(block_order, pl.BlockSpec(memory_space=pltpu.SMEM)),
        b_up=(b_up.reshape(8, -1), anywhere),
        x=(layer_in, anywhere),
        cot=(cotangent, anywhere),
        w_qkv=(w_qkv, anywhere),
        w_out=(w_out, anywhere),
        w_up=(w_up, anywhere),
        w_down=(w_down, anywhere),
    )
    outputs = dict(
        o_lo=((seqs, tokens, width), bf16, anywhere),
        o_ig=((seqs, tokens, width), bf16, anywhere),
        o_gq=((8, 32, 3 * HEAD_DIM), bf16, anywhere),
        o_gu=((8, 32, 4 * hid), bf16, anywhere),
        o_gd=((hid, width), bf16, anywhere),
        o_go=((32, width), f32, in_vmem),
        o_small=((16, 32), f32, in_vmem),
        o_bu=((8, HEAD_DIM), f32, anywhere),
    )
    whole = (seqs, seq_len, width)
    heads = (seqs, seq_len, HEAD_DIM)
    turned = (seqs, HEAD_DIM, seq_len)
    own = (seqs, tokens, width)
    vmem, sems = pltpu.VMEM, pltpu.SemaphoreType.DMA
    scratch = dict(
        h1=vmem(whole, bf16),
        ct=vmem(whole, bf16),
        h2=vmem(whole, bf16),
        po=vmem(whole, bf16),
        pd=vmem(whole, bf16),
        wq=vmem((width, 3 * HEAD_DIM), bf16),
        wo=vmem((4, 8, 32, width), bf16),
        wu=vmem((width, 4 * hid), bf16),
        wd=vmem((4 * hid, width), bf16),
        q=vmem(heads, bf16),
        k=vmem(heads, bf16),
        v=vmem(heads, bf16),
        kt=vmem(turned, bf16),
        vt=vmem(turned, bf16),
        ol=vmem(heads, bf16),
        dh=vmem(heads, bf16),
        ob=vmem(own, bf16),
        db=vmem(own, bf16),
        xb=vmem(own, bf16),
        dz=vmem(own, bf16),
        igs=vmem(own, bf16),
        los=vmem(own, bf16),
        r1=vmem(own, f32),
        dr=vmem(own, f32),
        r_sib=vmem((5, 4, tokens, width), bf16),
        r_diag=vmem((5, 2, tokens // 2, width), bf16),
        r_side=vmem((5, 2, tokens, width), bf16),
        kpos=vmem(heads, i32),
        qpos=vmem((seqs, 1, seq_len), i32),
        lse=vmem((seqs, 1, seq_len), f32),
        act=vmem((seqs, seq_len, 4 * hid), bf16),
        du=vmem((seqs, seq_len, 4 * hid), bf16),
        dp=vmem((seqs, seq_len, 3 * HEAD_DIM), bf16),
        dka=vmem(heads, f32),
        dva=vmem(heads, f32),
        gd=vmem((4 * hid, width), bf16),
        gu=vmem((8, 4, 32, 4 * hid), bf16),
        gq=vmem((8, 4, 32, 3 * HEAD_DIM), bf16),
        gws=vmem((tokens, width), bf16),
        gdo=vmem((hid, width), bf16),
        guo=vmem((8, 32, 4 * hid), bf16),
        gqo=vmem((8, 32, 3 * HEAD_DIM), bf16),
        zd=vmem((3, hid, width), bf16),
        zu=vmem((3, 8, 32, 4 * hid), bf16),
        zq=vmem((3, 8, 32, 3 * HEAD_DIM), bf16),
        zo=vmem((3, 32, width), bf16),
        pv=vmem((4, 8, 2, HEAD_DIM), bf16),
        pb=vmem((4, 8, HEAD_DIM), bf16),
        us=vmem((1, 4 * hid), f32),
        bz=vmem((8, HEAD_DIM), f32),
        bzs=vmem((8, HEAD_DIM), f32),
        bu=vmem((8, HEAD_DIM), f32),
        zb=vmem((4, 8, HEAD_DIM), f32),
        ev=vmem((8, width), f32),
        evr=vmem((7, 8, HEAD_DIM), f32),
        evp=vmem((8, HEAD_DIM), f32),
        evz=vmem((4, 8, HEAD_DIM), f32),
        lsem=sems((25,)),
        zs=sems((16, 3)),
        zr=sems((16, 3)),
        cs=sems((3, 2, 3)),
        cr=sems((3, 2, 3)),
        gs=sems((7, 10)),
        gr=sems((7, 10)),
        ss=sems((7, 10)),
        sr=sems((7, 10)),
        a_s=sems((6, 7)),
        a_r=sems((6, 7)),
        es=sems((7,)),
        er=sems((7,)),
        ps=sems((6,)),
    )
    names = list(inputs) + list(outputs) + list(scratch)

    def body(*refs):
        space = types.SimpleNamespace(**dict(zip(names, refs[8:])))
        space.vectors = refs[:8]
        layer_kernel(HEAD_DIM ** (-0.5), space)

    results = pl.pallas_call(
        body,
        out_shape=[jax.ShapeDtypeStruct(shape, kind) for shape, kind, _ in outputs.values()],
        in_specs=[anywhere] * 8 + [spec for _, spec in inputs.values()],
        out_specs=[spec for _, _, spec in outputs.values()],
        scratch_shapes=list(scratch.values()),
        compiler_params=pltpu.CompilerParams(
            collective_id=0, has_side_effects=True, vmem_limit_bytes=VMEM_BYTES
        ),
    )(*vectors, *(item for item, _ in inputs.values()))
    finals = dict(
        f_lo=((seqs, tokens, width), bf16, anywhere),
        f_ig=((seqs, tokens, width), bf16, anywhere),
        f_g1=((32,), f32, in_vmem),
        f_s1=((32,), f32, in_vmem),
        f_gq=((32, 3 * width), f32, anywhere),
        f_bq=((32,), f32, in_vmem),
        f_bv=((32,), f32, in_vmem),
        f_go=((32, width), f32, anywhere),
        f_bo=((32,), f32, in_vmem),
        f_g2=((32,), f32, in_vmem),
        f_s2=((32,), f32, in_vmem),
        f_gu=((32, ff), f32, anywhere),
        f_bu=((HEAD_DIM,), f32, in_vmem),
        f_gd=((hid, width), f32, anywhere),
        f_bd=((32,), f32, in_vmem),
    )
    held = dict(
        vd=vmem((hid, width), bf16),
        vu=vmem((8, 32, 4 * hid), bf16),
        vq=vmem((8, 32, 3 * HEAD_DIM), bf16),
        td=vmem((hid, width), f32),
        tu=vmem((32, ff), f32),
        tq=vmem((32, 3 * width), f32),
        vl=vmem(own, bf16),
        vi=vmem(own, bf16),
        vo=vmem((32, width), f32),
        sem=sems((12,)),
    )
    last_names = [item[2:] for item in outputs] + list(finals) + list(held)

    def last_body(*refs):
        space = types.SimpleNamespace(**dict(zip(last_names, refs)))
        space.rows = (
            (4, space.f_g1),
            (5, space.f_s1),
            (8, space.f_bq),
            (9, space.f_bv),
            (0, space.f_bo),
            (1, space.f_g2),
            (2, space.f_s2),
            (3, space.f_bd),
        )
        closing_kernel(space)

    return tuple(
        pl.pallas_call(
            last_body,
            out_shape=[jax.ShapeDtypeStruct(shape, kind) for shape, kind, _ in finals.values()],
            in_specs=[anywhere] * 6 + [in_vmem] * 2,
            out_specs=[spec for _, _, spec in finals.values()],
            scratch_shapes=list(held.values()),
        )(*results)
    )


def solution(mesh):
    placed = (
        P("fsdp", "ctx", None),
        P("fsdp", None),
        P("fsdp"),
        P("fsdp"),
        P("fsdp", None),
        P("fsdp"),
        P("fsdp"),
        P("fsdp", None),
        P("fsdp"),
        P("fsdp"),
        P("fsdp"),
        P("fsdp", None),
        P("fsdp"),
        P("fsdp", None),
        P("fsdp"),
        P("fsdp", "ctx", None),
    )
    by_heads = mesh.shape["ctx"] == HEADS and mesh.shape["fsdp"] == 4
    return jax.shard_map(
        per_device_tp if by_heads else per_device_ctx,
        mesh=mesh,
        in_specs=placed,
        out_specs=(
            P("fsdp", "ctx", None),
            P("fsdp", "ctx", None),
            P(("ctx", "fsdp")),
            P(("ctx", "fsdp")),
            P(("ctx", "fsdp"), None),
            P(("ctx", "fsdp")),
            P(("ctx", "fsdp")),
            P(("ctx", "fsdp"), None),
            P(("ctx", "fsdp")),
            P(("ctx", "fsdp")),
            P(("ctx", "fsdp")),
            P(("ctx", "fsdp"), None),
            P(("ctx", "fsdp")),
            P(("ctx", "fsdp"), None),
            P(("ctx", "fsdp")),
        ),
        check_vma=False,
    )
```

```python
import math
import types

import jax
import jax.numpy as jnp
from jax import lax
from jax.experimental import pallas as pl
from jax.experimental.pallas import tpu as pltpu
from jax.sharding import PartitionSpec as P

D = 1024
HEADS = 8
HEAD_DIM = 128


EPSILON = 1e-05
NEG_LARGE = -1e30
GELU_C = math.sqrt(2.0 / math.pi)
GELU_K = 0.044715
VMEM_BYTES = 63 << 20


def gelu_tanh(values):
    inner = jnp.tanh(GELU_C * (values + GELU_K * values * values * values))
    return 0.5 * values * (1.0 + inner)


def gelu_slope(values):
    inner = jnp.tanh(GELU_C * (values + GELU_K * values * values * values))
    return 0.5 * (1.0 + inner) + 0.5 * values * (1.0 - inner * inner) * GELU_C * (
        1.0 + 3.0 * GELU_K * values * values
    )


def normalize(values, gain_vec, shift_vec):
    average = jnp.mean(values, axis=-1, keepdims=True)
    centered = values - average
    inv_dev = lax.rsqrt(jnp.mean(centered * centered, axis=-1, keepdims=True) + EPSILON)
    normed = centered * inv_dev
    return (normed * gain_vec + shift_vec, normed, inv_dev)


def normalize_back(grad, normed, inv_dev, gain_vec):
    scaled = grad * gain_vec
    return inv_dev * (
        scaled
        - jnp.mean(scaled, axis=-1, keepdims=True)
        - normed * jnp.mean(scaled * normed, axis=-1, keepdims=True)
    )


def token_positions(order_row, seq_len, half_rows):
    rows = jnp.arange(seq_len, dtype=jnp.int32)
    slots = jnp.arange(order_row.shape[0], dtype=jnp.int32)
    picked = jnp.sum(
        jnp.where((rows // half_rows)[:, None] == slots[None, :], order_row[None, :], 0), axis=1
    )
    return picked * half_rows + rows % half_rows


def block_probs(query_heads, key_heads, query_pos, key_pos, row_lse, scale):
    raw_scores = jnp.einsum(
        "qhd,khd->hqk", query_heads, key_heads, preferred_element_type=jnp.float32
    )
    allowed = (query_pos[:, None] >= key_pos[None, :])[None]
    shifted = jnp.where(allowed, raw_scores * scale - row_lse[:, :, None], NEG_LARGE)
    return jnp.where(allowed, jnp.exp(shifted), 0.0)


def score_grads(probs, grad_probs, row_delta, scale):
    return (probs * (grad_probs - row_delta[:, :, None]) * scale).astype(jnp.bfloat16)


def per_device_ctx(
    layer_in,
    block_order,
    ln1_gain,
    ln1_shift,
    w_qkv,
    b_query,
    b_value,
    w_out,
    b_out,
    ln2_gain,
    ln2_shift,
    w_up,
    b_up,
    w_down,
    b_down,
    cotangent,
):
    full = (
        lax.all_gather(ln1_gain, "fsdp", axis=0, tiled=True),
        lax.all_gather(ln1_shift, "fsdp", axis=0, tiled=True),
        lax.all_gather(w_qkv, "fsdp", axis=0, tiled=True),
        lax.all_gather(b_query, "fsdp", axis=0, tiled=True),
        lax.all_gather(b_value, "fsdp", axis=0, tiled=True),
        lax.all_gather(w_out, "fsdp", axis=0, tiled=True),
        lax.all_gather(b_out, "fsdp", axis=0, tiled=True),
        lax.all_gather(ln2_gain, "fsdp", axis=0, tiled=True),
        lax.all_gather(ln2_shift, "fsdp", axis=0, tiled=True),
        lax.all_gather(w_up, "fsdp", axis=0, tiled=True),
        lax.all_gather(b_up, "fsdp", axis=0, tiled=True),
        lax.all_gather(w_down, "fsdp", axis=0, tiled=True),
        lax.all_gather(b_down, "fsdp", axis=0, tiled=True),
    )
    qkv_full, out_full, up_full, down_full = (full[2], full[5], full[9], full[11])
    first_gain = full[0].astype(jnp.float32)
    first_shift = full[1].astype(jnp.float32)
    query_bias = full[3].astype(jnp.float32)
    value_bias = full[4].astype(jnp.float32)
    out_bias = full[6].astype(jnp.float32)
    second_gain = full[7].astype(jnp.float32)
    second_shift = full[8].astype(jnp.float32)
    up_bias = full[10].astype(jnp.float32)
    down_bias = full[12].astype(jnp.float32)
    micro = layer_in.shape[0]
    tokens = layer_in.shape[1]
    seq_len = tokens * lax.axis_size("ctx")
    half_rows = tokens // 2
    key_block = min(512, seq_len)
    blocks = seq_len // key_block
    scale = HEAD_DIM ** (-0.5)
    here = lax.axis_index("ctx")
    heads_shape = (blocks, key_block, HEADS, HEAD_DIM)
    totals = [jnp.zeros(item.shape, jnp.float32) for item in full]
    outputs_fwd = []
    outputs_grad = []
    for micro_step in range(micro):
        pos_all = token_positions(block_order[micro_step], seq_len, half_rows)
        pos_mine = lax.dynamic_slice_in_dim(pos_all, here * tokens, tokens)
        pos_blocks = pos_all.reshape(blocks, key_block)
        inputs = layer_in[micro_step].astype(jnp.float32)
        first_out, first_normed, first_inv = normalize(inputs, first_gain, first_shift)
        first_low = first_out.astype(jnp.bfloat16)
        projected = jnp.dot(first_low, qkv_full, preferred_element_type=jnp.float32)
        query_low = (projected[:, :D] + query_bias).astype(jnp.bfloat16)
        key_low = projected[:, D : 2 * D].astype(jnp.bfloat16)
        value_low = (projected[:, 2 * D :] + value_bias).astype(jnp.bfloat16)
        keys_all, values_all = (
            lax.all_gather(key_low, "ctx", axis=0, tiled=True),
            lax.all_gather(value_low, "ctx", axis=0, tiled=True),
        )
        query_heads = query_low.reshape(tokens, HEADS, HEAD_DIM)
        key_blocks = keys_all.reshape(heads_shape)
        value_blocks = values_all.reshape(heads_shape)

        def stats_step(carry, piece):
            run_max, run_sum = carry
            key_piece, key_pos = piece
            raw_scores = (
                jnp.einsum(
                    "qhd,khd->hqk", query_heads, key_piece, preferred_element_type=jnp.float32
                )
                * scale
            )
            allowed = (pos_mine[:, None] >= key_pos[None, :])[None]
            masked = jnp.where(allowed, raw_scores, NEG_LARGE)
            new_max = jnp.maximum(run_max, jnp.max(masked, axis=-1))
            weights = jnp.where(allowed, jnp.exp(masked - new_max[:, :, None]), 0.0)
            run_sum = run_sum * jnp.exp(run_max - new_max) + jnp.sum(weights, axis=-1)
            return ((new_max, run_sum), None)

        start_state = (
            jnp.full((HEADS, tokens), NEG_LARGE, jnp.float32),
            jnp.zeros((HEADS, tokens), jnp.float32),
        )
        (run_max, run_sum), unused = lax.scan(stats_step, start_state, (key_blocks, pos_blocks))
        row_lse = run_max + jnp.log(run_sum)

        def output_step(carry, piece):
            acc_low, acc_exact = carry
            key_piece, value_piece, key_pos = piece
            probs = block_probs(query_heads, key_piece, pos_mine, key_pos, row_lse, scale)
            acc_low = acc_low + jnp.einsum(
                "hqk,khd->hqd",
                probs.astype(jnp.bfloat16),
                value_piece,
                preferred_element_type=jnp.float32,
            )
            acc_exact = acc_exact + jnp.einsum(
                "hqk,khd->hqd",
                probs,
                value_piece.astype(jnp.float32),
                preferred_element_type=jnp.float32,
            )
            return ((acc_low, acc_exact), None)

        start_acc = (
            jnp.zeros((HEADS, tokens, HEAD_DIM), jnp.float32),
            jnp.zeros((HEADS, tokens, HEAD_DIM), jnp.float32),
        )
        (attn_heads, exact_heads), unused = lax.scan(
            output_step, start_acc, (key_blocks, value_blocks, pos_blocks)
        )
        attn_low = jnp.transpose(attn_heads, (1, 0, 2)).reshape(tokens, D).astype(jnp.bfloat16)
        resid = inputs + jnp.dot(attn_low, out_full, preferred_element_type=jnp.float32) + out_bias
        second_out, second_normed, second_inv = normalize(resid, second_gain, second_shift)
        second_low = second_out.astype(jnp.bfloat16)
        hidden = jnp.dot(second_low, up_full, preferred_element_type=jnp.float32) + up_bias
        active_low = gelu_tanh(hidden).astype(jnp.bfloat16)
        result = (
            resid + jnp.dot(active_low, down_full, preferred_element_type=jnp.float32) + down_bias
        )
        outputs_fwd.append(result.astype(jnp.bfloat16))
        grad_out = cotangent[micro_step]
        grad_outf = grad_out.astype(jnp.float32)
        term_down = jnp.einsum(
            "tf,td->fd", active_low, grad_out, preferred_element_type=jnp.float32
        )
        grad_active = jnp.einsum(
            "td,fd->tf", grad_out, down_full, preferred_element_type=jnp.float32
        )
        grad_hidden = (grad_active * gelu_slope(hidden)).astype(jnp.bfloat16)
        term_up = jnp.einsum(
            "td,tf->df", second_low, grad_hidden, preferred_element_type=jnp.float32
        )
        grad_second = jnp.einsum(
            "tf,df->td", grad_hidden, up_full, preferred_element_type=jnp.float32
        )
        grad_resid = grad_outf + normalize_back(grad_second, second_normed, second_inv, second_gain)
        grad_branch = grad_resid.astype(jnp.bfloat16)
        term_out = jnp.einsum(
            "td,te->de", attn_low, grad_branch, preferred_element_type=jnp.float32
        )
        grad_attn = jnp.einsum(
            "te,de->td", grad_branch, out_full, preferred_element_type=jnp.float32
        ).astype(jnp.bfloat16)
        grad_heads = grad_attn.reshape(tokens, HEADS, HEAD_DIM)
        row_delta = jnp.einsum("qhd,hqd->hq", grad_heads.astype(jnp.float32), exact_heads)

        def backward_step(grad_query, piece):
            key_piece, value_piece, key_pos = piece
            probs = block_probs(query_heads, key_piece, pos_mine, key_pos, row_lse, scale)
            grad_value = jnp.einsum(
                "hqk,qhd->khd",
                probs.astype(jnp.bfloat16),
                grad_heads,
                preferred_element_type=jnp.float32,
            )
            grad_probs = jnp.einsum(
                "qhd,khd->hqk", grad_heads, value_piece, preferred_element_type=jnp.float32
            )
            grad_scores = score_grads(probs, grad_probs, row_delta, scale)
            grad_query = grad_query + jnp.einsum(
                "hqk,khd->qhd", grad_scores, key_piece, preferred_element_type=jnp.float32
            )
            grad_key = jnp.einsum(
                "hqk,qhd->khd", grad_scores, query_heads, preferred_element_type=jnp.float32
            )
            rows_here = key_piece.shape[0]
            return (
                grad_query,
                jnp.concatenate(
                    [grad_key.reshape(rows_here, D), grad_value.reshape(rows_here, D)], axis=1
                ),
            )

        grad_query, key_terms = lax.scan(
            backward_step,
            jnp.zeros((tokens, HEADS, HEAD_DIM), jnp.float32),
            (key_blocks, value_blocks, pos_blocks),
        )
        key_sums = lax.psum_scatter(
            key_terms.reshape(seq_len, 2 * D), "ctx", scatter_dimension=0, tiled=True
        )
        grad_key_low = key_sums[:, :D].astype(jnp.bfloat16)
        grad_value_low = key_sums[:, D:].astype(jnp.bfloat16)
        grad_query_low = grad_query.reshape(tokens, D).astype(jnp.bfloat16)
        grad_projected = jnp.concatenate([grad_query_low, grad_key_low, grad_value_low], axis=1)
        term_qkv = jnp.einsum(
            "td,te->de", first_low, grad_projected, preferred_element_type=jnp.float32
        )
        grad_first = jnp.einsum(
            "te,de->td", grad_projected, qkv_full, preferred_element_type=jnp.float32
        )
        grad_input = grad_resid + normalize_back(grad_first, first_normed, first_inv, first_gain)
        outputs_grad.append(grad_input.astype(jnp.bfloat16))
        terms = (
            jnp.sum(grad_first * first_normed, axis=0),
            jnp.sum(grad_first, axis=0),
            term_qkv,
            jnp.sum(grad_query_low.astype(jnp.float32), axis=0),
            jnp.sum(grad_value_low.astype(jnp.float32), axis=0),
            term_out,
            jnp.sum(grad_branch.astype(jnp.float32), axis=0),
            jnp.sum(grad_second * second_normed, axis=0),
            jnp.sum(grad_second, axis=0),
            term_up,
            jnp.sum(grad_hidden.astype(jnp.float32), axis=0),
            term_down,
            jnp.sum(grad_outf, axis=0),
        )
        totals = [older + newer for older, newer in zip(totals, terms)]
    summed = (
        lax.psum_scatter(totals[0], ("ctx", "fsdp"), scatter_dimension=0, tiled=True),
        lax.psum_scatter(totals[1], ("ctx", "fsdp"), scatter_dimension=0, tiled=True),
        lax.psum_scatter(totals[2], ("ctx", "fsdp"), scatter_dimension=0, tiled=True),
        lax.psum_scatter(totals[3], ("ctx", "fsdp"), scatter_dimension=0, tiled=True),
        lax.psum_scatter(totals[4], ("ctx", "fsdp"), scatter_dimension=0, tiled=True),
        lax.psum_scatter(totals[5], ("ctx", "fsdp"), scatter_dimension=0, tiled=True),
        lax.psum_scatter(totals[6], ("ctx", "fsdp"), scatter_dimension=0, tiled=True),
        lax.psum_scatter(totals[7], ("ctx", "fsdp"), scatter_dimension=0, tiled=True),
        lax.psum_scatter(totals[8], ("ctx", "fsdp"), scatter_dimension=0, tiled=True),
        lax.psum_scatter(totals[9], ("ctx", "fsdp"), scatter_dimension=0, tiled=True),
        lax.psum_scatter(totals[10], ("ctx", "fsdp"), scatter_dimension=0, tiled=True),
        lax.psum_scatter(totals[11], ("ctx", "fsdp"), scatter_dimension=0, tiled=True),
        lax.psum_scatter(totals[12], ("ctx", "fsdp"), scatter_dimension=0, tiled=True),
    )
    return (
        jnp.stack(outputs_fwd),
        jnp.stack(outputs_grad),
        summed[0],
        summed[1],
        summed[2],
        summed[3],
        summed[4],
        summed[5],
        summed[6],
        summed[7],
        summed[8],
        summed[9],
        summed[10],
        summed[11],
        summed[12],
    )


LOG2E = 1.4426950408889634


def dot_as(left, right, left_dim, right_dim):
    return lax.dot_general(
        left, right, (((left_dim,), (right_dim,)), ((), ())), preferred_element_type=jnp.float32
    )


def dot_nn(left, right):
    return dot_as(left, right, 1, 0)


def dot_nt(left, right):
    return dot_as(left, right, 1, 1)


def dot_tn(left, right):
    return dot_as(left, right, 0, 0)


class Ring:
    def __init__(self):
        self.col = lax.axis_index("ctx")
        self.layer = lax.axis_index("fsdp")
        col = self.col
        self.sib = col + 1 - 2 * (col % 2)
        self.xnb = col + 2 - 4 * ((col // 2) % 2)
        self.ynb = col + 4 - 8 * (col // 4)
        self.diag = self.xnb + self.ynb - col
        self.xsib = self.xnb + self.sib - col
        self.ysib = self.ynb + self.sib - col
        self.dsib = self.diag + self.sib - col

    def flat(self, col):
        return (col, self.layer)

    def up(self, hop):
        return (self.layer + hop) % 4


class Wire:
    def __init__(self):
        self.all = []

    def plan(self, src, dst, send_sem, recv_sem, where):
        copy = Sent(src, dst, send_sem, recv_sem, where)
        self.all.append(copy)
        return copy

    def send(self, src, dst, send_sem, recv_sem, where):
        copy = self.plan(src, dst, send_sem, recv_sem, where)
        copy.start()
        return copy

    def drain(self):
        for copy in self.all:
            copy.wait_send()


class Sent:
    def __init__(self, src, dst, send_sem, recv_sem, where):
        self.copy = pltpu.make_async_remote_copy(
            src_ref=src,
            dst_ref=dst,
            send_sem=send_sem,
            recv_sem=recv_sem,
            device_id=where,
            device_id_type=pl.DeviceIdType.MESH,
        )
        self.left = True
        self.came = False

    def start(self):
        self.copy.start()

    def copy_in(self):
        self.copy.wait_recv()

    def copy_out(self):
        self.copy.wait_send()

    def wait_recv(self):
        self.came = True
        self.copy.wait_recv()

    def wait_send(self):
        if self.left:
            self.left = False
            self.copy.wait_send()


def move(src, dst, sem):
    copy = pltpu.make_async_copy(src, dst, sem)
    copy.start()
    return copy


class Gather:
    def __init__(self, ring, wire, block, half, ssem, rsem):
        plan = (
            (half(ring.col, 0), ring.xnb),
            (half(ring.col, 1), ring.ynb),
            (block(ring.col), ring.sib),
            (half(ring.xnb, 0), ring.ynb),
            (block(ring.xnb), ring.sib),
            (half(ring.ynb, 1), ring.xnb),
            (block(ring.ynb), ring.sib),
            (block(ring.diag), ring.sib),
            (half(ring.col, 1), ring.xnb),
            (half(ring.col, 0), ring.ynb),
        )
        self.sent = [
            wire.plan(ref, ref, ssem.at[slot], rsem.at[slot], ring.flat(col))
            for slot, (ref, col) in enumerate(plan)
        ]

    def start(self):
        for slot in (0, 1, 8, 9, 2):
            self.sent[slot].start()

    def relay(self):
        self.sent[0].wait_recv()
        self.sent[3].start()
        self.sent[1].wait_recv()
        self.sent[5].start()
        self.sent[8].wait_recv()
        self.sent[4].start()
        self.sent[9].wait_recv()
        self.sent[6].start()

    def relay_diag(self):
        self.sent[3].wait_recv()
        self.sent[5].wait_recv()
        self.sent[7].start()

    def finish(self):
        for slot in (2, 4, 6, 7):
            self.sent[slot].wait_recv()

    def drain(self):
        for copy in self.sent:
            copy.wait_send()


class Scatter:
    def __init__(self, ring, wire, part, rows, from_sib, from_diag, from_side, ssem, rsem):
        self.ring, self.part, self.rows = ring, part, rows
        self.from_sib, self.from_diag, self.from_side = from_sib, from_diag, from_side
        self.ssem, self.rsem = ssem, rsem
        self.core = ring.sib % 2
        half = rows // 2
        plan = [
            (part.at[self.at(col)], from_sib.at[slot], ring.sib)
            for slot, col in enumerate((ring.sib, ring.xsib, ring.ysib, ring.dsib))
        ]
        plan += [
            (part.at[self.at(ring.diag, 0, half)], from_diag.at[0], ring.xnb),
            (part.at[self.at(ring.diag, half, half)], from_diag.at[1], ring.ynb),
            (part.at[self.at(ring.xnb, 0, half)], from_side.at[0, 0:half], ring.xnb),
            (part.at[self.at(ring.ynb, half, half)], from_side.at[1, half:rows], ring.ynb),
            (part.at[self.at(ring.xnb, half, half)], from_side.at[0, half:rows], ring.xnb),
            (part.at[self.at(ring.ynb, 0, half)], from_side.at[1, 0:half], ring.ynb),
        ]
        self.sent = [
            wire.plan(src, dst, ssem.at[slot], rsem.at[slot], ring.flat(col))
            for slot, (src, dst, col) in enumerate(plan)
        ]

    def at(self, col, first=0, count=None):
        count = self.rows if count is None else count
        return pl.ds(pl.multiple_of(col * self.rows + first, count), count)

    def start_of(self, chip, slot):
        ring = self.ring
        col = chip * 2 + self.core
        Sent(
            self.part.at[self.at(col)],
            self.from_sib.at[slot],
            self.ssem.at[slot],
            self.rsem.at[slot],
            ring.flat(ring.sib),
        ).start()

    def start(self):
        for slot in (3, 1, 2, 0):
            self.sent[slot].start()

    def add(self, col, extra, first=0, count=None):
        where = self.at(col, first, count)
        total = self.part[where].astype(jnp.float32)
        for item in extra:
            total = total + item.astype(jnp.float32)
        self.part[where] = total.astype(jnp.bfloat16)

    def middle(self):
        self.sent[3].wait_recv()
        self.add(self.ring.diag, [self.from_sib[3]])
        self.sent[4].start()
        self.sent[5].start()

    def early(self):
        half = self.rows // 2
        self.sent[1].wait_recv()
        self.add(self.ring.xnb, [self.from_sib[1, :half]], 0, half)
        self.sent[6].start()
        self.sent[2].wait_recv()
        self.add(self.ring.ynb, [self.from_sib[2, half:]], half, half)
        self.sent[7].start()

    def last(self):
        half = self.rows // 2
        self.sent[4].wait_recv()
        self.add(self.ring.ynb, [self.from_sib[2, :half], self.from_diag[0]], 0, half)
        self.sent[9].start()
        self.sent[5].wait_recv()
        self.add(self.ring.xnb, [self.from_sib[1, half:], self.from_diag[1]], half, half)
        self.sent[8].start()

    def finish(self):
        for slot in (0, 6, 7, 8, 9):
            self.sent[slot].wait_recv()
        total = self.part[self.at(self.ring.col)].astype(jnp.float32)
        total = total + self.from_sib[0].astype(jnp.float32)
        return (
            total + self.from_side[0].astype(jnp.float32) + self.from_side[1].astype(jnp.float32)
        )

    def drain(self):
        for copy in self.sent:
            copy.wait_send()


class Halve:
    def __init__(self, ring, wire, part, near, far, ssem, rsem):
        layer = ring.layer
        self.near_plane = layer + 1 - 2 * (layer % 2)
        self.far_plane = (layer + 2) % 4
        cross = (self.near_plane + 2) % 4
        self.ring, self.part, self.near, self.far = ring, part, near, far
        plan = (
            (part(cross), near.at[0], self.near_plane),
            (part(self.near_plane), near.at[1], self.near_plane),
            (part(self.far_plane), far, self.far_plane),
        )
        self.one, self.two, self.last = (
            wire.plan(src, dst, ssem.at[slot], rsem.at[slot], (ring.col, plane))
            for slot, (src, dst, plane) in enumerate(plan)
        )

    def start(self):
        self.one.start()
        self.two.start()

    def middle(self):
        self.one.wait_recv()
        ref = self.part(self.far_plane)
        total = ref[...].astype(jnp.float32) + self.near[0].astype(jnp.float32)
        ref[...] = total.astype(jnp.bfloat16)
        self.last.start()

    def finish(self):
        self.two.wait_recv()
        total = self.part(self.ring.layer)[...].astype(jnp.float32)
        total = total + self.near[1].astype(jnp.float32)
        self.last.wait_recv()
        return total + self.far[...].astype(jnp.float32)


class Chain:
    def __init__(self, ring, block, ssem, rsem):
        layer, col = ring.layer, ring.col
        self.ways = []
        for way, step in ((0, 1), (1, -1)):
            inside = layer < 3 if step > 0 else layer > 0
            copies = []
            for k in range(3):
                item = block(ring.up(4 - k * step))
                copies.append(
                    Sent(item, item, ssem.at[way, k], rsem.at[way, k], (col, ring.up(4 + step)))
                )
            reach = [layer >= k if step > 0 else layer + k <= 3 for k in range(4)]
            self.ways.append((inside, reach, copies))

    def start(self):
        for inside, _, copies in self.ways:
            pl.when(inside)(copies[0].start)

    def pass_on(self, k):
        for inside, reach, copies in self.ways:

            @pl.when(reach[k])
            def _():
                copies[k - 1].copy_in()
                if k < 3:
                    pl.when(inside)(copies[k].start)

    def drain(self):
        for inside, reach, copies in self.ways:
            for k in range(3):

                @pl.when(jnp.logical_and(inside, reach[k]))
                def _():
                    copies[k].copy_out()


def row_norm(values):
    average = jnp.mean(values, axis=-1, keepdims=True)
    centered = values - average
    inv_dev = lax.rsqrt(jnp.mean(centered * centered, axis=-1, keepdims=True) + EPSILON)
    return centered * inv_dev, inv_dev


def layer_kernel(scale, refs):
    f32, bf16 = jnp.float32, jnp.bfloat16
    ring = Ring()
    wire = Wire()
    send = wire.send
    col, layer = ring.col, ring.layer
    seqs, tokens, width = refs.x.shape
    seq_len = tokens * 8
    head = HEAD_DIM
    rows_z = width // 4
    hid = refs.wu.shape[1] // 4
    step_c2 = scale * LOG2E
    R = refs
    mine = pl.ds(pl.multiple_of(col * tokens, tokens), tokens)
    head_cols = pl.multiple_of(col * head, head)

    barrier = pltpu.get_barrier_semaphore()
    me = col * 4 + layer
    owner_col, owner_layer = 2 * layer + col // 4, col % 4
    at_home = owner_col * 4 + owner_layer == me
    giver = (col % 2 * 4 + layer) * 4 + col // 2
    moved = ((owner_col * 4 + owner_layer - me + 32) % 32 + 31) // 32
    peers = [((col + hop) % 8, layer) for hop in range(1, 8)]
    peers += [(col, ring.up(hop)) for hop in range(1, 4)]
    for other in (owner_col * 4 + owner_layer, giver):
        other = moved * other + (1 - moved) * (31 - me)
        peers.append((other // 4, other % 4))
    for where in peers:
        pl.semaphore_signal(barrier, 1, device_id=where, device_id_type=pl.DeviceIdType.MESH)
    local = R.lsem
    load_x = move(R.x, R.xb, local.at[0])
    load_ct = [move(R.cot.at[s], R.ct.at[s, mine], local.at[1 + s]) for s in range(seqs)]
    qkv_rows = pl.ds(pl.multiple_of(layer * rows_z, rows_z), rows_z)
    load_q = []
    for g in range(3):
        src = R.w_qkv.at[:, pl.ds(pl.multiple_of(g * width + col * head, head), head)]
        load_q.append(move(src, R.wq.at[qkv_rows, g * head : (g + 1) * head], local.at[3 + g]))
    small_rows = 32
    out_src = R.w_out.at[pl.ds(pl.multiple_of(col * small_rows, small_rows), small_rows)]
    load_o = move(out_src, R.wo.at[layer, col], local.at[6])
    load_u = []
    for g in range(4):
        src = R.w_up.at[:, pl.ds(pl.multiple_of(g * width + col * hid, hid), hid)]
        load_u.append(move(src, R.wu.at[qkv_rows, g * hid : (g + 1) * hid], local.at[7 + g]))
    down_src = R.w_down.at[pl.ds(pl.multiple_of(col * hid, hid), hid)]
    down_rows = pl.ds(pl.multiple_of(layer * hid, hid), hid)
    load_d = move(down_src, R.wd.at[down_rows], local.at[11])
    load_p = []
    for row, item in enumerate(R.vectors):
        load_p.append(move(item, R.pv.at[layer, row], local.at[12 + row]))
    load_b = move(R.b_up, R.pb.at[layer], local.at[11 + 9])
    load_x.wait()
    first, second = (row_norm(R.xb[s].astype(f32))[0] for s in range(2))
    R.r1[0] = first
    R.r1[1] = second
    for s in range(seqs):
        lane = lax.broadcasted_iota(jnp.int32, (1, seq_len), 1)
        half_rows = tokens // 2
        pos = jnp.zeros((1, seq_len), jnp.int32)
        down = lax.broadcasted_iota(jnp.int32, (half_rows, 128), 0)
        for j in range(seq_len // half_rows):
            start = R.order[s, j] * half_rows
            pos = jnp.where(lane // half_rows == j, start, pos)
            R.kpos[s, j * half_rows : (j + 1) * half_rows, :] = down + start
        R.qpos[s] = pos + lane % half_rows
    for copy in load_p:
        copy.wait()
    load_b.wait()
    pl.semaphore_wait(barrier, 12)

    zs, zr = R.zs, R.zr

    def to_planes(src, dst, slot):
        return [
            send(src, dst, zs.at[slot, hop - 1], zr.at[slot, hop - 1], (col, ring.up(hop)))
            for hop in range(1, 4)
        ]

    send_par = to_planes(R.pv.at[layer], R.pv.at[layer], 0)
    send_par += to_planes(R.pb.at[layer], R.pb.at[layer], 1)

    def rows_of(ref, count):
        return lambda index: ref.at[pl.ds(pl.multiple_of(index * count, count), count)]

    chain_q, chain_u, chain_d = (
        Chain(ring, rows_of(ref, count), R.cs.at[slot], R.cr.at[slot])
        for slot, (ref, count) in enumerate(((R.wq, rows_z), (R.wu, rows_z), (R.wd, hid)))
    )
    for copy in load_q:
        copy.wait()
    chain_q.start()

    def gather_rows(ref, s, slot):

        def block(index):
            return ref.at[s, pl.ds(pl.multiple_of(index * tokens, tokens), tokens)]

        def half(index, part):
            count = tokens // 2
            first = pl.multiple_of(index * tokens + part * count, count)
            return ref.at[s, pl.ds(first, count)]

        return Gather(ring, wire, block, half, R.gs.at[slot], R.gr.at[slot])

    h1_gather = [gather_rows(R.h1, s, s) for s in range(seqs)]
    ct_gather = [gather_rows(R.ct, s, 2 + s) for s in range(seqs)]
    h2_gather = [gather_rows(R.h2, s, 4 + s) for s in range(seqs)]
    wo_gather = Gather(
        ring,
        wire,
        lambda index: R.wo.at[:, index],
        lambda index, part: R.wo.at[2 * part : 2 * part + 2, index],
        R.gs.at[6],
        R.gr.at[6],
    )

    for copy in load_ct:
        copy.wait()
    ct_gather[0].start()


    def params_row(row):
        pieces = []
        for plane in range(4):
            both = R.pv[plane, row].astype(f32)
            pieces += [both[0:1, :], both[1:2, :]]
        return jnp.concatenate(pieces, axis=1)

    for copy in send_par:
        copy.wait_recv()
    gain1, shift1 = params_row(0), params_row(1)
    R.h1[0, mine] = (R.r1[0] * gain1 + shift1).astype(bf16)
    h1_gather[0].start()
    R.h1[1, mine] = (R.r1[1] * gain1 + shift1).astype(bf16)
    h1_gather[1].start()
    for copy in load_u:
        copy.wait()
    chain_u.start()
    load_o.wait()
    send_o = to_planes(out_src, R.wo.at[layer, col], 4)

    def chosen(rows):
        total = rows[0]
        for index, item in enumerate(rows[1:]):
            total = jnp.where(col == index + 1, item, total)
        return total

    def head_row(row):
        parts = [R.pv[plane, row].astype(f32) for plane in range(4)]
        return chosen([parts[j // 2][j % 2 : j % 2 + 1, :] for j in range(8)])

    bias_q, bias_v = head_row(2), head_row(3)
    pieces = []
    for plane in range(4):
        rows = R.pb[plane].astype(f32)
        pieces.append(chosen([rows[j : j + 1, :] for j in range(8)]))
    bias_u = jnp.concatenate(pieces, axis=1)
    tile = 256


    def span(chip):
        return pl.ds(pl.multiple_of(chip * tile, tile), tile)

    chip_x, chip_y = (col // 2) % 2, col // 4

    def order(t):
        flip_x, flip_y = 1 - t[0], 1 - t[1]
        place_x = chip_x + flip_x - 2 * chip_x * flip_x
        place_y = chip_y + flip_y - 2 * chip_y * flip_y
        return place_x + 2 * place_y, flip_x + 2 * flip_y

    def pairs(body, **between):
        @pl.loop(0, 2)
        def _(high):
            body((high, 0))
            body((high, 1))
            for name, action in between.items():
                pl.when(high == int(name[1:]))(action)

    def tiles(body, **between):
        @pl.loop(0, 2)
        def _(high):
            @pl.loop(0, 2)
            def _(low):
                body((high, low))
                t = 2 * high + low
                for name, action in between.items():
                    pl.when(t == int(name[1:]))(action)

    def project(s):
        @pl.loop(0, 4)
        def _(t):
            r = span(t)
            both = dot_nn(R.h1[s, r, :], R.wq[...])
            R.q[s, r, :] = (both[:, :head] + bias_q).astype(bf16)
            R.k[s, r, :] = both[:, head : 2 * head].astype(bf16)
            R.v[s, r, :] = (both[:, 2 * head :] + bias_v).astype(bf16)

        R.kt[s] = R.k[s].T
        R.vt[s] = R.v[s].T

    def masked(s, r, scores, other):
        keys = jnp.concatenate([R.kpos[s]] * (tile // 128), axis=1)
        return jnp.where(R.qpos[s, :, r] >= keys, scores, other)

    def attend(s, t):
        r = span(2 * t[0] + t[1])
        raw = masked(s, r, dot_nt(R.k[s], R.q[s, r, :]), NEG_LARGE)
        top = jnp.max(raw, axis=0, keepdims=True)
        weights = jnp.exp2((raw - top) * step_c2)
        total = jnp.sum(weights, axis=0, keepdims=True)
        turned = dot_nn(R.vt[s], weights.astype(bf16)) * (1.0 / total)
        R.ol[s, r, :] = turned.T.astype(bf16)
        R.lse[s, :, r] = top * step_c2 + jnp.log2(total)

    others = (ring.dsib, ring.diag, ring.xsib, ring.xnb, ring.ysib, ring.ynb, ring.sib)

    def heads_to_rows(s):
        R.ob[s, :, pl.ds(head_cols, head)] = R.ol[s, mine, :]
        copies = []
        for slot, other in enumerate(others):
            src = R.ol.at[s, pl.ds(pl.multiple_of(other * tokens, tokens), tokens)]
            dst = R.ob.at[s, :, pl.ds(head_cols, head)]
            copies.append(
                send(src, dst, R.a_s.at[s, slot], R.a_r.at[s, slot], ring.flat(other))
            )
        return copies

    def rows_to_heads(s):
        R.dh[s, mine, :] = R.db[s, :, pl.ds(head_cols, head)]
        copies = []
        for slot, other in enumerate(others):
            src = R.db.at[s, :, pl.ds(pl.multiple_of(other * head, head), head)]
            dst = R.dh.at[s, mine]
            copies.append(
                send(src, dst, R.a_s.at[2 + s, slot], R.a_r.at[2 + s, slot], ring.flat(other))
            )
        return copies

    bias_o = params_row(4)
    gain2, shift2 = params_row(5), params_row(6)
    out_w = R.wo

    def out_project(s):
        for copy in moved_o[s]:
            copy.wait_recv()
        weight = out_w[...].reshape(width, width)
        resid = R.xb[s].astype(f32) + dot_nn(R.ob[s], weight) + bias_o
        R.r1[s] = resid
        normed, _ = row_norm(resid)
        R.h2[s, mine] = (normed * gain2 + shift2).astype(bf16)

    def many(*actions):
        def run():
            for action in actions:
                action()

        return run

    ct_gather[0].relay()
    h1_gather[0].relay()
    chain_q.pass_on(1)
    h1_gather[1].relay()
    h1_gather[0].relay_diag()
    ct_gather[0].relay_diag()
    ct_gather[1].start()
    chain_q.pass_on(2)
    load_d.wait()
    chain_d.start()
    h1_gather[0].finish()
    chain_q.pass_on(3)
    project(0)
    chain_u.pass_on(1)
    h1_gather[1].relay_diag()
    for copy in send_o:
        copy.wait_recv()
    wo_gather.start()
    pairs(lambda t: attend(0, t), t0=wo_gather.relay)
    moved_o = [heads_to_rows(0)]
    h1_gather[1].finish()
    ct_gather[1].relay()
    project(1)
    wo_gather.relay_diag()
    chain_u.pass_on(2)

    def first_rows():
        out_project(0)
        h2_gather[0].start()

    pairs(
        lambda t: attend(1, t),
        t0=many(lambda: chain_d.pass_on(1), wo_gather.finish, first_rows),
        t1=ct_gather[1].relay_diag,
    )
    moved_o.append(heads_to_rows(1))
    h2_gather[0].relay()
    chain_u.pass_on(3)
    out_project(1)
    h2_gather[1].start()
    chain_d.pass_on(2)
    h2_gather[0].relay_diag()
    ct_gather[0].finish()
    h2_gather[0].finish()
    chain_d.pass_on(3)

    def feed(s, t):
        chip, slot = order(t)
        r = span(chip)
        hidden = dot_nn(R.h2[s, r, :], R.wu[...]) + bias_u
        grad = dot_nt(R.ct[s, r, :], R.wd[...])
        square = hidden * hidden
        bend = jnp.tanh(hidden * (GELU_C + (GELU_C * GELU_K) * square))
        half = 0.5 * (1.0 + bend)
        active = (hidden * half).astype(bf16)
        slope = half + (0.5 * hidden) * (1.0 - bend * bend) * (
            GELU_C + (3.0 * GELU_C * GELU_K) * square
        )
        R.act[s, r, :] = active
        grad = (grad * slope).astype(bf16)
        R.du[s, r, :] = grad
        R.pd[s, r, :] = dot_nt(grad, R.wu[...]).astype(bf16)
        R.po[s, r, :] = dot_nn(active, R.wd[...]).astype(bf16)
        R.us[...] += jnp.sum(grad.astype(f32), axis=0, keepdims=True)
        d2[s].start_of(chip, slot)
        out_sc[s].start_of(chip, slot)

    def scatter(part, s, recv, slot, rows=None):
        return Scatter(
            ring,
            wire,
            part,
            tokens,
            R.r_sib.at[recv],
            R.r_diag.at[recv],
            R.r_side.at[recv],
            R.ss.at[slot],
            R.sr.at[slot],
        )

    R.us[...] = jnp.zeros_like(R.us)
    d2 = [scatter(R.pd.at[s], s, s, s) for s in range(2)]
    out_sc = [scatter(R.po.at[s], s, 2 + s, 2 + s) for s in range(2)]
    pairs(
        lambda t: feed(0, t),
        t0=many(h2_gather[1].relay, d2[0].middle),
        t1=many(h2_gather[1].relay_diag, d2[0].early),
    )
    d2[0].last()
    h2_gather[1].finish()
    ct_gather[1].finish()
    pairs(lambda t: feed(1, t), t0=d2[1].middle, t1=d2[1].early)

    bz = R.bz
    for g in range(4):
        bz[2 + g : 3 + g, :] = R.us[:, g * hid : (g + 1) * hid]


    def grad_down():
        for j in range(2):
            cols = slice(j * 2 * hid, (j + 1) * 2 * hid)
            total = dot_tn(R.act[0, :, cols], R.ct[0])
            total = total + dot_tn(R.act[1, :, cols], R.ct[1])
            R.gd[cols, :] = total.astype(bf16)

    def grad_up():
        for j in range(2):
            cols = slice(j * 2 * hid, (j + 1) * 2 * hid)
            total = dot_tn(R.du[0, :, cols], R.h2[0])
            total = total + dot_tn(R.du[1, :, cols], R.h2[1])
            total = total.T.astype(bf16).reshape(8, 4, 32, 2 * hid)
            R.gu[:, :, :, cols] = total

    def to_planes_part(piece, dst, slot):
        return [
            send(
                piece(ring.up(hop)),
                dst.at[hop - 1],
                zs.at[slot, hop - 1],
                zr.at[slot, hop - 1],
                (col, ring.up(hop)),
            )
            for hop in range(1, 4)
        ]

    sums = {}

    def back_norm2(s):
        grad = d2[s].finish()
        normed, inv_dev = row_norm(R.r1[s])
        cot = R.ct[s, mine].astype(f32)
        scaled = grad * gain2
        resid = cot + inv_dev * (
            scaled
            - jnp.mean(scaled, axis=-1, keepdims=True)
            - normed * jnp.mean(scaled * normed, axis=-1, keepdims=True)
        )
        R.dr[s] = resid
        low = resid.astype(bf16)
        R.dz[s] = low
        lowf = low.astype(f32)
        parts = (
            jnp.sum(lowf, axis=0, keepdims=True),
            jnp.sum(grad * normed, axis=0, keepdims=True),
            jnp.sum(grad, axis=0, keepdims=True),
            jnp.sum(cot, axis=0, keepdims=True),
        )
        for row, item in enumerate(parts):
            sums[row] = sums[row] + item if row in sums else item
        R.db[s] = dot_nt(low, out_w[...].reshape(width, width)).astype(bf16)

    def attend_back(s, t):
        r = span(2 * t[0] + t[1])
        query, dout = R.q[s, r, :], R.dh[s, r, :]
        raw = dot_nt(R.k[s], query)
        probs = masked(s, r, jnp.exp2(raw * step_c2 - R.lse[s, :, r]), 0.0)
        grad = dot_nt(R.v[s], dout)
        part_v = dot_nn(probs.astype(bf16), dout)
        delta = jnp.sum(probs * grad, axis=0, keepdims=True)
        low = (probs * ((grad - delta) * scale)).astype(bf16)
        part_k = dot_nn(low, query)
        R.dp[s, r, :head] = dot_nn(R.kt[s], low).T.astype(bf16)
        R.dva[s] += part_v
        R.dka[s] += part_k

    def close_back(s):
        R.dp[s, :, head : 2 * head] = R.dka[s].astype(bf16)
        R.dp[s, :, 2 * head :] = R.dva[s].astype(bf16)

    def first_part(s, t):
        chip, slot = order(t)
        r = span(chip)
        R.pd[s, r, :] = dot_nt(R.dp[s, r, :], R.wq[...]).astype(bf16)
        d1[s].start_of(chip, slot)

    back_norm2(0)
    moved_d = [rows_to_heads(0)]
    d2[1].last()
    grad_down()
    z_down = Halve(ring, wire, rows_of(R.gd, hid), R.zd.at[0:2], R.zd.at[2], zs.at[10], zr.at[10])
    z_down.start()
    out_sc[0].middle()
    grad_up()
    z_up = Halve(
        ring, wire, lambda other: R.gu.at[:, other], R.zu.at[0:2], R.zu.at[2], zs.at[11], zr.at[11]
    )
    z_up.start()
    back_norm2(1)
    moved_d.append(rows_to_heads(1))
    out_sc[0].early()
    out_sc[0].last()

    h2_flat = R.h2.at[0]
    for gather in h2_gather:
        gather.drain()
    h2_flat[...] = (dot_tn(R.ob[0], R.dz[0]) + dot_tn(R.ob[1], R.dz[1])).astype(bf16)
    wo_sc = scatter(h2_flat, 0, 4, 6)
    wo_sc.start()
    R.dva[...] = jnp.zeros_like(R.dva)
    R.dka[...] = jnp.zeros_like(R.dka)
    for copy in moved_d[0]:
        copy.wait_recv()
    pairs(lambda t: attend_back(0, t), t0=wo_sc.middle)
    close_back(0)
    d2[0].drain()
    d1 = [scatter(R.pd.at[s], s, s, 4 + s) for s in range(2)]
    tiles(lambda t: first_part(0, t))
    z_down.middle()
    for copy in moved_d[1]:
        copy.wait_recv()
    tiles(
        lambda t: attend_back(1, t),
        t0=many(d1[0].middle, d1[0].early, out_sc[1].middle),
        t2=many(d1[0].last, z_up.middle),
        t3=many(wo_sc.early, wo_sc.last),
    )
    close_back(1)
    d2[1].drain()
    tiles(lambda t: first_part(1, t), t2=d1[1].middle)
    proj_sums = jnp.sum(R.dp[0].astype(f32), axis=0, keepdims=True) + jnp.sum(
        R.dp[1].astype(f32), axis=0, keepdims=True
    )
    bz[0:1, :] = proj_sums[:, :head]
    bz[1:2, :] = proj_sums[:, 2 * head :]
    bz[6:8, :] = jnp.zeros((2, head), f32)
    z_b = to_planes(bz, R.zb.at[layer], 13)
    for g in range(3):
        cols = slice(g * head, (g + 1) * head)
        total = dot_tn(R.dp[0, :, cols], R.h1[0]) + dot_tn(R.dp[1, :, cols], R.h1[1])
        R.gq[:, :, :, cols] = total.T.astype(bf16).reshape(8, 4, 32, head)
    z_q = Halve(
        ring, wire, lambda other: R.gq.at[:, other], R.zq.at[0:2], R.zq.at[2], zs.at[12], zr.at[12]
    )
    z_q.start()
    d1[1].early()
    d1[1].last()
    out_sc[1].early()
    out_sc[1].last()
    R.gws[...] = wo_sc.finish().astype(bf16)
    z_o = to_planes_part(
        lambda other: R.gws.at[pl.ds(pl.multiple_of(other * 32, 32), 32)], R.zo, 15
    )

    R.gdo[...] = z_down.finish().astype(bf16)
    for copy in z_b:
        copy.wait_recv()
    bz_all = bz[...] + (R.zb[ring.up(1)] + R.zb[ring.up(2)] + R.zb[ring.up(3)])
    R.bzs[...] = bz_all
    own_up = jnp.zeros((1, head), f32)
    for k in range(4):
        own_up = jnp.where(layer == k, bz_all[2 + k : 3 + k, :], own_up)
    R.bu[...] = jnp.broadcast_to(own_up, (8, head))
    psem = R.ps
    home_copies = (
        (R.gdo, R.o_gd, psem.at[0], psem.at[2], psem.at[3]),
        (R.bu, R.o_bu, psem.at[1], psem.at[4], psem.at[5]),
    )

    @pl.when(at_home)
    def _():
        for src, dst, sem, _, _ in home_copies:
            move(src, dst, sem).wait()

    away = [
        Sent(src, dst, ssem, rsem, (owner_col, owner_layer))
        for src, dst, _, ssem, rsem in home_copies
    ]

    @pl.when(jnp.logical_not(at_home))
    def _():
        for copy in away:
            copy.start()

    def to_columns(src, dst, row):
        keep = move(src.at[col], dst.at[col], local.at[21 + row])
        copies = []
        for slot, other in enumerate(others):
            copies.append(
                send(
                    src.at[other],
                    dst.at[col],
                    R.a_s.at[4 + row, slot],
                    R.a_r.at[4 + row, slot],
                    ring.flat(other),
                )
            )
        return keep, copies

    R.guo[...] = z_up.finish().astype(bf16)
    up_keep, up_moves = to_columns(R.guo, R.o_gu, 0)

    bias_d = params_row(7)
    for s in range(2):
        R.los[s] = (R.r1[s] + out_sc[s].finish() + bias_d).astype(bf16)
    save_lo = move(R.los, R.o_lo, local.at[24])

    def back_norm1(s):
        grad = d1[s].finish()
        normed, inv_dev = row_norm(R.xb[s].astype(f32))
        scaled = grad * gain1
        total = R.dr[s] + inv_dev * (
            scaled
            - jnp.mean(scaled, axis=-1, keepdims=True)
            - normed * jnp.mean(scaled * normed, axis=-1, keepdims=True)
        )
        R.igs[s] = total.astype(bf16)
        for row, item in ((4, grad * normed), (5, grad)):
            item = jnp.sum(item, axis=0, keepdims=True)
            sums[row] = sums[row] + item if row in sums else item

    back_norm1(0)
    z_q.middle()
    back_norm1(1)
    save_ig = move(R.igs, R.o_ig, local.at[23])
    for row in range(6):
        R.ev[row : row + 1, :] = sums[row]
    R.ev[6:8, :] = jnp.zeros((2, width), f32)
    ev_moves = []
    for hop in range(1, 8):
        other = (col + hop) % 8
        ev_moves.append(
            send(
                R.ev.at[:, pl.ds(pl.multiple_of(other * head, head), head)],
                R.evr.at[hop - 1],
                R.es.at[hop - 1],
                R.er.at[hop - 1],
                ring.flat(other),
            )
        )
    R.gqo[...] = z_q.finish().astype(bf16)
    q_keep, q_moves = to_columns(R.gqo, R.o_gq, 1)
    for copy in ev_moves:
        copy.wait_recv()
    plane = R.ev[:, pl.ds(head_cols, head)]
    for k in range(7):
        plane = plane + R.evr[k]
    R.evp[...] = plane
    z_e = to_planes(R.evp, R.evz.at[layer], 14)
    for copy in z_o:
        copy.wait_recv()
    go_rows = pl.ds(pl.multiple_of(layer * 32, 32), 32)
    total = R.gws[go_rows].astype(f32)
    for k in range(3):
        total = total + R.zo[k].astype(f32)
    R.o_go[...] = total
    for copy in z_e:
        copy.wait_recv()
    total = R.evp[...] + (R.evz[ring.up(1)] + R.evz[ring.up(2)] + R.evz[ring.up(3)])
    both = jnp.concatenate([total, R.bzs[...]], axis=0)
    picked = jnp.zeros((16, 32), f32)
    for k in range(4):
        picked = jnp.where(layer == k, both[:, k * 32 : (k + 1) * 32], picked)
    R.o_small[...] = picked

    @pl.when(jnp.logical_not(at_home))
    def _():
        for copy in away:
            copy.wait_recv()
            copy.wait_send()

    save_ig.wait()
    save_lo.wait()
    for keep, copies in ((up_keep, up_moves), (q_keep, q_moves)):
        keep.wait()
        for copy in copies:
            copy.wait_recv()
    wire.drain()
    for chain in (chain_q, chain_u, chain_d):
        chain.drain()


def closing_kernel(refs):
    R = refs
    f32 = jnp.float32
    head = HEAD_DIM
    sem = R.sem
    plan = (
        (R.gd, R.vd, R.td, R.f_gd),
        (R.gu, R.vu, R.tu, R.f_gu),
        (R.gq, R.vq, R.tq, R.f_gq),
        (R.lo, R.vl, R.vl, R.f_lo),
        (R.ig, R.vi, R.vi, R.f_ig),
        (R.go, R.vo, R.vo, R.f_go),
    )
    loads = [move(src, held, sem.at[slot]) for slot, (src, held, _, _) in enumerate(plan)]
    waits = []
    for slot, (_, held, wide, dst) in enumerate(plan):
        loads[slot].wait()
        if slot == 0:
            wide[...] = held[...].astype(f32)
        elif slot < 3:
            groups = held.shape[2] // head
            for g in range(groups):
                for c in range(8):
                    first = (g * 8 + c) * head
                    piece = held[c, :, g * head : (g + 1) * head]
                    wide[:, first : first + head] = piece.astype(f32)
        waits.append(move(wide, dst, sem.at[6 + slot]))
    for row, ref in R.rows:
        ref[...] = R.small[row]
    R.f_bu[...] = R.bu[0]
    for copy in waits:
        copy.wait()

def per_device_tp(
    layer_in,
    block_order,
    ln1_gain,
    ln1_shift,
    w_qkv,
    b_query,
    b_value,
    w_out,
    b_out,
    ln2_gain,
    ln2_shift,
    w_up,
    b_up,
    w_down,
    b_down,
    cotangent,
):
    f32, bf16, i32 = jnp.float32, jnp.bfloat16, jnp.int32
    seqs, tokens, width = layer_in.shape
    seq_len = tokens * 8
    ff = w_up.shape[1]
    hid = ff // 32
    vectors = [
        item.reshape(2, -1)
        for item in (ln1_gain, ln1_shift, b_query, b_value, b_out, ln2_gain, ln2_shift, b_down)
    ]
    anywhere = pl.BlockSpec(memory_space=pl.ANY)
    in_vmem = pl.BlockSpec(memory_space=pltpu.VMEM)
    inputs = dict(
        order=(block_order, pl.BlockSpec(memory_space=pltpu.SMEM)),
        b_up=(b_up.reshape(8, -1), anywhere),
        x=(layer_in, anywhere),
        cot=(cotangent, anywhere),
        w_qkv=(w_qkv, anywhere),
        w_out=(w_out, anywhere),
        w_up=(w_up, anywhere),
        w_down=(w_down, anywhere),
    )
    outputs = dict(
        o_lo=((seqs, tokens, width), bf16, anywhere),
        o_ig=((seqs, tokens, width), bf16, anywhere),
        o_gq=((8, 32, 3 * HEAD_DIM), bf16, anywhere),
        o_gu=((8, 32, 4 * hid), bf16, anywhere),
        o_gd=((hid, width), bf16, anywhere),
        o_go=((32, width), f32, in_vmem),
        o_small=((16, 32), f32, in_vmem),
        o_bu=((8, HEAD_DIM), f32, anywhere),
    )
    whole = (seqs, seq_len, width)
    heads = (seqs, seq_len, HEAD_DIM)
    turned = (seqs, HEAD_DIM, seq_len)
    own = (seqs, tokens, width)
    vmem, sems = pltpu.VMEM, pltpu.SemaphoreType.DMA
    scratch = dict(
        h1=vmem(whole, bf16),
        ct=vmem(whole, bf16),
        h2=vmem(whole, bf16),
        po=vmem(whole, bf16),
        pd=vmem(whole, bf16),
        wq=vmem((width, 3 * HEAD_DIM), bf16),
        wo=vmem((4, 8, 32, width), bf16),
        wu=vmem((width, 4 * hid), bf16),
        wd=vmem((4 * hid, width), bf16),
        q=vmem(heads, bf16),
        k=vmem(heads, bf16),
        v=vmem(heads, bf16),
        kt=vmem(turned, bf16),
        vt=vmem(turned, bf16),
        ol=vmem(heads, bf16),
        dh=vmem(heads, bf16),
        ob=vmem(own, bf16),
        db=vmem(own, bf16),
        xb=vmem(own, bf16),
        dz=vmem(own, bf16),
        igs=vmem(own, bf16),
        los=vmem(own, bf16),
        r1=vmem(own, f32),
        dr=vmem(own, f32),
        r_sib=vmem((5, 4, tokens, width), bf16),
        r_diag=vmem((5, 2, tokens // 2, width), bf16),
        r_side=vmem((5, 2, tokens, width), bf16),
        kpos=vmem(heads, i32),
        qpos=vmem((seqs, 1, seq_len), i32),
        lse=vmem((seqs, 1, seq_len), f32),
        act=vmem((seqs, seq_len, 4 * hid), bf16),
        du=vmem((seqs, seq_len, 4 * hid), bf16),
        dp=vmem((seqs, seq_len, 3 * HEAD_DIM), bf16),
        dka=vmem(heads, f32),
        dva=vmem(heads, f32),
        gd=vmem((4 * hid, width), bf16),
        gu=vmem((8, 4, 32, 4 * hid), bf16),
        gq=vmem((8, 4, 32, 3 * HEAD_DIM), bf16),
        gws=vmem((tokens, width), bf16),
        gdo=vmem((hid, width), bf16),
        guo=vmem((8, 32, 4 * hid), bf16),
        gqo=vmem((8, 32, 3 * HEAD_DIM), bf16),
        zd=vmem((3, hid, width), bf16),
        zu=vmem((3, 8, 32, 4 * hid), bf16),
        zq=vmem((3, 8, 32, 3 * HEAD_DIM), bf16),
        zo=vmem((3, 32, width), bf16),
        pv=vmem((4, 8, 2, HEAD_DIM), bf16),
        pb=vmem((4, 8, HEAD_DIM), bf16),
        us=vmem((1, 4 * hid), f32),
        bz=vmem((8, HEAD_DIM), f32),
        bzs=vmem((8, HEAD_DIM), f32),
        bu=vmem((8, HEAD_DIM), f32),
        zb=vmem((4, 8, HEAD_DIM), f32),
        ev=vmem((8, width), f32),
        evr=vmem((7, 8, HEAD_DIM), f32),
        evp=vmem((8, HEAD_DIM), f32),
        evz=vmem((4, 8, HEAD_DIM), f32),
        lsem=sems((25,)),
        zs=sems((16, 3)),
        zr=sems((16, 3)),
        cs=sems((3, 2, 3)),
        cr=sems((3, 2, 3)),
        gs=sems((7, 10)),
        gr=sems((7, 10)),
        ss=sems((7, 10)),
        sr=sems((7, 10)),
        a_s=sems((6, 7)),
        a_r=sems((6, 7)),
        es=sems((7,)),
        er=sems((7,)),
        ps=sems((6,)),
    )
    names = list(inputs) + list(outputs) + list(scratch)

    def body(*refs):
        space = types.SimpleNamespace(**dict(zip(names, refs[8:])))
        space.vectors = refs[:8]
        layer_kernel(HEAD_DIM ** (-0.5), space)

    results = pl.pallas_call(
        body,
        out_shape=[jax.ShapeDtypeStruct(shape, kind) for shape, kind, _ in outputs.values()],
        in_specs=[anywhere] * 8 + [spec for _, spec in inputs.values()],
        out_specs=[spec for _, _, spec in outputs.values()],
        scratch_shapes=list(scratch.values()),
        compiler_params=pltpu.CompilerParams(
            collective_id=0, has_side_effects=True, vmem_limit_bytes=VMEM_BYTES
        ),
    )(*vectors, *(item for item, _ in inputs.values()))
    finals = dict(
        f_lo=((seqs, tokens, width), bf16, anywhere),
        f_ig=((seqs, tokens, width), bf16, anywhere),
        f_g1=((32,), f32, in_vmem),
        f_s1=((32,), f32, in_vmem),
        f_gq=((32, 3 * width), f32, anywhere),
        f_bq=((32,), f32, in_vmem),
        f_bv=((32,), f32, in_vmem),
        f_go=((32, width), f32, anywhere),
        f_bo=((32,), f32, in_vmem),
        f_g2=((32,), f32, in_vmem),
        f_s2=((32,), f32, in_vmem),
        f_gu=((32, ff), f32, anywhere),
        f_bu=((HEAD_DIM,), f32, in_vmem),
        f_gd=((hid, width), f32, anywhere),
        f_bd=((32,), f32, in_vmem),
    )
    held = dict(
        vd=vmem((hid, width), bf16),
        vu=vmem((8, 32, 4 * hid), bf16),
        vq=vmem((8, 32, 3 * HEAD_DIM), bf16),
        td=vmem((hid, width), f32),
        tu=vmem((32, ff), f32),
        tq=vmem((32, 3 * width), f32),
        vl=vmem(own, bf16),
        vi=vmem(own, bf16),
        vo=vmem((32, width), f32),
        sem=sems((12,)),
    )
    last_names = [item[2:] for item in outputs] + list(finals) + list(held)

    def last_body(*refs):
        space = types.SimpleNamespace(**dict(zip(last_names, refs)))
        space.rows = (
            (4, space.f_g1),
            (5, space.f_s1),
            (8, space.f_bq),
            (9, space.f_bv),
            (0, space.f_bo),
            (1, space.f_g2),
            (2, space.f_s2),
            (3, space.f_bd),
        )
        closing_kernel(space)

    return tuple(
        pl.pallas_call(
            last_body,
            out_shape=[jax.ShapeDtypeStruct(shape, kind) for shape, kind, _ in finals.values()],
            in_specs=[anywhere] * 6 + [in_vmem] * 2,
            out_specs=[spec for _, _, spec in finals.values()],
            scratch_shapes=list(held.values()),
        )(*results)
    )


def solution(mesh):
    placed = (
        P("fsdp", "ctx", None),
        P("fsdp", None),
        P("fsdp"),
        P("fsdp"),
        P("fsdp", None),
        P("fsdp"),
        P("fsdp"),
        P("fsdp", None),
        P("fsdp"),
        P("fsdp"),
        P("fsdp"),
        P("fsdp", None),
        P("fsdp"),
        P("fsdp", None),
        P("fsdp"),
        P("fsdp", "ctx", None),
    )
    by_heads = mesh.shape["ctx"] == HEADS and mesh.shape["fsdp"] == 4
    return jax.shard_map(
        per_device_tp if by_heads else per_device_ctx,
        mesh=mesh,
        in_specs=placed,
        out_specs=(
            P("fsdp", "ctx", None),
            P("fsdp", "ctx", None),
            P(("ctx", "fsdp")),
            P(("ctx", "fsdp")),
            P(("ctx", "fsdp"), None),
            P(("ctx", "fsdp")),
            P(("ctx", "fsdp")),
            P(("ctx", "fsdp"), None),
            P(("ctx", "fsdp")),
            P(("ctx", "fsdp")),
            P(("ctx", "fsdp")),
            P(("ctx", "fsdp"), None),
            P(("ctx", "fsdp")),
            P(("ctx", "fsdp"), None),
            P(("ctx", "fsdp")),
        ),
        check_vma=False,
    )
```
